128 devices in a mesh: lat: 8 (over y_lo, x), lon: 16 (over z, y_hi, core).
Axes of the slice: x: 4, y: 4 (y_hi: 2, y_lo: 2; y = y_hi * 2 + y_lo), z: 4, core: 2. Of those that a mesh axis runs over, the one named last changes fastest.
Arguments:
- grad_out: bfloat16 [1, 720, 128, 1440], P(None, 'lat', None, 'lon'), may hold values from -6 to 6
- spectrum: bfloat16 [640, 720, 1, 2, 128], P('lon', 'lat'), may hold values from -0.8984375 to 0.8984375
- weights: bfloat16 [720, 128, 128], P('lat'), may hold values from -0.5 to 0.5
Outputs:
- grad_in: bfloat16 [1, 720, 128, 1440], P(None, 'lat', None, 'lon')
- weight_grad: float32 [720, 128, 128], P('lat', 'lon')
The draws below stay inside these ranges and needn't reach their ends.
All inputs are finite; a program needn't handle non-finite values.
Results may differ from the reference program's by a relative error of at most 0.015.
Values may be sent and summed in bfloat16 or wider, within the bound.
No kernel may reach another device: no remote copies, remote signals or barrier semaphores. Data moves between devices by JAX's collectives and lax.ppermute only.
A program may use at most 128 MiB of HBM per device.

```python
import math
import jax
import jax.numpy as jnp
from jax import lax

SAMPLES = 1
C = 128
LAT = 720
LON = 1440
L = 720
M = 640
N_LON = 16


def levels(rng, dims, cuts, least, high):
    level, own = 1.0, jax.random.fold_in(rng, 6)
    for axis_at, parts in cuts:
        draws = jnp.exp(jax.random.uniform(jax.random.fold_in(own, axis_at), (parts,), jnp.float32, least / len(cuts), high / len(cuts)))
        level = level * jnp.repeat(draws, dims[axis_at] // parts).reshape([-1 if axis == axis_at else 1 for axis in range(len(dims))])
    return level


def noise(own_key, shape, width, reach, cuts=(), held_as=jnp.bfloat16):
    drawn = jax.random.normal(own_key, shape, jnp.float32) * width
    if len(cuts) > 0:
        drawn = levels(own_key, shape, cuts, -0.22, 0.18) * drawn
    return jnp.clip(drawn, min=-reach, max=reach).astype(held_as)


def setup_inputs(seed: int = 0) -> dict:
    seeds = jax.random.split(jax.random.key(seed), 4)
    return {
        "grad_out": noise(seeds[0], (SAMPLES, LAT, C, LON), 1.0, 6.0, ((1, 8), (3, 16))),
        "spectrum": noise(seeds[1], (M, L, SAMPLES, 2, C), 0.15, 0.8984375, ((0, 16), (1, 8))),
        "weights": noise(seeds[2], (L, C, C), C ** -0.5, 0.5, ((0, 8),)),
    }


def fourier_table(point_count, mode_count):
    positions = jnp.arange(point_count, dtype=jnp.int32)[:, None]
    mode_index = jnp.arange(mode_count, dtype=jnp.int32)[None, :]
    phase_index = positions * mode_index % point_count
    angles = phase_index.astype(jnp.float32) * (2.0 * math.pi / point_count)
    factor = 1.0 / math.sqrt(point_count)
    stacked = jnp.stack([jnp.cos(angles) * factor, -jnp.sin(angles) * factor], axis=-1)
    return stacked.reshape(point_count, 2 * mode_count).astype(jnp.bfloat16)

def block_steps(degrees):
    step_count = -(-degrees // 30)
    while degrees % step_count != 0:
        step_count = step_count + 1
    return step_count

def legendre_table(orders, degrees, lat_count):
    colatitude = (jnp.arange(lat_count, dtype=jnp.float32) + 0.5) * (math.pi / lat_count)
    cosine = jnp.cos(colatitude)[None, :]
    sines = jnp.sin(colatitude)[None, :]
    root_weight = jnp.sqrt(sines * (math.pi / lat_count))
    order_val = orders.astype(jnp.float32)[:, None]
    order_col = orders[:, None]
    log_seed = 0.5 * jnp.log(order_val + 0.5) + 0.5 * lax.lgamma(2.0 * order_val + 1.0) - lax.lgamma(order_val + 1.0) - order_val * math.log(2.0) + order_val * jnp.log(sines)
    step_count = block_steps(degrees)

    def advance(carried, start_deg):
        current, previous, log_scale = carried
        outputs = []
        for offset in range(step_count):
            degree = start_deg + offset
            degree_val = degree.astype(jnp.float32)
            past_start = degree > order_col
            at_start = degree == order_col
            divisor = jnp.where(past_start, degree_val * degree_val - order_val * order_val, 1.0)
            coeff_up = jnp.sqrt(jnp.maximum((4.0 * degree_val * degree_val - 1.0) / divisor, 0.0))
            lower_term = (degree_val - 1.0) * (degree_val - 1.0) - order_val * order_val
            coeff_back = jnp.sqrt(jnp.maximum(lower_term * (2.0 * degree_val + 1.0) / ((2.0 * degree_val - 3.0) * divisor), 0.0))
            advanced = coeff_up * cosine * current - coeff_back * previous
            magnitude = jnp.where(past_start, jnp.maximum(jnp.abs(advanced), jnp.abs(current)), 1.0)
            previous = jnp.where(past_start, current / magnitude, 0.0)
            log_scale = jnp.where(at_start, log_seed, jnp.where(past_start, log_scale + jnp.log(magnitude), 0.0))
            current = jnp.where(at_start, 1.0, jnp.where(past_start, advanced / magnitude, 0.0))
            outputs.append(current * jnp.exp(log_scale) * root_weight)
        return ((current, previous, log_scale), jnp.stack(outputs))
    initial = jnp.zeros((orders.shape[0], lat_count), jnp.float32)
    starts = jnp.arange(degrees // step_count, dtype=jnp.int32) * step_count
    _, blocks = lax.scan(advance, (initial, initial, initial), starts)
    return blocks.reshape(degrees, orders.shape[0], lat_count)

def reference(grad_out, spectrum, weights):
    fourier = fourier_table(LON, M)
    spectra = jnp.dot(grad_out.reshape(SAMPLES * LAT * C, LON), fourier, preferred_element_type=jnp.float32).astype(jnp.bfloat16)
    order_group = M // N_LON
    block_count = N_LON
    spectra = spectra.reshape(SAMPLES, LAT, C, block_count, order_group, 2)
    spectra = jnp.moveaxis(spectra, 3, 0)
    stored = spectrum.reshape(block_count, order_group, L, SAMPLES, 2, C)
    starts = jnp.arange(block_count, dtype=jnp.int32) * order_group
    weights_full = weights.astype(jnp.float32)

    def one_block(summed, pieces):
        column, stored_block, start_order = pieces
        orders = start_order + jnp.arange(order_group, dtype=jnp.int32)
        legendre = lax.optimization_barrier(legendre_table(orders, L, LAT).astype(jnp.bfloat16)).astype(jnp.float32)
        analysed = jnp.einsum('lst,btcsp->slbpc', legendre, column.astype(jnp.float32)).astype(jnp.bfloat16)
        analysed_full = analysed.astype(jnp.float32)
        summed = summed + jnp.einsum('slbpc,slbpd->lcd', stored_block.astype(jnp.float32), analysed_full)
        spec_grad = jnp.einsum('lcd,slbpd->slbpc', weights_full, analysed_full).astype(jnp.bfloat16)
        col_grad = jnp.einsum('lst,slbpc->btcsp', legendre, spec_grad.astype(jnp.float32)).astype(jnp.bfloat16)
        return (summed, col_grad)
    weight_grad, col_grad = lax.scan(one_block, jnp.zeros((L, C, C), jnp.float32), (spectra, stored, starts))
    col_grad = jnp.moveaxis(col_grad, 0, 3).reshape(SAMPLES * LAT * C, 2 * M)
    grad_in = jnp.dot(col_grad, fourier.T, preferred_element_type=jnp.float32).astype(jnp.bfloat16)
    return (grad_in.reshape(SAMPLES, LAT, C, LON), weight_grad)
```

```python
import math

import jax
import jax.numpy as jnp
import numpy as np
from jax import lax
from jax.experimental import pallas as pl
from jax.experimental.pallas import tpu as pltpu
from jax.sharding import PartitionSpec as P

LAT = 720
LON = 1440
L = 720
M = 640
C = 128
LATS = 8
LONS = 16
ROWS = LAT // LATS
COLS = LON // LONS
SLOT = 6
USED = ROWS // SLOT
PAD = 96
ORDERS = M // (LATS * LONS)
Q = 2 * ORDERS
DEGREES = L // LATS
BLOCK = 16
SHIFT = 40

F32 = jnp.float32
BF16 = jnp.bfloat16


def cosine_values(position, order, part):
    step = position * order + part * (LON // 4)
    turn = step - LON * jnp.floor(step * (1.0 / LON))
    fold = (LON // 4) - jnp.abs(turn - LON // 2)
    angle = fold * (2.0 * math.pi / LON)
    square = angle * angle
    series = -1.0 / 39916800.0
    for term in (1.0 / 362880.0, -1.0 / 5040.0, 1.0 / 120.0, -1.0 / 6.0, 1.0):
        series = series * square + term
    return -(angle * series) * (1.0 / math.sqrt(LON))


def fourier_tables():
    def line(shape, axis):
        at = lax.broadcasted_iota(jnp.int32, shape, axis)
        inner = at % PAD
        return (at // PAD * COLS + inner).astype(F32), (inner < COLS).astype(F32)

    def modes(shape, axis):
        at = lax.broadcasted_iota(jnp.int32, shape, axis)
        return (at // 2).astype(F32), (at % 2).astype(F32)

    wide = LONS * PAD
    position, live = line((1, wide), 1)
    order, part = modes((2 * M, 1), 0)
    forward = (cosine_values(position, order, part) * live).astype(BF16)
    position, live = line((wide, 1), 0)
    order, part = modes((1, 2 * M), 1)
    backward = (cosine_values(position, order, part) * live).astype(BF16)
    return forward, backward


def seed_constants():
    out = []
    for m in range(M):
        out.append(
            0.5 * math.log(m + 0.5)
            + 0.5 * math.lgamma(2.0 * m + 1.0)
            - math.lgamma(m + 1.0)
            - m * math.log(2.0)
        )
    return np.asarray(out, np.float32)


def legendre_kernel(up, back, start, seed, order, x_ref, root_ref, sine_ref, out, buf):
    x = x_ref[...]
    root = root_ref[...]
    base = [seed[k] + order[k] * sine_ref[...] for k in range(ORDERS)]
    zero = jnp.zeros_like(x)
    small = 2.0**-SHIFT
    unit = SHIFT * math.log(2.0)

    def block(step, carry):
        current, previous, count = (list(part) for part in carry)
        first = step * BLOCK
        factor = [None] * ORDERS
        for offset in range(BLOCK):
            if offset % 8 == 0:
                for k in range(ORDERS):
                    big = jnp.maximum(jnp.abs(current[k]), jnp.abs(previous[k])) > 1.0
                    scale = jnp.where(big, small, 1.0)
                    current[k] = current[k] * scale
                    previous[k] = previous[k] * scale
                    count[k] = count[k] + jnp.where(big, 1.0, 0.0)
                    factor[k] = jnp.exp(base[k] + unit * count[k]) * root
            for k in range(ORDERS):
                at = k * L + first + offset
                advanced = (up[at] * x) * current[k] - back[at] * previous[k] + start[at]
                previous[k] = current[k]
                current[k] = advanced
                buf[k, offset * 8 : offset * 8 + 8, :] = advanced * factor[k]
        for k in range(ORDERS):
            for row in range(6):
                low = buf[k, pl.ds(row, 8, stride=8), :]
                high = buf[k, pl.ds(64 + row, 8, stride=8), :]
                both = jnp.concatenate([low, high], axis=0).astype(BF16)
                width = min(128, LAT - row * 128)
                rows = pl.ds(pl.multiple_of(first, BLOCK), BLOCK)
                out[k, rows, row * 128 : row * 128 + width] = both[:, :width]
        return tuple(current), tuple(previous), tuple(count)

    none = (zero,) * ORDERS
    lax.fori_loop(0, L // BLOCK, block, (none, none, none))


def legendre_table(first_order):
    orders = first_order + jnp.arange(ORDERS, dtype=jnp.int32)
    order = orders.astype(F32)
    seed = lax.dynamic_slice(jnp.asarray(seed_constants()), (first_order,), (ORDERS,))
    slot = jnp.arange(1024, dtype=jnp.int32)
    live = slot < LAT
    slot = jnp.minimum(slot, LAT - 1)
    row = ROWS * (slot % (LATS * SLOT) // SLOT) + SLOT * (slot // (LATS * SLOT)) + slot % SLOT
    angle = (row.astype(F32) + 0.5) * (math.pi / LAT)
    sine = jnp.sin(angle)
    x = jnp.where(live, jnp.cos(angle), 0.0).reshape(8, 128)
    root = jnp.where(live, jnp.sqrt(sine * (math.pi / LAT)), 0.0).reshape(8, 128)
    log_sine = jnp.log(sine).reshape(8, 128)
    degree = jnp.arange(L, dtype=jnp.int32)[None, :]
    past = degree > orders[:, None]
    val, ord_val = degree.astype(F32), order[:, None]
    divisor = jnp.where(past, val * val - ord_val * ord_val, 1.0)
    up = jnp.where(past, jnp.sqrt(jnp.maximum((4.0 * val * val - 1.0) / divisor, 0.0)), 0.0)
    lower = (val - 1.0) * (val - 1.0) - ord_val * ord_val
    back = jnp.sqrt(
        jnp.maximum(lower * (2.0 * val + 1.0) / ((2.0 * val - 3.0) * divisor), 0.0)
    )
    back = jnp.where(past, back, 0.0)
    start = (degree == orders[:, None]).astype(F32)
    smem = pl.BlockSpec(memory_space=pltpu.SMEM)
    vmem = pl.BlockSpec(memory_space=pltpu.VMEM)
    return pl.pallas_call(
        legendre_kernel,
        out_shape=jax.ShapeDtypeStruct((ORDERS, L, LAT), BF16),
        in_specs=[smem] * 5 + [vmem] * 3,
        out_specs=vmem,
        scratch_shapes=[pltpu.VMEM((ORDERS, 8 * BLOCK, 128), F32)],
        name="legendre",
    )(up.reshape(-1), back.reshape(-1), start.reshape(-1), seed, order, x, root, log_sine)


def eye(rows, cols):
    same = lax.broadcasted_iota(jnp.int32, (rows, cols), 0) == lax.broadcasted_iota(
        jnp.int32, (rows, cols), 1
    )
    return same.astype(F32).astype(BF16)


def spread_kernel(x_ref, out_ref):
    @pl.when(pl.program_id(0) < USED)
    def _():
        unit = eye(PAD, COLS)
        for t in range(SLOT):
            out_ref[0, t] = lax.dot_general(
                unit, x_ref[t], (((1,), (1,)), ((), ())), preferred_element_type=F32
            ).astype(BF16)

    @pl.when(pl.program_id(0) >= USED)
    def _():
        out_ref[...] = jnp.zeros_like(out_ref)


def spread(x):
    return pl.pallas_call(
        spread_kernel,
        grid=(LONS,),
        out_shape=jax.ShapeDtypeStruct((LONS, SLOT, PAD, C), BF16),
        in_specs=[pl.BlockSpec((SLOT, C, COLS), lambda g: (jnp.minimum(g, USED - 1), 0, 0))],
        out_specs=pl.BlockSpec((1, SLOT, PAD, C), lambda g: (g, 0, 0, 0)),
        name="spread",
    )(x)


def collect_kernel(x_ref, out_ref):
    unit = eye(PAD, COLS)
    for t in range(SLOT):
        out_ref[t] = lax.dot_general(
            x_ref[0, t], unit, (((0,), (0,)), ((), ())), preferred_element_type=F32
        ).astype(BF16)


def collect(x):
    return pl.pallas_call(
        collect_kernel,
        grid=(USED,),
        out_shape=jax.ShapeDtypeStruct((ROWS, C, COLS), BF16),
        in_specs=[pl.BlockSpec((1, SLOT, PAD, C), lambda g: (g, 0, 0, 0))],
        out_specs=pl.BlockSpec((SLOT, C, COLS), lambda g: (g, 0, 0)),
        name="collect",
    )(x)


def forward_kernel(table, x_ref, out_ref, buf):
    rows = table.shape[0]
    for pair in range(SLOT // 2):
        right = jnp.concatenate(
            [x_ref[:, 2 * pair + half].reshape(LONS * PAD, C) for half in range(2)], axis=1
        )
        done = jnp.dot(table[...], right, preferred_element_type=F32)
        for half in range(2):
            buf[pl.ds(2 * pair + half, rows, stride=SLOT), :] = done[:, half * C : half * C + C]
    out_ref[...] = buf[...].astype(BF16)


def fourier_forward(table, x):
    steps = 2
    rows = 2 * M // steps
    return pl.pallas_call(
        forward_kernel,
        grid=(steps,),
        out_shape=jax.ShapeDtypeStruct((2 * M * SLOT, C), BF16),
        in_specs=[
            pl.BlockSpec((rows, LONS * PAD), lambda g: (g, 0)),
            pl.BlockSpec((LONS, SLOT, PAD, C), lambda g: (0, 0, 0, 0)),
        ],
        out_specs=pl.BlockSpec((rows * SLOT, C), lambda g: (g, 0)),
        scratch_shapes=[pltpu.VMEM((rows * SLOT, C), F32)],
        name="fourier_forward",
    )(table, x)


def backward_kernel(table, x_ref, out_ref):
    for pair in range(SLOT // 2):
        right = jnp.concatenate([x_ref[2 * pair], x_ref[2 * pair + 1]], axis=1)
        done = jnp.dot(table[...], right, preferred_element_type=F32).astype(BF16)
        for half in range(2):
            for j in range(out_ref.shape[0]):
                out_ref[j, 2 * pair + half] = done[
                    j * PAD : j * PAD + PAD, half * C : half * C + C
                ]


def fourier_backward(table, x):
    steps = 4
    each = LONS // steps
    return pl.pallas_call(
        backward_kernel,
        grid=(steps,),
        out_shape=jax.ShapeDtypeStruct((LONS, SLOT, PAD, C), BF16),
        in_specs=[
            pl.BlockSpec((each * PAD, 2 * M), lambda g: (g, 0)),
            pl.BlockSpec((SLOT, 2 * M, C), lambda g: (0, 0, 0)),
        ],
        out_specs=pl.BlockSpec((each, SLOT, PAD, C), lambda g: (g, 0, 0, 0)),
        name="fourier_backward",
    )(table, x)


def transform_kernel(table, x_ref, out_ref, buf):
    g = pl.program_id(0)
    rows = table.shape[1]
    right = jnp.concatenate([x_ref[0], x_ref[1]], axis=1)
    done = jnp.dot(table[0], right, preferred_element_type=F32)
    for half in range(2):
        buf[pl.ds(2 * g + half, rows, stride=Q), :] = done[:, half * C : half * C + C]

    @pl.when(g == ORDERS - 1)
    def _():
        out_ref[: rows * Q, :] = buf[...].astype(BF16)
        if out_ref.shape[0] > rows * Q:
            out_ref[rows * Q :, :] = jnp.zeros((out_ref.shape[0] - rows * Q, C), BF16)


def transform(table, x, out_rows, name):
    _, rows, inner = table.shape
    return pl.pallas_call(
        transform_kernel,
        grid=(ORDERS,),
        out_shape=jax.ShapeDtypeStruct((out_rows, C), BF16),
        in_specs=[
            pl.BlockSpec((1, rows, inner), lambda g: (g, 0, 0)),
            pl.BlockSpec((2, inner, C), lambda g: (g, 0, 0)),
        ],
        out_specs=pl.BlockSpec((out_rows, C), lambda g: (0, 0)),
        scratch_shapes=[pltpu.VMEM((rows * Q, C), F32)],
        name=name,
    )(table, x)


def exchange(x, axis):
    return lax.all_to_all(x, axis, split_axis=0, concat_axis=0, tiled=True)


def share_sum(partial):
    me = lax.axis_index("lon")
    held = partial.reshape(DEGREES, 2, 2, 2, 2, C // LONS, C)
    for bit in range(4):
        axis = 4 - bit
        mine = (me >> bit) & 1
        keep = lax.dynamic_index_in_dim(held, mine, axis, keepdims=False)
        give = lax.dynamic_index_in_dim(held, 1 - mine, axis, keepdims=False)
        got = lax.ppermute(
            give.astype(BF16), "lon", [(k, k ^ (1 << bit)) for k in range(LONS)]
        )
        held = keep + got.astype(F32)
    return held


def on_device(grad_out, spectrum, weights):
    both = ("lon", "lat")
    first_order = (lax.axis_index("lon") * LATS + lax.axis_index("lat")) * ORDERS
    rows = exchange(spread(grad_out[0]), "lon")
    forward, backward = fourier_tables()
    legendre = legendre_table(first_order)
    turned = jnp.swapaxes(legendre, 1, 2)
    stored = spectrum.reshape(LATS * ORDERS, DEGREES, 2, C).transpose(1, 0, 2, 3)
    stored = stored.reshape(DEGREES, LATS * Q, C)

    spectra = fourier_forward(forward, rows).reshape(LATS * LONS, Q, SLOT // 2, 2, C)
    columns = exchange(spectra, both)[: USED * LATS]
    columns = columns.transpose(1, 0, 2, 3, 4).reshape(Q, LAT, C)
    analysed = transform(legendre, columns, L * Q, "legendre_forward")
    gathered = exchange(analysed.reshape(LATS, DEGREES, ORDERS, 2, C), "lat")
    gathered = gathered.transpose(1, 0, 2, 3, 4).reshape(DEGREES, LATS * Q, C)
    spec_local = jnp.einsum("lrd,lcd->lrc", gathered, weights, preferred_element_type=F32)
    spec_local = spec_local.astype(BF16).reshape(DEGREES, LATS, Q, C).transpose(1, 2, 0, 3)
    spec_local = spec_local.reshape(LATS, Q, DEGREES // 2, 2, C)
    partial_sum = jnp.einsum("lrc,lrd->lcd", stored, gathered, preferred_element_type=F32)
    weight_grad = share_sum(partial_sum)

    spec_grad = exchange(spec_local, "lat").transpose(1, 0, 2, 3, 4).reshape(Q, L, C)
    col_grad = transform(turned, spec_grad, LATS * LONS * SLOT * Q, "legendre_backward")
    row_block = exchange(col_grad.reshape(LATS * LONS, SLOT, ORDERS, 2, C), both)
    row_block = row_block.transpose(1, 0, 2, 3, 4).reshape(SLOT, 2 * M, C)
    grid_part = fourier_backward(backward, row_block)
    grad_in = collect(exchange(grid_part, "lon"))
    return grad_in[None], weight_grad


def solution(mesh):
    in_specs = (
        P(None, "lat", None, "lon"),
        P("lon", "lat", None, None, None),
        P("lat", None, None),
    )
    out_specs = (P(None, "lat", None, "lon"), P("lat", "lon", None))
    return jax.shard_map(
        on_device, mesh=mesh, in_specs=in_specs, out_specs=out_specs, check_vma=False
    )
```

```python
import math

import jax
import jax.numpy as jnp
import numpy as np
from jax import lax
from jax.experimental import pallas as pl
from jax.experimental.pallas import tpu as pltpu
from jax.sharding import PartitionSpec as P

LAT = 720
LON = 1440
L = 720
M = 640
C = 128
LATS = 8
LONS = 16
DEVICES = LATS * LONS
ROWS = LAT // LATS
COLS = LON // LONS
SLOT = 6
USED = ROWS // SLOT
PAD = 96
ORDERS = M // (LATS * LONS)
Q = 2 * ORDERS
CHUNK = Q * SLOT
DEGREES = L // LATS
BLOCK = 16
SHIFT = 40

F32 = jnp.float32
BF16 = jnp.bfloat16


def cosine_values(position, order, part):
    step = position * order + part * (LON // 4)
    turn = step - LON * jnp.floor(step * (1.0 / LON))
    fold = (LON // 4) - jnp.abs(turn - LON // 2)
    angle = fold * (2.0 * math.pi / LON)
    square = angle * angle
    series = -1.0 / 39916800.0
    for term in (1.0 / 362880.0, -1.0 / 5040.0, 1.0 / 120.0, -1.0 / 6.0, 1.0):
        series = series * square + term
    return -(angle * series) * (1.0 / math.sqrt(LON))


def fourier_tables():
    def line(shape, axis):
        at = lax.broadcasted_iota(jnp.int32, shape, axis)
        inner = at % PAD
        return (at // PAD * COLS + inner).astype(F32), (inner < COLS).astype(F32)

    def modes(shape, axis):
        at = lax.broadcasted_iota(jnp.int32, shape, axis)
        return (at // 2).astype(F32), (at % 2).astype(F32)

    wide = LONS * PAD
    position, live = line((1, wide), 1)
    order, part = modes((2 * M, 1), 0)
    forward = (cosine_values(position, order, part) * live).astype(BF16)
    position, live = line((wide, 1), 0)
    order, part = modes((1, 2 * M), 1)
    backward = (cosine_values(position, order, part) * live).astype(BF16)
    return forward, backward


def seed_constants():
    out = []
    for m in range(M):
        out.append(
            0.5 * math.log(m + 0.5)
            + 0.5 * math.lgamma(2.0 * m + 1.0)
            - math.lgamma(m + 1.0)
            - m * math.log(2.0)
        )
    return np.asarray(out, np.float32)


def legendre_kernel(up, back, start, seed, order, x_ref, root_ref, sine_ref, out, buf):
    x = x_ref[...]
    root = root_ref[...]
    base = [seed[k] + order[k] * sine_ref[...] for k in range(ORDERS)]
    zero = jnp.zeros_like(x)
    small = 2.0**-SHIFT
    unit = SHIFT * math.log(2.0)

    def block(first, row, steps, carry):
        current, previous, count = (list(part) for part in carry)
        factor = [None] * ORDERS
        for offset in range(steps):
            if offset % 8 == 0:
                for k in range(ORDERS):
                    big = jnp.maximum(jnp.abs(current[k]), jnp.abs(previous[k])) > 1.0
                    scale = jnp.where(big, small, 1.0)
                    current[k] = current[k] * scale
                    previous[k] = previous[k] * scale
                    count[k] = count[k] + jnp.where(big, 1.0, 0.0)
                    factor[k] = jnp.exp(base[k] + unit * count[k]) * root
            for k in range(ORDERS):
                at = k * L + first + offset
                advanced = (up[at] * x) * current[k] - back[at] * previous[k] + start[at]
                previous[k] = current[k]
                current[k] = advanced
                buf[k, offset * 8 : offset * 8 + 8, :] = advanced * factor[k]
        for k in range(ORDERS):
            for offset in range(steps, BLOCK):
                buf[k, offset * 8 : offset * 8 + 8, :] = zero
            for tt in range(SLOT):
                low = buf[k, pl.ds(tt, 8, stride=8), :]
                high = buf[k, pl.ds(64 + tt, 8, stride=8), :]
                both = jnp.concatenate([low, high], axis=0).astype(BF16)
                out[k, pl.ds(pl.multiple_of(row, BLOCK), BLOCK), tt * 128 : tt * 128 + 128] = both
        return tuple(current), tuple(previous), tuple(count)

    def band(k, carry):
        first, row = k * DEGREES, k * PAD
        whole = DEGREES // BLOCK

        def inner(step, carry):
            return block(first + step * BLOCK, row + step * BLOCK, BLOCK, carry)

        carry = lax.fori_loop(0, whole, inner, carry)
        done = whole * BLOCK
        return block(first + done, row + done, DEGREES - done, carry)

    none = (zero,) * ORDERS
    lax.fori_loop(0, LATS, band, (none, none, none))


def legendre_table(first_order):
    orders = first_order + jnp.arange(ORDERS, dtype=jnp.int32)
    order = orders.astype(F32)
    seed = lax.dynamic_slice(jnp.asarray(seed_constants()), (first_order,), (ORDERS,))
    slot = jnp.arange(1024, dtype=jnp.int32)
    tt, device = slot // DEVICES, slot % DEVICES
    lon, lat = device // LATS, device % LATS
    live = (tt < SLOT) & (lon < USED)
    row = jnp.where(live, ROWS * lat + SLOT * lon + tt, 0)
    angle = (row.astype(F32) + 0.5) * (math.pi / LAT)
    sine = jnp.sin(angle)
    x = jnp.where(live, jnp.cos(angle), 0.0).reshape(8, 128)
    root = jnp.where(live, jnp.sqrt(sine * (math.pi / LAT)), 0.0).reshape(8, 128)
    log_sine = jnp.log(sine).reshape(8, 128)
    degree = jnp.arange(L, dtype=jnp.int32)[None, :]
    past = degree > orders[:, None]
    val, ord_val = degree.astype(F32), order[:, None]
    divisor = jnp.where(past, val * val - ord_val * ord_val, 1.0)
    up = jnp.where(past, jnp.sqrt(jnp.maximum((4.0 * val * val - 1.0) / divisor, 0.0)), 0.0)
    lower = (val - 1.0) * (val - 1.0) - ord_val * ord_val
    back = jnp.sqrt(
        jnp.maximum(lower * (2.0 * val + 1.0) / ((2.0 * val - 3.0) * divisor), 0.0)
    )
    back = jnp.where(past, back, 0.0)
    start = (degree == orders[:, None]).astype(F32)
    smem = pl.BlockSpec(memory_space=pltpu.SMEM)
    vmem = pl.BlockSpec(memory_space=pltpu.VMEM)
    return pl.pallas_call(
        legendre_kernel,
        out_shape=jax.ShapeDtypeStruct((ORDERS, LATS * PAD, DEVICES * SLOT), BF16),
        in_specs=[smem] * 5 + [vmem] * 3,
        out_specs=vmem,
        scratch_shapes=[pltpu.VMEM((ORDERS, 8 * BLOCK, 128), F32)],
        name="legendre",
    )(up.reshape(-1), back.reshape(-1), start.reshape(-1), seed, order, x, root, log_sine)


def forward_kernel(table, x_ref, out_ref, buf):
    rows = table.shape[0]
    for pair in range(SLOT // 2):
        right = jnp.concatenate(
            [x_ref[:, 2 * pair + half].reshape(LONS * PAD, C) for half in range(2)], axis=1
        )
        done = jnp.dot(table[...], right, preferred_element_type=F32)
        for half in range(2):
            buf[pl.ds(2 * pair + half, rows, stride=SLOT), :] = done[:, half * C : half * C + C]
    out_ref[...] = buf[...].astype(BF16)


def fourier_forward(table, x):
    steps = 2
    rows = 2 * M // steps
    return pl.pallas_call(
        forward_kernel,
        grid=(steps,),
        out_shape=jax.ShapeDtypeStruct((2 * M * SLOT, C), BF16),
        in_specs=[
            pl.BlockSpec((rows, LONS * PAD), lambda g: (g, 0)),
            pl.BlockSpec((LONS, SLOT, PAD, C), lambda g: (0, 0, 0, 0)),
        ],
        out_specs=pl.BlockSpec((rows * SLOT, C), lambda g: (g, 0)),
        scratch_shapes=[pltpu.VMEM((rows * SLOT, C), F32)],
        name="fourier_forward",
    )(table, x)


def analyse_kernel(table, x_ref, out_ref, wide):
    g = pl.program_id(0)

    @pl.when(g == 0)
    def _():
        wide[...] = x_ref[...].astype(F32)

    def column(q):
        parts = [wide[pl.ds(q * SLOT + tt, DEVICES, stride=CHUNK), :] for tt in range(SLOT)]
        return jnp.concatenate(parts, axis=0).astype(BF16)

    right = jnp.concatenate([column(2 * g), column(2 * g + 1)], axis=1)
    done = jnp.dot(table[0], right, preferred_element_type=F32).astype(BF16)
    for half in range(2):
        out_ref[:, half] = done[:, half * C : half * C + C].reshape(LATS, PAD, C)


def analyse(table, x):
    return pl.pallas_call(
        analyse_kernel,
        grid=(ORDERS,),
        out_shape=jax.ShapeDtypeStruct((LATS, Q, PAD, C), BF16),
        in_specs=[
            pl.BlockSpec((1, LATS * PAD, DEVICES * SLOT), lambda g: (g, 0, 0)),
            pl.BlockSpec((DEVICES * CHUNK, C), lambda g: (0, 0)),
        ],
        out_specs=pl.BlockSpec((LATS, 2, PAD, C), lambda g: (0, g, 0, 0)),
        scratch_shapes=[pltpu.VMEM((DEVICES * CHUNK, C), F32)],
        name="analyse",
    )(table, x)


def mix_kernel(x_ref, weights, gathered, out_ref, wide, made):
    g = pl.program_id(0)
    each = weights.shape[0]

    @pl.when(g == 0)
    def _():
        wide[...] = x_ref[...].astype(F32)
        made[...] = jnp.zeros_like(made)

    for offset in range(each):
        rows = pl.ds(g * each + offset, LATS * Q, stride=PAD)
        part = wide[rows, :].astype(BF16)
        gathered[offset] = part
        made[rows, :] = lax.dot_general(
            part, weights[offset], (((1,), (1,)), ((), ())), preferred_element_type=F32
        )

    @pl.when(g == pl.num_programs(0) - 1)
    def _():
        out_ref[...] = made[...].astype(BF16)


def mix(x, weights):
    steps = 10
    each = DEGREES // steps
    whole = LATS * Q * PAD
    return pl.pallas_call(
        mix_kernel,
        grid=(steps,),
        out_shape=(
            jax.ShapeDtypeStruct((DEGREES, LATS * Q, C), BF16),
            jax.ShapeDtypeStruct((whole, C), BF16),
        ),
        in_specs=[
            pl.BlockSpec((whole, C), lambda g: (0, 0)),
            pl.BlockSpec((each, C, C), lambda g: (g, 0, 0)),
        ],
        out_specs=(
            pl.BlockSpec((each, LATS * Q, C), lambda g: (g, 0, 0)),
            pl.BlockSpec((whole, C), lambda g: (0, 0)),
        ),
        scratch_shapes=[pltpu.VMEM((whole, C), F32), pltpu.VMEM((whole, C), F32)],
        name="mix",
    )(x, weights)


def synthesise_kernel(table, x_ref, out_ref, made):
    g = pl.program_id(0)
    right = jnp.concatenate([x_ref[:, half].reshape(LATS * PAD, C) for half in range(2)], axis=1)
    done = jnp.dot(table[0], right, preferred_element_type=F32)
    for half in range(2):
        for tt in range(SLOT):
            made[pl.ds((2 * g + half) * SLOT + tt, DEVICES, stride=CHUNK), :] = done[
                tt * DEVICES : tt * DEVICES + DEVICES, half * C : half * C + C
            ]

    @pl.when(g == ORDERS - 1)
    def _():
        out_ref[...] = made[...].astype(BF16)


def synthesise(table, x):
    return pl.pallas_call(
        synthesise_kernel,
        grid=(ORDERS,),
        out_shape=jax.ShapeDtypeStruct((DEVICES * CHUNK, C), BF16),
        in_specs=[
            pl.BlockSpec((1, DEVICES * SLOT, LATS * PAD), lambda g: (g, 0, 0)),
            pl.BlockSpec((LATS, 2, PAD, C), lambda g: (0, g, 0, 0)),
        ],
        out_specs=pl.BlockSpec((DEVICES * CHUNK, C), lambda g: (0, 0)),
        scratch_shapes=[pltpu.VMEM((DEVICES * CHUNK, C), F32)],
        name="synthesise",
    )(table, x)


def backward_kernel(table, x_ref, out_ref, wide, right):
    @pl.when(pl.program_id(0) == 0)
    def _():
        wide[...] = x_ref[...].astype(F32)
        for tt in range(SLOT):
            right[:, tt * C : tt * C + C] = wide[pl.ds(tt, 2 * M, stride=SLOT), :].astype(BF16)

    for pair in range(SLOT // 2):
        both = right[:, 2 * pair * C : 2 * pair * C + 2 * C]
        done = jnp.dot(table[...], both, preferred_element_type=F32).astype(BF16)
        for half in range(2):
            for j in range(out_ref.shape[0]):
                out_ref[j, 2 * pair + half] = done[
                    j * PAD : j * PAD + PAD, half * C : half * C + C
                ]


def fourier_backward(table, x):
    steps = 4
    each = LONS // steps
    return pl.pallas_call(
        backward_kernel,
        grid=(steps,),
        out_shape=jax.ShapeDtypeStruct((LONS, SLOT, PAD, C), BF16),
        in_specs=[
            pl.BlockSpec((each * PAD, 2 * M), lambda g: (g, 0)),
            pl.BlockSpec((DEVICES * CHUNK, C), lambda g: (0, 0)),
        ],
        out_specs=pl.BlockSpec((each, SLOT, PAD, C), lambda g: (g, 0, 0, 0)),
        scratch_shapes=[
            pltpu.VMEM((DEVICES * CHUNK, C), F32),
            pltpu.VMEM((2 * M, SLOT * C), BF16),
        ],
        name="fourier_backward",
    )(table, x)


def exchange(x, axis):
    return lax.all_to_all(x, axis, split_axis=0, concat_axis=0, tiled=True)


def halve(held, bit, axis):
    mine = (lax.axis_index("lon") >> bit) & 1
    keep = lax.dynamic_index_in_dim(held, mine, axis, keepdims=False)
    give = lax.dynamic_index_in_dim(held, 1 - mine, axis, keepdims=False)
    got = lax.ppermute(give.astype(BF16), "lon", [(k, k ^ (1 << bit)) for k in range(LONS)])
    return keep.astype(F32) + got.astype(F32)


def cells(x):
    return x.reshape(DEVICES, CHUNK // 2, 2, C)


def on_device(grad_out, spectrum, weights):
    both = ("lon", "lat")
    first_order = (lax.axis_index("lon") * LATS + lax.axis_index("lat")) * ORDERS
    rows = jnp.swapaxes(grad_out[0], 1, 2)
    rows = jnp.pad(rows, ((0, LONS * SLOT - ROWS), (0, PAD - COLS), (0, 0)))
    rows = exchange(rows.reshape(LONS, SLOT, PAD, C), "lon")
    forward, backward = fourier_tables()
    legendre = legendre_table(first_order)
    rows, forward, legendre = lax.optimization_barrier((rows, forward, legendre))

    spectra = fourier_forward(forward, rows)
    columns = exchange(cells(spectra), both).reshape(DEVICES * CHUNK, C)
    turned = jnp.swapaxes(legendre, 1, 2)
    stored = spectrum.reshape(LATS * ORDERS, DEGREES, 2, C).transpose(1, 0, 2, 3)
    stored = stored.reshape(DEGREES, LATS * Q, C)
    columns, turned, stored = lax.optimization_barrier((columns, turned, stored))

    analysed = exchange(analyse(legendre, columns), "lat").reshape(LATS * Q * PAD, C)
    analysed, backward = lax.optimization_barrier((analysed, backward))
    gathered, spec_local = mix(analysed, weights)
    spec_grad = exchange(spec_local.reshape(LATS, Q, PAD, C), "lat")

    held = jnp.einsum("lrc,lrd->lcd", stored, gathered, preferred_element_type=F32)
    held = held.reshape(DEGREES, 2, 2, 2, 2, C // LONS, C)
    held = halve(halve(held, 0, 4), 2, 2)
    spec_grad, held = lax.optimization_barrier((spec_grad, held))

    row_block = exchange(cells(synthesise(turned, spec_grad)), both)
    held = halve(held, 3, 1)
    row_block, held = lax.optimization_barrier((row_block, held))
    grid_part = fourier_backward(backward, row_block.reshape(DEVICES * CHUNK, C))
    grid_part = exchange(grid_part, "lon")
    weight_grad = halve(held, 1, 1)
    grad_in = grid_part[:USED].reshape(ROWS, PAD, C)[:, :COLS]
    return jnp.swapaxes(grad_in, 1, 2)[None], weight_grad


def solution(mesh):
    in_specs = (
        P(None, "lat", None, "lon"),
        P("lon", "lat", None, None, None),
        P("lat", None, None),
    )
    out_specs = (P(None, "lat", None, "lon"), P("lat", "lon", None))
    return jax.shard_map(
        on_device, mesh=mesh, in_specs=in_specs, out_specs=out_specs, check_vma=False
    )
```

```python
import math

import jax
import jax.numpy as jnp
import numpy as np
from jax import lax
from jax.experimental import pallas as pl
from jax.experimental.pallas import tpu as pltpu
from jax.sharding import PartitionSpec as P

LAT = 720
LON = 1440
L = 720
M = 640
C = 128
LATS = 8
LONS = 16
DEVICES = LATS * LONS
ROWS = LAT // LATS
COLS = LON // LONS
SLOT = 6
USED = ROWS // SLOT
PAD = 96
ODD = PAD + 1
ORDERS = M // (LATS * LONS)
Q = 2 * ORDERS
CHUNK = Q * SLOT
DEGREES = L // LATS
BLOCK = 16
SHIFT = 40

F32 = jnp.float32
BF16 = jnp.bfloat16


def limit(mebibytes):
    return pltpu.CompilerParams(vmem_limit_bytes=mebibytes << 20)


def far(x):
    return pltpu.with_memory_space_constraint(x, pltpu.HBM)


def cosine_values(position, order, part):
    step = position * order + part * (LON // 4)
    turn = step - LON * jnp.floor(step * (1.0 / LON))
    fold = (LON // 4) - jnp.abs(turn - LON // 2)
    angle = fold * (2.0 * math.pi / LON)
    square = angle * angle
    series = -1.0 / 39916800.0
    for term in (1.0 / 362880.0, -1.0 / 5040.0, 1.0 / 120.0, -1.0 / 6.0, 1.0):
        series = series * square + term
    return -(angle * series) * (1.0 / math.sqrt(LON))


def fourier_tables():
    def line(shape, axis):
        at = lax.broadcasted_iota(jnp.int32, shape, axis)
        inner = at % PAD
        return (at // PAD * COLS + inner).astype(F32), (inner < COLS).astype(F32)

    def modes(shape, axis):
        at = lax.broadcasted_iota(jnp.int32, shape, axis)
        return (at // 2).astype(F32), (at % 2).astype(F32)

    wide = LONS * PAD
    position, live = line((1, wide), 1)
    order, part = modes((2 * M, 1), 0)
    forward = (cosine_values(position, order, part) * live).astype(BF16)
    position, live = line((wide, 1), 0)
    order, part = modes((1, 2 * M), 1)
    backward = (cosine_values(position, order, part) * live).astype(BF16)
    return forward, backward


def seed_constants():
    out = []
    for m in range(M):
        out.append(
            0.5 * math.log(m + 0.5)
            + 0.5 * math.lgamma(2.0 * m + 1.0)
            - math.lgamma(m + 1.0)
            - m * math.log(2.0)
        )
    return np.asarray(out, np.float32)


def legendre_kernel(up, back, start, seed, order, x_ref, root_ref, sine_ref, out, buf):
    x = x_ref[...]
    root = root_ref[...]
    base = [seed[k] + order[k] * sine_ref[...] for k in range(ORDERS)]
    zero = jnp.zeros_like(x)
    small = 2.0**-SHIFT
    unit = SHIFT * math.log(2.0)

    def block(first, row, steps, carry):
        current, previous, count = (list(part) for part in carry)
        factor = [None] * ORDERS
        for offset in range(steps):
            if offset % 8 == 0:
                for k in range(ORDERS):
                    big = jnp.maximum(jnp.abs(current[k]), jnp.abs(previous[k])) > 1.0
                    scale = jnp.where(big, small, 1.0)
                    current[k] = current[k] * scale
                    previous[k] = previous[k] * scale
                    count[k] = count[k] + jnp.where(big, 1.0, 0.0)
                    factor[k] = jnp.exp(base[k] + unit * count[k]) * root
            for k in range(ORDERS):
                at = k * L + first + offset
                advanced = (up[at] * x) * current[k] - back[at] * previous[k] + start[at]
                previous[k] = current[k]
                current[k] = advanced
                buf[k, offset * 8 : offset * 8 + 8, :] = advanced * factor[k]
        for k in range(ORDERS):
            for offset in range(steps, BLOCK):
                buf[k, offset * 8 : offset * 8 + 8, :] = zero
            for tt in range(SLOT):
                low = buf[k, pl.ds(tt, 8, stride=8), :]
                high = buf[k, pl.ds(64 + tt, 8, stride=8), :]
                both = jnp.concatenate([low, high], axis=0).astype(BF16)
                out[k, pl.ds(pl.multiple_of(row, BLOCK), BLOCK), tt * 128 : tt * 128 + 128] = both
        return tuple(current), tuple(previous), tuple(count)

    def band(k, carry):
        first, row = k * DEGREES, k * PAD
        whole = DEGREES // BLOCK

        def inner(step, carry):
            return block(first + step * BLOCK, row + step * BLOCK, BLOCK, carry)

        carry = lax.fori_loop(0, whole, inner, carry)
        done = whole * BLOCK
        return block(first + done, row + done, DEGREES - done, carry)

    none = (zero,) * ORDERS
    lax.fori_loop(0, LATS, band, (none, none, none))


def legendre_table(first_order):
    orders = first_order + jnp.arange(ORDERS, dtype=jnp.int32)
    order = orders.astype(F32)
    seed = lax.dynamic_slice(jnp.asarray(seed_constants()), (first_order,), (ORDERS,))
    slot = jnp.arange(1024, dtype=jnp.int32)
    tt, device = slot // DEVICES, slot % DEVICES
    lon, lat = device // LATS, device % LATS
    live = (tt < SLOT) & (lon < USED)
    row = jnp.where(live, ROWS * lat + SLOT * lon + tt, 0)
    angle = (row.astype(F32) + 0.5) * (math.pi / LAT)
    sine = jnp.sin(angle)
    x = jnp.where(live, jnp.cos(angle), 0.0).reshape(8, 128)
    root = jnp.where(live, jnp.sqrt(sine * (math.pi / LAT)), 0.0).reshape(8, 128)
    log_sine = jnp.log(sine).reshape(8, 128)
    degree = jnp.arange(L, dtype=jnp.int32)[None, :]
    past = degree > orders[:, None]
    val, ord_val = degree.astype(F32), order[:, None]
    divisor = jnp.where(past, val * val - ord_val * ord_val, 1.0)
    up = jnp.where(past, jnp.sqrt(jnp.maximum((4.0 * val * val - 1.0) / divisor, 0.0)), 0.0)
    lower = (val - 1.0) * (val - 1.0) - ord_val * ord_val
    back = jnp.sqrt(
        jnp.maximum(lower * (2.0 * val + 1.0) / ((2.0 * val - 3.0) * divisor), 0.0)
    )
    back = jnp.where(past, back, 0.0)
    start = (degree == orders[:, None]).astype(F32)
    smem = pl.BlockSpec(memory_space=pltpu.SMEM)
    vmem = pl.BlockSpec(memory_space=pltpu.VMEM)
    return pl.pallas_call(
        legendre_kernel,
        out_shape=jax.ShapeDtypeStruct((ORDERS, LATS * PAD, DEVICES * SLOT), BF16),
        in_specs=[smem] * 5 + [vmem] * 3,
        out_specs=vmem,
        scratch_shapes=[pltpu.VMEM((ORDERS, 8 * BLOCK, 128), F32)],
        compiler_params=limit(16),
        name="legendre",
    )(up.reshape(-1), back.reshape(-1), start.reshape(-1), seed, order, x, root, log_sine)


def forward_kernel(table, x_ref, out_ref, buf):
    rows = table.shape[0]
    for pair in range(SLOT // 2):
        right = jnp.concatenate(
            [x_ref[:, 2 * pair + half].reshape(LONS * PAD, C) for half in range(2)], axis=1
        )
        done = jnp.dot(table[...], right, preferred_element_type=F32)
        for half in range(2):
            buf[pl.ds(2 * pair + half, rows, stride=SLOT), :] = done[:, half * C : half * C + C]
    out_ref[...] = buf[...].astype(BF16)


def fourier_forward(table, x):
    steps = 4
    rows = 2 * M // steps
    return pl.pallas_call(
        forward_kernel,
        grid=(steps,),
        out_shape=pltpu.HBM((2 * M * SLOT, C), BF16),
        in_specs=[
            pl.BlockSpec((rows, LONS * PAD), lambda g: (g, 0)),
            pl.BlockSpec((LONS, SLOT, PAD, C), lambda g: (0, 0, 0, 0)),
        ],
        out_specs=pl.BlockSpec((rows * SLOT, C), lambda g: (g, 0)),
        scratch_shapes=[pltpu.VMEM((rows * SLOT, C), F32)],
        compiler_params=limit(24),
        name="fourier_forward",
    )(table, x)


def analyse_kernel(table, x_ref, out_ref, wide):
    g = pl.program_id(0)

    @pl.when(g == 0)
    def _():
        wide[...] = x_ref[...].astype(F32)

    def column(q):
        parts = [wide[pl.ds(q * SLOT + tt, DEVICES, stride=CHUNK), :] for tt in range(SLOT)]
        return jnp.concatenate(parts, axis=0).astype(BF16)

    right = jnp.concatenate([column(2 * g), column(2 * g + 1)], axis=1)
    done = jnp.dot(table[0], right, preferred_element_type=F32).astype(BF16)
    for half in range(2):
        out_ref[:, half] = done[:, half * C : half * C + C].reshape(LATS, PAD, C)


def analyse(table, x):
    return pl.pallas_call(
        analyse_kernel,
        grid=(ORDERS,),
        out_shape=pltpu.HBM((LATS, Q, PAD, C), BF16),
        in_specs=[
            pl.BlockSpec((1, LATS * PAD, DEVICES * SLOT), lambda g: (g, 0, 0)),
            pl.BlockSpec((DEVICES * CHUNK, C), lambda g: (0, 0)),
        ],
        out_specs=pl.BlockSpec((LATS, 2, PAD, C), lambda g: (0, g, 0, 0)),
        scratch_shapes=[pltpu.VMEM((DEVICES * CHUNK, C), F32)],
        compiler_params=limit(22),
        name="analyse",
    )(table, x)


def mix_kernel(x_ref, weights, gathered, out_ref, wide, made):
    g = pl.program_id(0)
    each = weights.shape[0]
    slabs = LATS * Q

    @pl.when(g == 0)
    def _():
        for slab in range(slabs):
            wide[slab * ODD : slab * ODD + PAD, :] = x_ref[
                slab * PAD : slab * PAD + PAD, :
            ].astype(F32)
            made[slab * ODD + PAD - 8 : slab * ODD + PAD, :] = jnp.zeros((8, C), F32)

    for offset in range(each):
        rows = pl.ds(g * each + offset, slabs, stride=ODD)
        part = wide[rows, :].astype(BF16)
        gathered[offset] = part
        made[rows, :] = lax.dot_general(
            part, weights[offset], (((1,), (1,)), ((), ())), preferred_element_type=F32
        )

    @pl.when(g == pl.num_programs(0) - 1)
    def _():
        for slab in range(slabs):
            out_ref[slab * PAD : slab * PAD + PAD, :] = made[
                slab * ODD : slab * ODD + PAD, :
            ].astype(BF16)


def mix(x, weights):
    steps = 10
    each = DEGREES // steps
    whole = LATS * Q * PAD
    return pl.pallas_call(
        mix_kernel,
        grid=(steps,),
        out_shape=(
            pltpu.HBM((DEGREES, LATS * Q, C), BF16),
            pltpu.HBM((whole, C), BF16),
        ),
        in_specs=[
            pl.BlockSpec((whole, C), lambda g: (0, 0)),
            pl.BlockSpec((each, C, C), lambda g: (g, 0, 0)),
        ],
        out_specs=(
            pl.BlockSpec((each, LATS * Q, C), lambda g: (g, 0, 0)),
            pl.BlockSpec((whole, C), lambda g: (0, 0)),
        ),
        scratch_shapes=[pltpu.VMEM((LATS * Q * ODD, C), F32)] * 2,
        compiler_params=limit(26),
        name="mix",
    )(x, weights)


def synthesise_kernel(table, x_ref, out_ref, made):
    g = pl.program_id(0)
    right = jnp.concatenate([x_ref[:, half].reshape(LATS * PAD, C) for half in range(2)], axis=1)
    done = jnp.dot(table[0], right, preferred_element_type=F32)
    for half in range(2):
        for tt in range(SLOT):
            made[pl.ds((2 * g + half) * SLOT + tt, DEVICES, stride=CHUNK), :] = done[
                tt * DEVICES : tt * DEVICES + DEVICES, half * C : half * C + C
            ]

    @pl.when(g == ORDERS - 1)
    def _():
        out_ref[...] = made[...].astype(BF16)


def synthesise(table, x):
    return pl.pallas_call(
        synthesise_kernel,
        grid=(ORDERS,),
        out_shape=pltpu.HBM((DEVICES * CHUNK, C), BF16),
        in_specs=[
            pl.BlockSpec((1, DEVICES * SLOT, LATS * PAD), lambda g: (g, 0, 0)),
            pl.BlockSpec((LATS, 2, PAD, C), lambda g: (0, g, 0, 0)),
        ],
        out_specs=pl.BlockSpec((DEVICES * CHUNK, C), lambda g: (0, 0)),
        scratch_shapes=[pltpu.VMEM((DEVICES * CHUNK, C), F32)],
        compiler_params=limit(22),
        name="synthesise",
    )(table, x)


def backward_kernel(table, x_ref, out_ref, wide, right):
    @pl.when(pl.program_id(0) == 0)
    def _():
        wide[...] = x_ref[...].astype(F32)
        for tt in range(SLOT):
            right[:, tt * C : tt * C + C] = wide[pl.ds(tt, 2 * M, stride=SLOT), :].astype(BF16)

    for pair in range(SLOT // 2):
        both = right[:, 2 * pair * C : 2 * pair * C + 2 * C]
        done = jnp.dot(table[...], both, preferred_element_type=F32).astype(BF16)
        for half in range(2):
            for j in range(out_ref.shape[0]):
                out_ref[j, 2 * pair + half] = done[
                    j * PAD : j * PAD + PAD, half * C : half * C + C
                ]


def fourier_backward(table, x):
    steps = 4
    each = LONS // steps
    return pl.pallas_call(
        backward_kernel,
        grid=(steps,),
        out_shape=pltpu.HBM((LONS, SLOT, PAD, C), BF16),
        in_specs=[
            pl.BlockSpec((each * PAD, 2 * M), lambda g: (g, 0)),
            pl.BlockSpec((DEVICES * CHUNK, C), lambda g: (0, 0)),
        ],
        out_specs=pl.BlockSpec((each, SLOT, PAD, C), lambda g: (g, 0, 0, 0)),
        scratch_shapes=[
            pltpu.VMEM((DEVICES * CHUNK, C), F32),
            pltpu.VMEM((2 * M, SLOT * C), BF16),
        ],
        compiler_params=limit(22),
        name="fourier_backward",
    )(table, x)


def exchange(x, axis):
    return lax.all_to_all(x, axis, split_axis=0, concat_axis=0, tiled=True)


def share_cores(held):
    core = lax.axis_index("lon") & 1
    held = held.reshape(DEGREES, LONS // 2, 2, C // LONS, C)
    keep = lax.dynamic_index_in_dim(held, core, 2, keepdims=False)
    give = lax.dynamic_index_in_dim(held, 1 - core, 2, keepdims=False).astype(BF16)
    return keep + lax.ppermute(give, "lon", [(k, k ^ 1) for k in range(LONS)]).astype(F32)


def share_columns(held):
    z = lax.axis_index("lon") >> 2
    held = held.reshape(DEGREES, 4, 2, C // LONS, C)
    got = []
    for step in (1, 3, 2):
        give = lax.dynamic_index_in_dim(held, (z + step) % 4, 1, keepdims=False).astype(BF16)
        pairs = [(k, (k + 4 * step) % LONS) for k in range(LONS)]
        got.append(lax.ppermute(give, "lon", pairs))
    return lax.dynamic_index_in_dim(held, z, 1, keepdims=False), got


def share_pair(held):
    y = (lax.axis_index("lon") >> 1) & 1
    keep = lax.dynamic_index_in_dim(held, y, 1, keepdims=False)
    give = lax.dynamic_index_in_dim(held, 1 - y, 1, keepdims=False).astype(BF16)
    return keep + lax.ppermute(give, "lon", [(k, k ^ 2) for k in range(LONS)]).astype(F32)


def cells(x):
    return x.reshape(DEVICES, CHUNK // 2, 2, C)


def on_device(grad_out, spectrum, weights):
    both = ("lon", "lat")
    first_order = (lax.axis_index("lon") * LATS + lax.axis_index("lat")) * ORDERS
    rows = jnp.swapaxes(grad_out[0], 1, 2)
    rows = jnp.pad(rows, ((0, LONS * SLOT - ROWS), (0, PAD - COLS), (0, 0)))
    rows = exchange(rows.reshape(LONS, SLOT, PAD, C), "lon")
    forward, backward = fourier_tables()
    legendre = legendre_table(first_order)
    rows, forward, legendre = lax.optimization_barrier((rows, forward, legendre))

    spectra = fourier_forward(far(forward), rows)
    columns = exchange(cells(spectra), both).reshape(DEVICES * CHUNK, C)
    turned = jnp.swapaxes(legendre, 1, 2)
    stored = spectrum.reshape(LATS * ORDERS, DEGREES, 2, C).transpose(1, 0, 2, 3)
    stored = stored.reshape(DEGREES, LATS * Q, C)
    columns, turned, stored = lax.optimization_barrier((columns, turned, stored))

    analysed = exchange(analyse(far(legendre), columns), "lat").reshape(LATS * Q * PAD, C)
    analysed, backward = lax.optimization_barrier((analysed, backward))
    gathered, spec_local = mix(analysed, far(weights))
    spec_grad = exchange(spec_local.reshape(LATS, Q, PAD, C), "lat")

    held = jnp.einsum("lrc,lrd->lcd", stored, gathered, preferred_element_type=F32)
    held = share_cores(held)
    held, got = share_columns(held)
    spec_grad, held = lax.optimization_barrier((spec_grad, held))

    row_block = synthesise(far(turned), spec_grad)
    row_block = exchange(cells(row_block), both)
    row_block, held, *got = lax.optimization_barrier((row_block, held, *got))
    for part in got:
        held = held + part.astype(F32)
    grid_part = fourier_backward(far(backward), row_block.reshape(DEVICES * CHUNK, C))
    grid_part = exchange(grid_part, "lon")
    weight_grad = share_pair(held)
    grid_part, weight_grad = lax.optimization_barrier((grid_part, weight_grad))
    grad_in = grid_part[:USED].reshape(ROWS, PAD, C)[:, :COLS]
    return jnp.swapaxes(grad_in, 1, 2)[None], weight_grad


def solution(mesh):
    in_specs = (
        P(None, "lat", None, "lon"),
        P("lon", "lat", None, None, None),
        P("lat", None, None),
    )
    out_specs = (P(None, "lat", None, "lon"), P("lat", "lon", None))
    return jax.shard_map(
        on_device, mesh=mesh, in_specs=in_specs, out_specs=out_specs, check_vma=False
    )
```

```python
import math

import jax
import jax.numpy as jnp
import numpy as np
from jax import lax
from jax.experimental import pallas as pl
from jax.experimental.pallas import tpu as pltpu
from jax.sharding import PartitionSpec as P

LAT = 720
LON = 1440
L = 720
M = 640
C = 128
LATS = 8
LONS = 16
DEVICES = LATS * LONS
ROWS = LAT // LATS
COLS = LON // LONS
SLOT = 6
USED = ROWS // SLOT
PAD = 96
ODD = PAD + 1
ORDERS = M // (LATS * LONS)
Q = 2 * ORDERS
CHUNK = Q * SLOT
DEGREES = L // LATS
BLOCK = 16
TAIL = 2
SHIFT = 40

F32 = jnp.float32
BF16 = jnp.bfloat16


def limit(mebibytes):
    return pltpu.CompilerParams(vmem_limit_bytes=mebibytes << 20)


def near(x):
    return pltpu.with_memory_space_constraint(x, pltpu.VMEM)


def far(x):
    return pltpu.with_memory_space_constraint(x, pltpu.HBM)


def whole(space=pltpu.VMEM):
    return pl.BlockSpec(memory_space=space)


def stream(table, held, ready, steps):
    g = pl.program_id(0)

    def copy(step):
        return pltpu.make_async_copy(table.at[step], held.at[step], ready.at[step])

    @pl.when(g == 0)
    def _():
        for step in range(steps):
            copy(step).start()

    def arrive():
        @pl.when(g < steps)
        def _():
            copy(jnp.minimum(g, steps - 1)).wait()

    return arrive


def streamed(table):
    return [pltpu.VMEM(table.shape, table.dtype), pltpu.SemaphoreType.DMA((table.shape[0],))]


def cosine_values(position, order, part):
    step = position * order + part * (LON // 4)
    turn = step - LON * jnp.floor(step * (1.0 / LON))
    fold = (LON // 4) - jnp.abs(turn - LON // 2)
    angle = fold * (2.0 * math.pi / LON)
    square = angle * angle
    series = -1.0 / 39916800.0
    for term in (1.0 / 362880.0, -1.0 / 5040.0, 1.0 / 120.0, -1.0 / 6.0, 1.0):
        series = series * square + term
    return -(angle * series) * (1.0 / math.sqrt(LON))


def fourier_tables():
    def line(shape, axis):
        at = lax.broadcasted_iota(jnp.int32, shape, axis)
        inner = at % PAD
        return (at // PAD * COLS + inner).astype(F32), (inner < COLS).astype(F32)

    def modes(shape, axis):
        at = lax.broadcasted_iota(jnp.int32, shape, axis)
        return (at // 2).astype(F32), (at % 2).astype(F32)

    wide = LONS * PAD
    position, live = line((1, wide), 1)
    order, part = modes((2 * M, 1), 0)
    forward = (cosine_values(position, order, part) * live).astype(BF16)
    position, live = line((wide, 1), 0)
    order, part = modes((1, 2 * M), 1)
    backward = (cosine_values(position, order, part) * live).astype(BF16)
    return forward, backward


def seed_constants():
    out = []
    for m in range(M):
        out.append(
            0.5 * math.log(m + 0.5)
            + 0.5 * math.lgamma(2.0 * m + 1.0)
            - math.lgamma(m + 1.0)
            - m * math.log(2.0)
        )
    return np.asarray(out, np.float32)


def legendre_kernel(up, back, start, seed, order, x_ref, root_ref, sine_ref, out, buf):
    x = x_ref[...]
    root = root_ref[...]
    base = [seed[k] + order[k] * sine_ref[...] for k in range(ORDERS)]
    zero = jnp.zeros_like(x)
    small = 2.0**-SHIFT
    unit = SHIFT * math.log(2.0)

    def block(first, row, steps, carry):
        current, previous, count = (list(part) for part in carry)
        factor = [None] * ORDERS
        for offset in range(steps):
            if offset % 8 == 0:
                for k in range(ORDERS):
                    big = jnp.maximum(jnp.abs(current[k]), jnp.abs(previous[k])) > 1.0
                    scale = jnp.where(big, small, 1.0)
                    current[k] = current[k] * scale
                    previous[k] = previous[k] * scale
                    count[k] = count[k] + jnp.where(big, 1.0, 0.0)
                    factor[k] = jnp.exp(base[k] + unit * count[k]) * root
            for k in range(ORDERS):
                at = k * L + first + offset
                advanced = (up[at] * x) * current[k] - back[at] * previous[k] + start[at]
                previous[k] = current[k]
                current[k] = advanced
                buf[k, offset * 8 : offset * 8 + 8, :] = advanced * factor[k]
        for k in range(ORDERS):
            for offset in range(steps, BLOCK):
                buf[k, offset * 8 : offset * 8 + 8, :] = zero
            for tt in range(SLOT):
                low = buf[k, pl.ds(tt, 8, stride=8), :]
                high = buf[k, pl.ds(64 + tt, 8, stride=8), :]
                both = jnp.concatenate([low, high], axis=0).astype(BF16)
                out[k, pl.ds(pl.multiple_of(row, BLOCK), BLOCK), tt * 128 : tt * 128 + 128] = both
        return tuple(current), tuple(previous), tuple(count)

    def band(k, carry):
        first, row = k * DEGREES, k * PAD
        whole = DEGREES // BLOCK

        def inner(step, carry):
            return block(first + step * BLOCK, row + step * BLOCK, BLOCK, carry)

        carry = lax.fori_loop(0, whole, inner, carry)
        done = whole * BLOCK
        return block(first + done, row + done, DEGREES - done, carry)

    none = (zero,) * ORDERS
    lax.fori_loop(0, LATS, band, (none, none, none))


def legendre_table(first_order):
    orders = first_order + jnp.arange(ORDERS, dtype=jnp.int32)
    order = orders.astype(F32)
    seed = lax.dynamic_slice(jnp.asarray(seed_constants()), (first_order,), (ORDERS,))
    slot = jnp.arange(1024, dtype=jnp.int32)
    tt, device = slot // DEVICES, slot % DEVICES
    lon, lat = device // LATS, device % LATS
    live = (tt < SLOT) & (lon < USED)
    row = jnp.where(live, ROWS * lat + SLOT * lon + tt, 0)
    angle = (row.astype(F32) + 0.5) * (math.pi / LAT)
    sine = jnp.sin(angle)
    x = jnp.where(live, jnp.cos(angle), 0.0).reshape(8, 128)
    root = jnp.where(live, jnp.sqrt(sine * (math.pi / LAT)), 0.0).reshape(8, 128)
    log_sine = jnp.log(sine).reshape(8, 128)
    degree = jnp.arange(L, dtype=jnp.int32)[None, :]
    past = degree > orders[:, None]
    val, ord_val = degree.astype(F32), order[:, None]
    divisor = jnp.where(past, val * val - ord_val * ord_val, 1.0)
    up = jnp.where(past, jnp.sqrt(jnp.maximum((4.0 * val * val - 1.0) / divisor, 0.0)), 0.0)
    lower = (val - 1.0) * (val - 1.0) - ord_val * ord_val
    back = jnp.sqrt(
        jnp.maximum(lower * (2.0 * val + 1.0) / ((2.0 * val - 3.0) * divisor), 0.0)
    )
    back = jnp.where(past, back, 0.0)
    start = (degree == orders[:, None]).astype(F32)
    smem = pl.BlockSpec(memory_space=pltpu.SMEM)
    vmem = pl.BlockSpec(memory_space=pltpu.VMEM)
    return pl.pallas_call(
        legendre_kernel,
        out_shape=jax.ShapeDtypeStruct((ORDERS, LATS * PAD, DEVICES * SLOT), BF16),
        in_specs=[smem] * 5 + [vmem] * 3,
        out_specs=vmem,
        scratch_shapes=[pltpu.VMEM((ORDERS, 8 * BLOCK, 128), F32)],
        compiler_params=limit(16),
        name="legendre",
    )(up.reshape(-1), back.reshape(-1), start.reshape(-1), seed, order, x, root, log_sine)


def forward_kernel(table, x_ref, out_ref, buf, held, ready):
    steps, rows, _ = held.shape
    arrive = stream(table, held, ready, steps)
    arrive()
    for pair in range(SLOT // 2):
        right = jnp.concatenate(
            [x_ref[:, 2 * pair + half].reshape(LONS * PAD, C) for half in range(2)], axis=1
        )
        done = jnp.dot(held[pl.program_id(0)], right, preferred_element_type=F32)
        for half in range(2):
            buf[pl.ds(2 * pair + half, rows, stride=SLOT), :] = done[:, half * C : half * C + C]
    out_ref[...] = buf[...].astype(BF16)


def fourier_forward(table, x):
    steps = 2
    rows = 2 * M // steps
    table = table.reshape(steps, rows, LONS * PAD)
    return pl.pallas_call(
        forward_kernel,
        grid=(steps,),
        out_shape=pltpu.HBM((2 * M * SLOT, C), BF16),
        in_specs=[whole(pltpu.HBM), whole()],
        out_specs=pl.BlockSpec((rows * SLOT, C), lambda g: (g, 0)),
        scratch_shapes=[pltpu.VMEM((rows * SLOT, C), F32)] + streamed(table),
        compiler_params=limit(24),
        name="fourier_forward",
    )(far(table), near(x))


def analyse_kernel(table, x_ref, out_ref, wide, held, ready):
    g = pl.program_id(0)
    arrive = stream(table, held, ready, ORDERS)

    @pl.when(g == 0)
    def _():
        wide[...] = x_ref[...].astype(F32)

    def column(q):
        parts = [wide[pl.ds(q * SLOT + tt, DEVICES, stride=CHUNK), :] for tt in range(SLOT)]
        return jnp.concatenate(parts, axis=0).astype(BF16)

    right = jnp.concatenate([column(2 * g), column(2 * g + 1)], axis=1)
    arrive()
    done = jnp.dot(held[g], right, preferred_element_type=F32).astype(BF16)
    for half in range(2):
        out_ref[:, half] = done[:, half * C : half * C + C].reshape(LATS, PAD, C)


def analyse(table, x):
    return pl.pallas_call(
        analyse_kernel,
        grid=(ORDERS,),
        out_shape=pltpu.HBM((LATS, Q, PAD, C), BF16),
        in_specs=[whole(pltpu.HBM), whole()],
        out_specs=pl.BlockSpec((LATS, 2, PAD, C), lambda g: (0, g, 0, 0)),
        scratch_shapes=[pltpu.VMEM((DEVICES * CHUNK, C), F32)] + streamed(table),
        compiler_params=limit(26),
        name="analyse",
    )(far(table), near(x))


def mix_kernel(x_ref, weights, gathered, out_ref, wide, made, held, ready):
    g = pl.program_id(0)
    steps, each = held.shape[:2]
    slabs = LATS * Q
    arrive = stream(weights, held, ready, steps)

    @pl.when(g == 0)
    def _():
        for slab in range(slabs):
            wide[slab * ODD : slab * ODD + PAD, :] = x_ref[
                slab * PAD : slab * PAD + PAD, :
            ].astype(F32)
            made[slab * ODD + PAD - 8 : slab * ODD + PAD, :] = jnp.zeros((8, C), F32)

    arrive()

    @pl.when(g < steps)
    def _():
        for offset in range(each):
            rows = pl.ds(g * each + offset, slabs, stride=ODD)
            part = wide[rows, :].astype(BF16)
            gathered[offset] = part
            made[rows, :] = lax.dot_general(
                part, held[g, offset], (((1,), (1,)), ((), ())), preferred_element_type=F32
            )

    for step in range(TAIL):

        @pl.when(g == steps + step)
        def _():
            for slab in range(slabs // TAIL):
                first = (step * (slabs // TAIL) + slab) * ODD
                out_ref[slab * PAD : slab * PAD + PAD, :] = made[first : first + PAD, :].astype(
                    BF16
                )


def mix(x, weights):
    steps = 5
    each = DEGREES // steps
    size = LATS * Q * PAD
    weights = weights.reshape(steps, each, C, C)
    return pl.pallas_call(
        mix_kernel,
        grid=(steps + TAIL,),
        out_shape=(
            pltpu.HBM((DEGREES, LATS * Q, C), BF16),
            pltpu.HBM((size, C), BF16),
        ),
        in_specs=[whole(), whole(pltpu.HBM)],
        out_specs=(
            pl.BlockSpec((each, LATS * Q, C), lambda g: (jnp.minimum(g, steps - 1), 0, 0)),
            pl.BlockSpec((size // TAIL, C), lambda g: (jnp.maximum(g - steps, 0), 0)),
        ),
        scratch_shapes=[pltpu.VMEM((LATS * Q * ODD, C), F32)] * 2 + streamed(weights),
        compiler_params=limit(26),
        name="mix",
    )(near(x), far(weights))


def synthesise_kernel(table, x_ref, out_ref, made, held, ready):
    g = pl.program_id(0)
    arrive = stream(table, held, ready, ORDERS)
    arrive()

    @pl.when(g < ORDERS)
    def _():
        right = jnp.concatenate(
            [x_ref[:, 2 * g + half].reshape(LATS * PAD, C) for half in range(2)], axis=1
        )
        done = jnp.dot(held[g], right, preferred_element_type=F32)
        for half in range(2):
            for tt in range(SLOT):
                made[pl.ds((2 * g + half) * SLOT + tt, DEVICES, stride=CHUNK), :] = done[
                    tt * DEVICES : tt * DEVICES + DEVICES, half * C : half * C + C
                ]

    rows = out_ref.shape[0]
    for step in range(TAIL):

        @pl.when(g == ORDERS + step)
        def _():
            out_ref[...] = made[step * rows : step * rows + rows, :].astype(BF16)


def synthesise(table, x):
    return pl.pallas_call(
        synthesise_kernel,
        grid=(ORDERS + TAIL,),
        out_shape=pltpu.HBM((DEVICES * CHUNK, C), BF16),
        in_specs=[whole(pltpu.HBM), whole()],
        out_specs=pl.BlockSpec(
            (DEVICES * CHUNK // TAIL, C), lambda g: (jnp.maximum(g - ORDERS, 0), 0)
        ),
        scratch_shapes=[pltpu.VMEM((DEVICES * CHUNK, C), F32)] + streamed(table),
        compiler_params=limit(26),
        name="synthesise",
    )(far(table), near(x))


def backward_kernel(table, x_ref, out_ref, wide, right, held, ready):
    arrive = stream(table, held, ready, held.shape[0])

    @pl.when(pl.program_id(0) == 0)
    def _():
        wide[...] = x_ref[...].astype(F32)
        for tt in range(SLOT):
            right[:, tt * C : tt * C + C] = wide[pl.ds(tt, 2 * M, stride=SLOT), :].astype(BF16)

    arrive()
    for pair in range(SLOT // 2):
        both = right[:, 2 * pair * C : 2 * pair * C + 2 * C]
        done = jnp.dot(held[pl.program_id(0)], both, preferred_element_type=F32).astype(BF16)
        for half in range(2):
            for j in range(out_ref.shape[0]):
                out_ref[j, 2 * pair + half] = done[
                    j * PAD : j * PAD + PAD, half * C : half * C + C
                ]


def fourier_backward(table, x):
    steps = 4
    each = LONS // steps
    table = table.reshape(steps, each * PAD, 2 * M)
    return pl.pallas_call(
        backward_kernel,
        grid=(steps,),
        out_shape=pltpu.HBM((LONS, SLOT, PAD, C), BF16),
        in_specs=[whole(pltpu.HBM), whole()],
        out_specs=pl.BlockSpec((each, SLOT, PAD, C), lambda g: (g, 0, 0, 0)),
        scratch_shapes=[
            pltpu.VMEM((DEVICES * CHUNK, C), F32),
            pltpu.VMEM((2 * M, SLOT * C), BF16),
        ]
        + streamed(table),
        compiler_params=limit(24),
        name="fourier_backward",
    )(far(table), near(x))


def exchange(x, axis):
    return lax.all_to_all(x, axis, split_axis=0, concat_axis=0, tiled=True)


def share_cores(held):
    core = lax.axis_index("lon") & 1
    held = held.reshape(DEGREES, LONS // 2, 2, C // LONS, C)
    keep = lax.dynamic_index_in_dim(held, core, 2, keepdims=False)
    give = lax.dynamic_index_in_dim(held, 1 - core, 2, keepdims=False).astype(BF16)
    return keep + lax.ppermute(give, "lon", [(k, k ^ 1) for k in range(LONS)]).astype(F32)


def share_columns(held):
    z = lax.axis_index("lon") >> 2
    held = held.reshape(DEGREES, 4, 2, C // LONS, C)
    got = []
    for step in (1, 3, 2):
        give = lax.dynamic_index_in_dim(held, (z + step) % 4, 1, keepdims=False).astype(BF16)
        pairs = [(k, (k + 4 * step) % LONS) for k in range(LONS)]
        got.append(lax.ppermute(give, "lon", pairs))
    return lax.dynamic_index_in_dim(held, z, 1, keepdims=False), got


def share_pair(held):
    y = (lax.axis_index("lon") >> 1) & 1
    keep = lax.dynamic_index_in_dim(held, y, 1, keepdims=False)
    give = lax.dynamic_index_in_dim(held, 1 - y, 1, keepdims=False).astype(BF16)
    return keep + lax.ppermute(give, "lon", [(k, k ^ 2) for k in range(LONS)]).astype(F32)


def cells(x):
    return x.reshape(DEVICES, CHUNK // 2, 2, C)


def on_device(grad_out, spectrum, weights):
    both = ("lon", "lat")
    first_order = (lax.axis_index("lon") * LATS + lax.axis_index("lat")) * ORDERS
    rows = jnp.swapaxes(grad_out[0], 1, 2)
    rows = jnp.pad(rows, ((0, LONS * SLOT - ROWS), (0, PAD - COLS), (0, 0)))
    rows = exchange(rows.reshape(LONS, SLOT, PAD, C), "lon")
    forward, backward = fourier_tables()
    legendre = legendre_table(first_order)
    rows, forward, legendre = lax.optimization_barrier((rows, forward, legendre))

    spectra = fourier_forward(forward, rows)
    columns = exchange(cells(spectra), both).reshape(DEVICES * CHUNK, C)
    turned = jnp.swapaxes(legendre, 1, 2)
    stored = spectrum.reshape(LATS * ORDERS, DEGREES, 2, C).transpose(1, 0, 2, 3)
    stored = stored.reshape(DEGREES, LATS * Q, C)
    columns, turned, stored = lax.optimization_barrier((columns, turned, stored))

    analysed = exchange(analyse(legendre, columns), "lat").reshape(LATS * Q * PAD, C)
    analysed, backward = lax.optimization_barrier((analysed, backward))
    gathered, spec_local = mix(analysed, weights)
    spec_grad = exchange(spec_local.reshape(LATS, Q, PAD, C), "lat")

    held = jnp.einsum("lrc,lrd->lcd", stored, gathered, preferred_element_type=F32)
    held = share_cores(held)
    held, got = share_columns(held)
    spec_grad, held = lax.optimization_barrier((spec_grad, held))

    row_block = synthesise(turned, spec_grad)
    row_block = exchange(cells(row_block), both)
    for part in got:
        held = held + part.astype(F32)
    row_block, held = lax.optimization_barrier((row_block, held))
    grid_part = fourier_backward(backward, row_block.reshape(DEVICES * CHUNK, C))
    grid_part = exchange(grid_part, "lon")
    weight_grad = share_pair(held)
    grad_in = grid_part[:USED].reshape(ROWS, PAD, C)[:, :COLS]
    return jnp.swapaxes(grad_in, 1, 2)[None], weight_grad


def solution(mesh):
    in_specs = (
        P(None, "lat", None, "lon"),
        P("lon", "lat", None, None, None),
        P("lat", None, None),
    )
    out_specs = (P(None, "lat", None, "lon"), P("lat", "lon", None))
    return jax.shard_map(
        on_device, mesh=mesh, in_specs=in_specs, out_specs=out_specs, check_vma=False
    )
```

```python
import math

import jax
import jax.numpy as jnp
import numpy as np
from jax import lax
from jax.experimental import pallas as pl
from jax.experimental.pallas import tpu as pltpu
from jax.sharding import PartitionSpec as P

LAT = 720
LON = 1440
L = 720
M = 640
C = 128
LATS = 8
LONS = 16
DEVICES = LATS * LONS
ROWS = LAT // LATS
COLS = LON // LONS
SLOT = 6
USED = ROWS // SLOT
PAD = 96
ODD = PAD + 1
ORDERS = M // (LATS * LONS)
HALF = LONS // 2
Q = 2 * ORDERS
CHUNK = Q * SLOT
DEGREES = L // LATS
BLOCK = 16
TAIL = 2
SHIFT = 40

F32 = jnp.float32
BF16 = jnp.bfloat16


def limit(mebibytes):
    return pltpu.CompilerParams(vmem_limit_bytes=mebibytes << 20)


def near(x):
    return pltpu.with_memory_space_constraint(x, pltpu.VMEM)


def far(x):
    return pltpu.with_memory_space_constraint(x, pltpu.HBM)


def whole(space=pltpu.VMEM):
    return pl.BlockSpec(memory_space=space)


def stream(table, held, ready, steps):
    g = pl.program_id(0)

    def copy(step):
        return pltpu.make_async_copy(table.at[step], held.at[step], ready.at[step])

    @pl.when(g == 0)
    def _():
        for step in range(steps):
            copy(step).start()

    def arrive():
        @pl.when(g < steps)
        def _():
            copy(jnp.minimum(g, steps - 1)).wait()

    return arrive


def streamed(table):
    return [pltpu.VMEM(table.shape, table.dtype), pltpu.SemaphoreType.DMA((table.shape[0],))]


def cosine_values(position, order, part):
    step = position * order + part * (LON // 4)
    turn = step - LON * jnp.floor(step * (1.0 / LON))
    fold = (LON // 4) - jnp.abs(turn - LON // 2)
    angle = fold * (2.0 * math.pi / LON)
    square = angle * angle
    series = -1.0 / 39916800.0
    for term in (1.0 / 362880.0, -1.0 / 5040.0, 1.0 / 120.0, -1.0 / 6.0, 1.0):
        series = series * square + term
    return -(angle * series) * (1.0 / math.sqrt(LON))


def fourier_tables():
    def line(shape, axis):
        at = lax.broadcasted_iota(jnp.int32, shape, axis)
        inner = at % PAD
        return (at // PAD * COLS + inner).astype(F32), (inner < COLS).astype(F32)

    def modes(shape, axis):
        at = lax.broadcasted_iota(jnp.int32, shape, axis)
        device, kind = at // Q, at % Q
        parity, device = device // (DEVICES // 2), device % (DEVICES // 2)
        lat = device // LONS * 2 + parity
        order = device % LONS * (LATS * ORDERS) + kind // 2 * LATS + lat
        return order.astype(F32), (kind % 2).astype(F32)

    wide = HALF * PAD
    position, live = line((1, wide), 1)
    order, part = modes((2 * M, 1), 0)
    forward = (cosine_values(position, order, part) * live).astype(BF16)
    position, live = line((wide, 1), 0)
    order, part = modes((1, 2 * M), 1)
    backward = (cosine_values(position, order, part) * live).astype(BF16)
    return forward.reshape(2, M, wide), backward


def seed_constants():
    out = []
    for m in range(M):
        out.append(
            0.5 * math.log(m + 0.5)
            + 0.5 * math.lgamma(2.0 * m + 1.0)
            - math.lgamma(m + 1.0)
            - m * math.log(2.0)
        )
    return np.asarray(out, np.float32)


def legendre_kernel(up, back, start, seed, order, x_ref, root_ref, sine_ref, out, buf):
    x = x_ref[...]
    root = root_ref[...]
    base = [seed[k] + order[k] * sine_ref[...] for k in range(ORDERS)]
    zero = jnp.zeros_like(x)
    small = 2.0**-SHIFT
    unit = SHIFT * math.log(2.0)

    def block(first, row, steps, carry):
        current, previous, count = (list(part) for part in carry)
        factor = [None] * ORDERS
        for offset in range(steps):
            if offset % 8 == 0:
                for k in range(ORDERS):
                    big = jnp.maximum(jnp.abs(current[k]), jnp.abs(previous[k])) > 1.0
                    scale = jnp.where(big, small, 1.0)
                    current[k] = current[k] * scale
                    previous[k] = previous[k] * scale
                    count[k] = count[k] + jnp.where(big, 1.0, 0.0)
                    factor[k] = jnp.exp(base[k] + unit * count[k]) * root
            for k in range(ORDERS):
                at = k * L + first + offset
                advanced = (up[at] * x) * current[k] - back[at] * previous[k] + start[at]
                previous[k] = current[k]
                current[k] = advanced
                buf[k, offset * 8 : offset * 8 + 8, :] = advanced * factor[k]
        for k in range(ORDERS):
            for offset in range(steps, BLOCK):
                buf[k, offset * 8 : offset * 8 + 8, :] = zero
            for tt in range(SLOT):
                low = buf[k, pl.ds(tt, 8, stride=8), :]
                high = buf[k, pl.ds(64 + tt, 8, stride=8), :]
                both = jnp.concatenate([low, high], axis=0).astype(BF16)
                out[k, pl.ds(pl.multiple_of(row, BLOCK), BLOCK), tt * 128 : tt * 128 + 128] = both
        return tuple(current), tuple(previous), tuple(count)

    def band(k, carry):
        first, row = k * DEGREES, k * PAD
        whole = DEGREES // BLOCK

        def inner(step, carry):
            return block(first + step * BLOCK, row + step * BLOCK, BLOCK, carry)

        carry = lax.fori_loop(0, whole, inner, carry)
        done = whole * BLOCK
        return block(first + done, row + done, DEGREES - done, carry)

    none = (zero,) * ORDERS
    lax.fori_loop(0, LATS, band, (none, none, none))


def legendre_table():
    lon, lat = lax.axis_index("lon"), lax.axis_index("lat")
    orders = (lon * ORDERS + jnp.arange(ORDERS, dtype=jnp.int32)) * LATS + lat
    order = orders.astype(F32)
    seeds = jnp.asarray(seed_constants().reshape(LONS, ORDERS, LATS))
    seed = lax.dynamic_slice(seeds, (lon, 0, lat), (1, ORDERS, 1)).reshape(ORDERS)
    slot = jnp.arange(1024, dtype=jnp.int32)
    tt, device = slot // DEVICES, slot % DEVICES
    lat, lon = device // LONS, device % LONS
    live = (tt < SLOT) & (lon < USED)
    row = jnp.where(live, ROWS * lat + SLOT * lon + tt, 0)
    angle = (row.astype(F32) + 0.5) * (math.pi / LAT)
    sine = jnp.sin(angle)
    x = jnp.where(live, jnp.cos(angle), 0.0).reshape(8, 128)
    root = jnp.where(live, jnp.sqrt(sine * (math.pi / LAT)), 0.0).reshape(8, 128)
    log_sine = jnp.log(sine).reshape(8, 128)
    degree = jnp.arange(L, dtype=jnp.int32)[None, :]
    past = degree > orders[:, None]
    val, ord_val = degree.astype(F32), order[:, None]
    divisor = jnp.where(past, val * val - ord_val * ord_val, 1.0)
    up = jnp.where(past, jnp.sqrt(jnp.maximum((4.0 * val * val - 1.0) / divisor, 0.0)), 0.0)
    lower = (val - 1.0) * (val - 1.0) - ord_val * ord_val
    back = jnp.sqrt(
        jnp.maximum(lower * (2.0 * val + 1.0) / ((2.0 * val - 3.0) * divisor), 0.0)
    )
    back = jnp.where(past, back, 0.0)
    start = (degree == orders[:, None]).astype(F32)
    smem = pl.BlockSpec(memory_space=pltpu.SMEM)
    vmem = pl.BlockSpec(memory_space=pltpu.VMEM)
    return pl.pallas_call(
        legendre_kernel,
        out_shape=jax.ShapeDtypeStruct((ORDERS, LATS * PAD, DEVICES * SLOT), BF16),
        in_specs=[smem] * 5 + [vmem] * 3,
        out_specs=vmem,
        scratch_shapes=[pltpu.VMEM((ORDERS, 8 * BLOCK, 128), F32)],
        compiler_params=limit(16),
        name="legendre",
    )(up.reshape(-1), back.reshape(-1), start.reshape(-1), seed, order, x, root, log_sine)


def forward_kernel(table, x_ref, out_ref, buf, held, ready):
    g = pl.program_id(0)
    arrive = stream(table, held, ready, 2)
    arrive()
    rows = LONS * Q

    for parity in range(2):

        @pl.when(g == parity)
        def _():
            for pair in range(SLOT // 2):
                both = []
                for half in range(2):
                    low = x_ref[:HALF, 2 * pair + half]
                    high = x_ref[HALF:, 2 * pair + half]
                    both.append((low - high if parity else low + high).reshape(HALF * PAD, C))
                done = jnp.dot(
                    held[parity], jnp.concatenate(both, axis=1), preferred_element_type=F32
                )
                for half in range(2):
                    for lat in range(LATS // 2):
                        first = lat * rows * SLOT + 2 * pair + half
                        buf[pl.ds(first, rows, stride=SLOT), :] = done[
                            lat * rows : lat * rows + rows, half * C : half * C + C
                        ]

    for lat in range(LATS // 2):
        first = lat * rows * SLOT
        out_ref[lat, 0] = buf[first : first + rows * SLOT, :].astype(BF16)


def fourier_forward(table, x):
    shape = (LATS // 2, 2, LONS * CHUNK, C)
    return pl.pallas_call(
        forward_kernel,
        grid=(2,),
        out_shape=pltpu.HBM(shape, BF16),
        in_specs=[whole(pltpu.HBM), whole()],
        out_specs=pl.BlockSpec((shape[0], 1) + shape[2:], lambda g: (0, g, 0, 0)),
        scratch_shapes=[pltpu.VMEM((M * SLOT, C), F32)] + streamed(table),
        compiler_params=limit(24),
        name="fourier_forward",
    )(far(table), near(x))


def analyse_kernel(table, x_ref, out_ref, wide, held, ready):
    g = pl.program_id(0)
    arrive = stream(table, held, ready, ORDERS)

    @pl.when(g == 0)
    def _():
        wide[...] = x_ref[...].astype(F32)

    def column(q):
        parts = [wide[pl.ds(q * SLOT + tt, DEVICES, stride=CHUNK), :] for tt in range(SLOT)]
        return jnp.concatenate(parts, axis=0).astype(BF16)

    right = jnp.concatenate([column(2 * g), column(2 * g + 1)], axis=1)
    arrive()
    done = jnp.dot(held[g], right, preferred_element_type=F32).astype(BF16)
    for half in range(2):
        out_ref[:, half] = done[:, half * C : half * C + C].reshape(LATS, PAD, C)


def analyse(table, x):
    return pl.pallas_call(
        analyse_kernel,
        grid=(ORDERS,),
        out_shape=pltpu.HBM((LATS, Q, PAD, C), BF16),
        in_specs=[whole(pltpu.HBM), whole()],
        out_specs=pl.BlockSpec((LATS, 2, PAD, C), lambda g: (0, g, 0, 0)),
        scratch_shapes=[pltpu.VMEM((DEVICES * CHUNK, C), F32)] + streamed(table),
        compiler_params=limit(26),
        name="analyse",
    )(far(table), near(x))


def mix_kernel(x_ref, weights, gathered, out_ref, wide, made, held, ready):
    g = pl.program_id(0)
    steps, each = held.shape[:2]
    slabs = LATS * Q
    arrive = stream(weights, held, ready, steps)

    @pl.when(g == 0)
    def _():
        for slab in range(slabs):
            wide[slab * ODD : slab * ODD + PAD, :] = x_ref[
                slab * PAD : slab * PAD + PAD, :
            ].astype(F32)
            made[slab * ODD + PAD - 8 : slab * ODD + PAD, :] = jnp.zeros((8, C), F32)

    arrive()

    @pl.when(g < steps)
    def _():
        for offset in range(each):
            rows = pl.ds(g * each + offset, slabs, stride=ODD)
            part = wide[rows, :].astype(BF16)
            gathered[offset] = part
            made[rows, :] = lax.dot_general(
                part, held[g, offset], (((1,), (1,)), ((), ())), preferred_element_type=F32
            )

    for step in range(TAIL):

        @pl.when(g == steps + step)
        def _():
            for slab in range(slabs // TAIL):
                first = (step * (slabs // TAIL) + slab) * ODD
                out_ref[slab * PAD : slab * PAD + PAD, :] = made[first : first + PAD, :].astype(
                    BF16
                )


def mix(x, weights):
    steps = 5
    each = DEGREES // steps
    size = LATS * Q * PAD
    weights = weights.reshape(steps, each, C, C)
    return pl.pallas_call(
        mix_kernel,
        grid=(steps + TAIL,),
        out_shape=(
            pltpu.HBM((DEGREES, LATS * Q, C), BF16),
            pltpu.HBM((size, C), BF16),
        ),
        in_specs=[whole(), whole(pltpu.HBM)],
        out_specs=(
            pl.BlockSpec((each, LATS * Q, C), lambda g: (jnp.minimum(g, steps - 1), 0, 0)),
            pl.BlockSpec((size // TAIL, C), lambda g: (jnp.maximum(g - steps, 0), 0)),
        ),
        scratch_shapes=[pltpu.VMEM((LATS * Q * ODD, C), F32)] * 2 + streamed(weights),
        compiler_params=limit(26),
        name="mix",
    )(near(x), far(weights))


def synthesise_kernel(table, x_ref, out_ref, made, held, ready):
    g = pl.program_id(0)
    arrive = stream(table, held, ready, ORDERS)
    arrive()

    @pl.when(g < ORDERS)
    def _():
        right = jnp.concatenate(
            [x_ref[:, 2 * g + half].reshape(LATS * PAD, C) for half in range(2)], axis=1
        )
        done = jnp.dot(held[g], right, preferred_element_type=F32)
        for half in range(2):
            for tt in range(SLOT):
                made[pl.ds((2 * g + half) * SLOT + tt, DEVICES, stride=CHUNK), :] = done[
                    tt * DEVICES : tt * DEVICES + DEVICES, half * C : half * C + C
                ]

    rows = out_ref.shape[0]
    for step in range(TAIL):

        @pl.when(g == ORDERS + step)
        def _():
            out_ref[...] = made[step * rows : step * rows + rows, :].astype(BF16)


def synthesise(table, x):
    return pl.pallas_call(
        synthesise_kernel,
        grid=(ORDERS + TAIL,),
        out_shape=pltpu.HBM((DEVICES * CHUNK, C), BF16),
        in_specs=[whole(pltpu.HBM), whole()],
        out_specs=pl.BlockSpec(
            (DEVICES * CHUNK // TAIL, C), lambda g: (jnp.maximum(g - ORDERS, 0), 0)
        ),
        scratch_shapes=[pltpu.VMEM((DEVICES * CHUNK, C), F32)] + streamed(table),
        compiler_params=limit(26),
        name="synthesise",
    )(far(table), near(x))


def backward_kernel(table, x_ref, out_ref, wide, right, held, ready):
    g = pl.program_id(0)
    arrive = stream(table, held, ready, held.shape[0])
    rows = LONS * Q

    @pl.when(g == 0)
    def _():
        wide[...] = x_ref[...].astype(F32)
        for tt in range(SLOT):
            part = wide[pl.ds(tt, 2 * M, stride=SLOT), :].astype(BF16)
            for lat in range(LATS):
                first = lat // 2 * rows
                right[lat % 2, first : first + rows, tt * C : tt * C + C] = part[
                    lat * rows : lat * rows + rows
                ]

    arrive()
    for pair in range(SLOT // 2):
        lanes = slice(2 * pair * C, 2 * pair * C + 2 * C)
        even = jnp.dot(held[g, :, :M], right[0, :, lanes], preferred_element_type=F32)
        odd = jnp.dot(held[g, :, M:], right[1, :, lanes], preferred_element_type=F32)
        for side, done in enumerate((even + odd, even - odd)):
            done = done.astype(BF16)
            for half in range(2):
                for j in range(out_ref.shape[1]):
                    out_ref[side, j, 2 * pair + half] = done[
                        j * PAD : j * PAD + PAD, half * C : half * C + C
                    ]


def fourier_backward(table, x):
    steps = 2
    each = HALF // steps
    table = table.reshape(steps, each * PAD, 2 * M)
    return pl.pallas_call(
        backward_kernel,
        grid=(steps,),
        out_shape=pltpu.HBM((2, HALF, SLOT, PAD, C), BF16),
        in_specs=[whole(pltpu.HBM), whole()],
        out_specs=pl.BlockSpec((2, each, SLOT, PAD, C), lambda g: (0, g, 0, 0, 0)),
        scratch_shapes=[
            pltpu.VMEM((DEVICES * CHUNK, C), F32),
            pltpu.VMEM((2, M, SLOT * C), BF16),
        ]
        + streamed(table),
        compiler_params=limit(26),
        name="fourier_backward",
    )(far(table), near(x))


def exchange(x, axis):
    return lax.all_to_all(x, axis, split_axis=0, concat_axis=0, tiled=True)


def share_cores(held):
    core = lax.axis_index("lon") & 1
    held = held.reshape(DEGREES, LONS // 2, 2, C // LONS, C)
    keep = lax.dynamic_index_in_dim(held, core, 2, keepdims=False)
    give = lax.dynamic_index_in_dim(held, 1 - core, 2, keepdims=False)
    got = lax.ppermute(give, "lon", [(k, k ^ 1) for k in range(LONS)])
    return (keep.astype(F32) + got.astype(F32)).astype(BF16)


def share_columns(held):
    z = lax.axis_index("lon") >> 2
    held = held.reshape(DEGREES, 4, 2, C // LONS, C)
    got = []
    for step in (1, 3, 2):
        give = lax.dynamic_index_in_dim(held, (z + step) % 4, 1, keepdims=False)
        pairs = [(k, (k + 4 * step) % LONS) for k in range(LONS)]
        got.append(lax.ppermute(give, "lon", pairs))
    return lax.dynamic_index_in_dim(held, z, 1, keepdims=False), got


def share_pair(held):
    y = (lax.axis_index("lon") >> 1) & 1
    keep = lax.dynamic_index_in_dim(held, y, 1, keepdims=False)
    give = lax.dynamic_index_in_dim(held, 1 - y, 1, keepdims=False).astype(BF16)
    return keep + lax.ppermute(give, "lon", [(k, k ^ 2) for k in range(LONS)]).astype(F32)


def cells(x):
    return x.reshape(DEVICES, CHUNK // 2, 2, C)


def on_device(grad_out, spectrum, weights):
    both = ("lat", "lon")
    rows = jnp.swapaxes(grad_out[0], 1, 2)
    rows = jnp.pad(rows, ((0, LONS * SLOT - ROWS), (0, PAD - COLS), (0, 0)))
    rows = exchange(rows.reshape(LONS, SLOT, PAD, C), "lon")
    forward, backward = fourier_tables()
    legendre = legendre_table()
    rows, forward, legendre = lax.optimization_barrier((rows, forward, legendre))

    spectra = fourier_forward(forward, rows)
    columns = exchange(cells(spectra), both).reshape(DEVICES * CHUNK, C)
    turned = jnp.swapaxes(legendre, 1, 2)
    stored = spectrum.reshape(ORDERS, LATS, DEGREES, 2, C).transpose(2, 1, 0, 3, 4)
    stored = stored.reshape(DEGREES, LATS * Q, C)
    columns, turned, stored = lax.optimization_barrier((columns, turned, stored))

    analysed = exchange(analyse(legendre, columns), "lat").reshape(LATS * Q * PAD, C)
    analysed, backward = lax.optimization_barrier((analysed, backward))
    gathered, spec_local = mix(analysed, weights)
    spec_grad = exchange(spec_local.reshape(LATS, Q, PAD, C), "lat")

    held = jnp.einsum("lrc,lrd->lcd", stored, gathered, preferred_element_type=F32)
    held = held.astype(BF16)
    held = share_cores(held)
    held, got = share_columns(held)
    spec_grad, held = lax.optimization_barrier((spec_grad, held))

    row_block = synthesise(turned, spec_grad)
    row_block = exchange(cells(row_block), both)
    held = held.astype(F32)
    for part in got:
        held = held + part.astype(F32)
    row_block, held = lax.optimization_barrier((row_block, held))
    grid_part = fourier_backward(backward, row_block.reshape(DEVICES * CHUNK, C))
    grid_part = exchange(grid_part.reshape(LONS, SLOT, PAD, C), "lon")
    weight_grad = share_pair(held)
    grad_in = grid_part[:USED].reshape(ROWS, PAD, C)[:, :COLS]
    return jnp.swapaxes(grad_in, 1, 2)[None], weight_grad


def solution(mesh):
    in_specs = (
        P(None, "lat", None, "lon"),
        P("lon", "lat", None, None, None),
        P("lat", None, None),
    )
    out_specs = (P(None, "lat", None, "lon"), P("lat", "lon", None))
    return jax.shard_map(
        on_device, mesh=mesh, in_specs=in_specs, out_specs=out_specs, check_vma=False
    )
```

```python
import math

import jax
import jax.numpy as jnp
import numpy as np
from jax import lax
from jax.experimental import pallas as pl
from jax.experimental.pallas import tpu as pltpu
from jax.sharding import PartitionSpec as P

LAT = 720
LON = 1440
L = 720
M = 640
C = 128
LATS = 8
LONS = 16
DEVICES = LATS * LONS
ROWS = LAT // LATS
COLS = LON // LONS
SLOT = 6
USED = ROWS // SLOT
PAD = 96
ODD = PAD + 1
ORDERS = M // (LATS * LONS)
HALF = LONS // 2
Q = 2 * ORDERS
CHUNK = Q * SLOT
DEGREES = L // LATS
BLOCK = 16
TAIL = 2
SHIFT = 40

F32 = jnp.float32
BF16 = jnp.bfloat16


def limit(mebibytes):
    return pltpu.CompilerParams(vmem_limit_bytes=mebibytes << 20)


def near(x):
    return pltpu.with_memory_space_constraint(x, pltpu.VMEM)


def far(x):
    return pltpu.with_memory_space_constraint(x, pltpu.HBM)


def whole(space=pltpu.VMEM):
    return pl.BlockSpec(memory_space=space)


def stream(table, held, ready, steps):
    g = pl.program_id(0)

    def copy(step):
        return pltpu.make_async_copy(table.at[step], held.at[step], ready.at[step])

    @pl.when(g == 0)
    def _():
        for step in range(steps):
            copy(step).start()

    def arrive():
        @pl.when(g < steps)
        def _():
            copy(jnp.minimum(g, steps - 1)).wait()

    return arrive


def streamed(table):
    return [pltpu.VMEM(table.shape, table.dtype), pltpu.SemaphoreType.DMA((table.shape[0],))]


def cosine_values(position, order, part):
    step = position * order + part * (LON // 4)
    turn = step - LON * jnp.floor(step * (1.0 / LON))
    fold = (LON // 4) - jnp.abs(turn - LON // 2)
    angle = fold * (2.0 * math.pi / LON)
    square = angle * angle
    series = -1.0 / 39916800.0
    for term in (1.0 / 362880.0, -1.0 / 5040.0, 1.0 / 120.0, -1.0 / 6.0, 1.0):
        series = series * square + term
    return -(angle * series) * (1.0 / math.sqrt(LON))


def fourier_tables():
    def line(shape, axis):
        at = lax.broadcasted_iota(jnp.int32, shape, axis)
        inner = at % PAD
        return (at // PAD * COLS + inner).astype(F32), (inner < COLS).astype(F32)

    def modes(shape, axis):
        at = lax.broadcasted_iota(jnp.int32, shape, axis)
        device, kind = at // Q, at % Q
        parity, device = device // (DEVICES // 2), device % (DEVICES // 2)
        lat = device // LONS * 2 + parity
        order = device % LONS * (LATS * ORDERS) + kind // 2 * LATS + lat
        return order.astype(F32), (kind % 2).astype(F32)

    wide = HALF * PAD
    position, live = line((1, wide), 1)
    order, part = modes((2 * M, 1), 0)
    forward = (cosine_values(position, order, part) * live).astype(BF16)
    position, live = line((wide, 1), 0)
    order, part = modes((1, 2 * M), 1)
    backward = (cosine_values(position, order, part) * live).astype(BF16)
    return forward.reshape(2, M, wide), backward


def seed_constants():
    out = []
    for m in range(M):
        out.append(
            0.5 * math.log(m + 0.5)
            + 0.5 * math.lgamma(2.0 * m + 1.0)
            - math.lgamma(m + 1.0)
            - m * math.log(2.0)
        )
    return np.asarray(out, np.float32)


def legendre_kernel(up, back, start, seed, order, x_ref, root_ref, sine_ref, out, buf):
    x = x_ref[...]
    root = root_ref[...]
    base = [seed[k] + order[k] * sine_ref[...] for k in range(ORDERS)]
    zero = jnp.zeros_like(x)
    small = 2.0**-SHIFT
    unit = SHIFT * math.log(2.0)

    def block(first, row, steps, carry):
        current, previous, count = (list(part) for part in carry)
        factor = [None] * ORDERS
        for offset in range(steps):
            if offset % 8 == 0:
                for k in range(ORDERS):
                    big = jnp.maximum(jnp.abs(current[k]), jnp.abs(previous[k])) > 1.0
                    scale = jnp.where(big, small, 1.0)
                    current[k] = current[k] * scale
                    previous[k] = previous[k] * scale
                    count[k] = count[k] + jnp.where(big, 1.0, 0.0)
                    factor[k] = jnp.exp(base[k] + unit * count[k]) * root
            for k in range(ORDERS):
                at = k * L + first + offset
                advanced = (up[at] * x) * current[k] - back[at] * previous[k] + start[at]
                previous[k] = current[k]
                current[k] = advanced
                buf[k, offset * 8 : offset * 8 + 8, :] = advanced * factor[k]
        for k in range(ORDERS):
            for offset in range(steps, BLOCK):
                buf[k, offset * 8 : offset * 8 + 8, :] = zero
            for tt in range(SLOT):
                low = buf[k, pl.ds(tt, 8, stride=8), :]
                high = buf[k, pl.ds(64 + tt, 8, stride=8), :]
                both = jnp.concatenate([low, high], axis=0).astype(BF16)
                out[k, pl.ds(pl.multiple_of(row, BLOCK), BLOCK), tt * 128 : tt * 128 + 128] = both
        return tuple(current), tuple(previous), tuple(count)

    def band(k, carry):
        first, row = k * DEGREES, k * PAD
        whole = DEGREES // BLOCK

        def inner(step, carry):
            return block(first + step * BLOCK, row + step * BLOCK, BLOCK, carry)

        carry = lax.fori_loop(0, whole, inner, carry)
        done = whole * BLOCK
        return block(first + done, row + done, DEGREES - done, carry)

    none = (zero,) * ORDERS
    lax.fori_loop(0, LATS, band, (none, none, none))


def legendre_table():
    lon, lat = lax.axis_index("lon"), lax.axis_index("lat")
    orders = (lon * ORDERS + jnp.arange(ORDERS, dtype=jnp.int32)) * LATS + lat
    order = orders.astype(F32)
    seeds = jnp.asarray(seed_constants().reshape(LONS, ORDERS, LATS))
    seed = lax.dynamic_slice(seeds, (lon, 0, lat), (1, ORDERS, 1)).reshape(ORDERS)
    slot = jnp.arange(1024, dtype=jnp.int32)
    tt, device = slot // DEVICES, slot % DEVICES
    lat, lon = device // LONS, device % LONS
    live = (tt < SLOT) & (lon < USED)
    row = jnp.where(live, ROWS * lat + SLOT * lon + tt, 0)
    angle = (row.astype(F32) + 0.5) * (math.pi / LAT)
    sine = jnp.sin(angle)
    x = jnp.where(live, jnp.cos(angle), 0.0).reshape(8, 128)
    root = jnp.where(live, jnp.sqrt(sine * (math.pi / LAT)), 0.0).reshape(8, 128)
    log_sine = jnp.log(sine).reshape(8, 128)
    degree = jnp.arange(L, dtype=jnp.int32)[None, :]
    past = degree > orders[:, None]
    val, ord_val = degree.astype(F32), order[:, None]
    divisor = jnp.where(past, val * val - ord_val * ord_val, 1.0)
    up = jnp.where(past, jnp.sqrt(jnp.maximum((4.0 * val * val - 1.0) / divisor, 0.0)), 0.0)
    lower = (val - 1.0) * (val - 1.0) - ord_val * ord_val
    back = jnp.sqrt(
        jnp.maximum(lower * (2.0 * val + 1.0) / ((2.0 * val - 3.0) * divisor), 0.0)
    )
    back = jnp.where(past, back, 0.0)
    start = (degree == orders[:, None]).astype(F32)
    smem = pl.BlockSpec(memory_space=pltpu.SMEM)
    vmem = pl.BlockSpec(memory_space=pltpu.VMEM)
    return pl.pallas_call(
        legendre_kernel,
        out_shape=jax.ShapeDtypeStruct((ORDERS, LATS * PAD, DEVICES * SLOT), BF16),
        in_specs=[smem] * 5 + [vmem] * 3,
        out_specs=vmem,
        scratch_shapes=[pltpu.VMEM((ORDERS, 8 * BLOCK, 128), F32)],
        compiler_params=limit(16),
        name="legendre",
    )(up.reshape(-1), back.reshape(-1), start.reshape(-1), seed, order, x, root, log_sine)


def forward_kernel(table, x_ref, out_ref, buf, held, ready):
    g = pl.program_id(0)
    arrive = stream(table, held, ready, 2)
    arrive()
    rows = LONS * Q

    for parity in range(2):

        @pl.when(g == parity)
        def _():
            for pair in range(SLOT // 2):
                both = []
                for half in range(2):
                    low = x_ref[:HALF, 2 * pair + half]
                    high = x_ref[HALF:, 2 * pair + half]
                    both.append((low - high if parity else low + high).reshape(HALF * PAD, C))
                done = jnp.dot(
                    held[parity], jnp.concatenate(both, axis=1), preferred_element_type=F32
                )
                for half in range(2):
                    for lat in range(LATS // 2):
                        first = lat * rows * SLOT + 2 * pair + half
                        buf[pl.ds(first, rows, stride=SLOT), :] = done[
                            lat * rows : lat * rows + rows, half * C : half * C + C
                        ]

    for lat in range(LATS // 2):
        first = lat * rows * SLOT
        out_ref[lat, 0] = buf[first : first + rows * SLOT, :].astype(BF16)


def fourier_forward(table, x):
    shape = (LATS // 2, 2, LONS * CHUNK, C)
    return pl.pallas_call(
        forward_kernel,
        grid=(2,),
        out_shape=pltpu.HBM(shape, BF16),
        in_specs=[whole(pltpu.HBM), whole()],
        out_specs=pl.BlockSpec((shape[0], 1) + shape[2:], lambda g: (0, g, 0, 0)),
        scratch_shapes=[pltpu.VMEM((M * SLOT, C), F32)] + streamed(table),
        compiler_params=limit(24),
        name="fourier_forward",
    )(far(table), near(x))


def analyse_kernel(table, x_ref, out_ref, wide, held, ready):
    g = pl.program_id(0)
    arrive = stream(table, held, ready, ORDERS)

    @pl.when(g == 0)
    def _():
        wide[...] = x_ref[...].astype(F32)

    def column(q):
        parts = [wide[pl.ds(q * SLOT + tt, DEVICES, stride=CHUNK), :] for tt in range(SLOT)]
        return jnp.concatenate(parts, axis=0).astype(BF16)

    right = jnp.concatenate([column(2 * g), column(2 * g + 1)], axis=1)
    arrive()
    done = jnp.dot(held[g], right, preferred_element_type=F32).astype(BF16)
    for half in range(2):
        out_ref[:, half] = done[:, half * C : half * C + C].reshape(LATS, PAD, C)


def analyse(table, x):
    return pl.pallas_call(
        analyse_kernel,
        grid=(ORDERS,),
        out_shape=pltpu.HBM((LATS, Q, PAD, C), BF16),
        in_specs=[whole(pltpu.HBM), whole()],
        out_specs=pl.BlockSpec((LATS, 2, PAD, C), lambda g: (0, g, 0, 0)),
        scratch_shapes=[pltpu.VMEM((DEVICES * CHUNK, C), F32)] + streamed(table),
        compiler_params=limit(26),
        name="analyse",
    )(far(table), near(x))


def mix_kernel(x_ref, weights, gathered, out_ref, wide, made, held, ready):
    g = pl.program_id(0)
    steps, each = held.shape[:2]
    slabs = LATS * Q
    arrive = stream(weights, held, ready, steps)

    @pl.when(g == 0)
    def _():
        for slab in range(slabs):
            wide[slab * ODD : slab * ODD + PAD, :] = x_ref[
                slab * PAD : slab * PAD + PAD, :
            ].astype(F32)
            made[slab * ODD + PAD - 8 : slab * ODD + PAD, :] = jnp.zeros((8, C), F32)

    arrive()

    @pl.when(g < steps)
    def _():
        for offset in range(each):
            rows = pl.ds(g * each + offset, slabs, stride=ODD)
            part = wide[rows, :].astype(BF16)
            gathered[offset] = part
            made[rows, :] = lax.dot_general(
                part, held[g, offset], (((1,), (1,)), ((), ())), preferred_element_type=F32
            )

    for step in range(TAIL):

        @pl.when(g == steps + step)
        def _():
            for slab in range(slabs // TAIL):
                first = (step * (slabs // TAIL) + slab) * ODD
                out_ref[slab * PAD : slab * PAD + PAD, :] = made[first : first + PAD, :].astype(
                    BF16
                )


def mix(x, weights):
    steps = 5
    each = DEGREES // steps
    size = LATS * Q * PAD
    weights = weights.reshape(steps, each, C, C)
    return pl.pallas_call(
        mix_kernel,
        grid=(steps + TAIL,),
        out_shape=(
            pltpu.HBM((DEGREES, LATS * Q, C), BF16),
            pltpu.HBM((size, C), BF16),
        ),
        in_specs=[whole(), whole(pltpu.HBM)],
        out_specs=(
            pl.BlockSpec((each, LATS * Q, C), lambda g: (jnp.minimum(g, steps - 1), 0, 0)),
            pl.BlockSpec((size // TAIL, C), lambda g: (jnp.maximum(g - steps, 0), 0)),
        ),
        scratch_shapes=[pltpu.VMEM((LATS * Q * ODD, C), F32)] * 2 + streamed(weights),
        compiler_params=limit(26),
        name="mix",
    )(near(x), far(weights))


def weigh_kernel(place, stored, gathered, keep, give):
    core, z = place[0], place[1]
    share = C // LONS
    for offset in range(stored.shape[0]):
        part = lax.dot_general(
            stored[offset], gathered[offset], (((0,), (0,)), ((), ())), preferred_element_type=F32
        )
        for column in range(4):
            to = lax.rem(column + 4 - z, 4)
            piece = part[column * 4 * share : column * 4 * share + 4 * share]
            here = jnp.concatenate([piece[:share], piece[2 * share : 3 * share]], axis=0)
            there = jnp.concatenate([piece[share : 2 * share], piece[3 * share :]], axis=0)
            keep[to, offset] = jnp.where(core == 0, here, there).astype(BF16)
            give[to, offset] = jnp.where(core == 0, there, here).astype(BF16)


def weigh(stored, gathered):
    steps = 5
    each = DEGREES // steps
    lon = lax.axis_index("lon")
    shape = (4, DEGREES, C // 8, C)
    rows = pl.BlockSpec((each, LATS * Q, C), lambda g: (g, 0, 0))
    sums = pl.BlockSpec((4, each, C // 8, C), lambda g: (0, g, 0, 0))
    return pl.pallas_call(
        weigh_kernel,
        grid=(steps,),
        out_shape=(pltpu.HBM(shape, BF16), pltpu.HBM(shape, BF16)),
        in_specs=[pl.BlockSpec(memory_space=pltpu.SMEM), rows, rows],
        out_specs=(sums, sums),
        compiler_params=limit(20),
        name="weigh",
    )(jnp.stack([lon & 1, lon >> 2]), far(stored), far(gathered))


def synthesise_kernel(table, x_ref, out_ref, made, held, ready):
    g = pl.program_id(0)
    arrive = stream(table, held, ready, ORDERS)
    arrive()

    @pl.when(g < ORDERS)
    def _():
        right = jnp.concatenate(
            [x_ref[:, 2 * g + half].reshape(LATS * PAD, C) for half in range(2)], axis=1
        )
        done = jnp.dot(held[g], right, preferred_element_type=F32)
        for half in range(2):
            for tt in range(SLOT):
                made[pl.ds((2 * g + half) * SLOT + tt, DEVICES, stride=CHUNK), :] = done[
                    tt * DEVICES : tt * DEVICES + DEVICES, half * C : half * C + C
                ]

    rows = out_ref.shape[0]
    for step in range(TAIL):

        @pl.when(g == ORDERS + step)
        def _():
            out_ref[...] = made[step * rows : step * rows + rows, :].astype(BF16)


def synthesise(table, x):
    return pl.pallas_call(
        synthesise_kernel,
        grid=(ORDERS + TAIL,),
        out_shape=pltpu.HBM((DEVICES * CHUNK, C), BF16),
        in_specs=[whole(pltpu.HBM), whole()],
        out_specs=pl.BlockSpec(
            (DEVICES * CHUNK // TAIL, C), lambda g: (jnp.maximum(g - ORDERS, 0), 0)
        ),
        scratch_shapes=[pltpu.VMEM((DEVICES * CHUNK, C), F32)] + streamed(table),
        compiler_params=limit(26),
        name="synthesise",
    )(far(table), near(x))


def backward_kernel(table, x_ref, out_ref, wide, right, held, ready):
    g = pl.program_id(0)
    arrive = stream(table, held, ready, held.shape[0])
    rows = LONS * Q

    @pl.when(g == 0)
    def _():
        wide[...] = x_ref[...].astype(F32)
        for tt in range(SLOT):
            part = wide[pl.ds(tt, 2 * M, stride=SLOT), :].astype(BF16)
            for lat in range(LATS):
                first = lat // 2 * rows
                right[lat % 2, first : first + rows, tt * C : tt * C + C] = part[
                    lat * rows : lat * rows + rows
                ]

    arrive()
    for pair in range(SLOT // 2):
        lanes = slice(2 * pair * C, 2 * pair * C + 2 * C)
        even = jnp.dot(held[g, :, :M], right[0, :, lanes], preferred_element_type=F32)
        odd = jnp.dot(held[g, :, M:], right[1, :, lanes], preferred_element_type=F32)
        for side, done in enumerate((even + odd, even - odd)):
            done = done.astype(BF16)
            for half in range(2):
                for j in range(out_ref.shape[1]):
                    out_ref[side, j, 2 * pair + half] = done[
                        j * PAD : j * PAD + PAD, half * C : half * C + C
                    ]


def fourier_backward(table, x):
    steps = 2
    each = HALF // steps
    table = table.reshape(steps, each * PAD, 2 * M)
    return pl.pallas_call(
        backward_kernel,
        grid=(steps,),
        out_shape=pltpu.HBM((2, HALF, SLOT, PAD, C), BF16),
        in_specs=[whole(pltpu.HBM), whole()],
        out_specs=pl.BlockSpec((2, each, SLOT, PAD, C), lambda g: (0, g, 0, 0, 0)),
        scratch_shapes=[
            pltpu.VMEM((DEVICES * CHUNK, C), F32),
            pltpu.VMEM((2, M, SLOT * C), BF16),
        ]
        + streamed(table),
        compiler_params=limit(26),
        name="fourier_backward",
    )(far(table), near(x))


def exchange(x, axis):
    return lax.all_to_all(x, axis, split_axis=0, concat_axis=0, tiled=True)


def share_pair(held):
    y = (lax.axis_index("lon") >> 1) & 1
    keep = lax.dynamic_index_in_dim(held, y, 1, keepdims=False)
    give = lax.dynamic_index_in_dim(held, 1 - y, 1, keepdims=False).astype(BF16)
    return keep + lax.ppermute(give, "lon", [(k, k ^ 2) for k in range(LONS)]).astype(F32)


def cells(x):
    return x.reshape(DEVICES, CHUNK // 2, 2, C)


def on_device(grad_out, spectrum, weights):
    both = ("lat", "lon")
    rows = jnp.swapaxes(grad_out[0], 1, 2)
    rows = jnp.pad(rows, ((0, LONS * SLOT - ROWS), (0, PAD - COLS), (0, 0)))
    rows = exchange(rows.reshape(LONS, SLOT, PAD, C), "lon")
    forward, backward = fourier_tables()
    legendre = legendre_table()
    rows, forward, legendre = lax.optimization_barrier((rows, forward, legendre))

    spectra = fourier_forward(forward, rows)
    columns = exchange(cells(spectra), both).reshape(DEVICES * CHUNK, C)
    turned = jnp.swapaxes(legendre, 1, 2)
    stored = spectrum.reshape(ORDERS, LATS, DEGREES, 2, C).transpose(2, 1, 0, 3, 4)
    stored = stored.reshape(DEGREES, LATS * Q, C)
    columns, turned, stored = lax.optimization_barrier((columns, turned, stored))

    analysed = exchange(analyse(legendre, columns), "lat").reshape(LATS * Q * PAD, C)
    analysed, backward = lax.optimization_barrier((analysed, backward))
    gathered, spec_local = mix(analysed, weights)
    spec_grad = exchange(spec_local.reshape(LATS, Q, PAD, C), "lat")

    keep, give = weigh(stored, gathered)
    got = lax.ppermute(give, "lon", [(k, k ^ 1) for k in range(LONS)])
    sums = [keep[step].astype(F32) + got[step].astype(F32) for step in range(4)]
    held, got = sums[0], []
    for step in (1, 3, 2):
        pairs = [(k, (k + 4 * step) % LONS) for k in range(LONS)]
        got.append(lax.ppermute(sums[step].astype(BF16), "lon", pairs))
    spec_grad, held = lax.optimization_barrier((spec_grad, held))

    row_block = synthesise(turned, spec_grad)
    row_block = exchange(cells(row_block), both)
    for part in got:
        held = held + part.astype(F32)
    held = held.reshape(DEGREES, 2, C // LONS, C)
    row_block, held = lax.optimization_barrier((row_block, held))
    grid_part = fourier_backward(backward, row_block.reshape(DEVICES * CHUNK, C))
    grid_part = exchange(grid_part.reshape(LONS, SLOT, PAD, C), "lon")
    weight_grad = share_pair(held)
    grad_in = grid_part[:USED].reshape(ROWS, PAD, C)[:, :COLS]
    return jnp.swapaxes(grad_in, 1, 2)[None], weight_grad


def solution(mesh):
    in_specs = (
        P(None, "lat", None, "lon"),
        P("lon", "lat", None, None, None),
        P("lat", None, None),
    )
    out_specs = (P(None, "lat", None, "lon"), P("lat", "lon", None))
    return jax.shard_map(
        on_device, mesh=mesh, in_specs=in_specs, out_specs=out_specs, check_vma=False
    )
```

```python
import math

import jax
import jax.numpy as jnp
import numpy as np
from jax import lax
from jax.experimental import pallas as pl
from jax.experimental.pallas import tpu as pltpu
from jax.sharding import PartitionSpec as P

LAT = 720
LON = 1440
L = 720
M = 640
C = 128
LATS = 8
LONS = 16
DEVICES = LATS * LONS
ROWS = LAT // LATS
COLS = LON // LONS
SLOT = 6
USED = ROWS // SLOT
PAD = 96
ODD = PAD + 1
ORDERS = M // (LATS * LONS)
HALF = LONS // 2
Q = 2 * ORDERS
CHUNK = Q * SLOT
DEGREES = L // LATS
BLOCK = 16
AHEAD = 2
TAIL = 4
SHIFT = 40

F32 = jnp.float32
BF16 = jnp.bfloat16


def limit(mebibytes):
    return pltpu.CompilerParams(vmem_limit_bytes=mebibytes << 20)


def near(x):
    return pltpu.with_memory_space_constraint(x, pltpu.VMEM)


def far(x):
    return pltpu.with_memory_space_constraint(x, pltpu.HBM)


def whole(space=pltpu.VMEM):
    return pl.BlockSpec(memory_space=space)


def stream(table, held, ready, steps):
    g = pl.program_id(0)

    def copy(step):
        return pltpu.make_async_copy(table.at[step], held.at[step], ready.at[step])

    @pl.when(g == 0)
    def _():
        for step in range(min(AHEAD, steps)):
            copy(step).start()

    def arrive():
        @pl.when(g < steps)
        def _():
            copy(jnp.minimum(g, steps - 1)).wait()

        @pl.when(g + AHEAD < steps)
        def _():
            copy(jnp.minimum(g + AHEAD, steps - 1)).start()

    return arrive


def streamed(table):
    return [pltpu.VMEM(table.shape, table.dtype), pltpu.SemaphoreType.DMA((table.shape[0],))]


def cosine_values(position, order, part):
    step = position * order + part * (LON // 4)
    turn = step - LON * jnp.floor(step * (1.0 / LON))
    fold = (LON // 4) - jnp.abs(turn - LON // 2)
    angle = fold * (2.0 * math.pi / LON)
    square = angle * angle
    series = -1.0 / 39916800.0
    for term in (1.0 / 362880.0, -1.0 / 5040.0, 1.0 / 120.0, -1.0 / 6.0, 1.0):
        series = series * square + term
    return -(angle * series) * (1.0 / math.sqrt(LON))


def fourier_tables():
    def line(shape, axis):
        at = lax.broadcasted_iota(jnp.int32, shape, axis)
        inner = at % PAD
        return (at // PAD * COLS + inner).astype(F32), (inner < COLS).astype(F32)

    def modes(shape, axis):
        at = lax.broadcasted_iota(jnp.int32, shape, axis)
        device, kind = at // Q, at % Q
        parity, device = device // (DEVICES // 2), device % (DEVICES // 2)
        lat = device // LONS * 2 + parity
        order = device % LONS * (LATS * ORDERS) + kind // 2 * LATS + lat
        return order.astype(F32), (kind % 2).astype(F32)

    wide = HALF * PAD
    position, live = line((1, wide), 1)
    order, part = modes((2 * M, 1), 0)
    forward = (cosine_values(position, order, part) * live).astype(BF16)
    position, live = line((wide, 1), 0)
    order, part = modes((1, 2 * M), 1)
    backward = (cosine_values(position, order, part) * live).astype(BF16)
    return forward.reshape(2, M, wide), backward


def seed_constants():
    out = []
    for m in range(M):
        out.append(
            0.5 * math.log(m + 0.5)
            + 0.5 * math.lgamma(2.0 * m + 1.0)
            - math.lgamma(m + 1.0)
            - m * math.log(2.0)
        )
    return np.asarray(out, np.float32)


def legendre_kernel(up, back, start, seed, order, x_ref, root_ref, sine_ref, out, buf):
    x = x_ref[...]
    root = root_ref[...]
    base = [seed[k] + order[k] * sine_ref[...] for k in range(ORDERS)]
    zero = jnp.zeros_like(x)
    small = 2.0**-SHIFT
    unit = SHIFT * math.log(2.0)

    def block(first, row, steps, carry):
        current, previous, count = (list(part) for part in carry)
        factor = [None] * ORDERS
        for offset in range(steps):
            if offset % 8 == 0:
                for k in range(ORDERS):
                    big = jnp.maximum(jnp.abs(current[k]), jnp.abs(previous[k])) > 1.0
                    scale = jnp.where(big, small, 1.0)
                    current[k] = current[k] * scale
                    previous[k] = previous[k] * scale
                    count[k] = count[k] + jnp.where(big, 1.0, 0.0)
                    factor[k] = jnp.exp(base[k] + unit * count[k]) * root
            for k in range(ORDERS):
                at = k * L + first + offset
                advanced = (up[at] * x) * current[k] - back[at] * previous[k] + start[at]
                previous[k] = current[k]
                current[k] = advanced
                buf[k, offset * 8 : offset * 8 + 8, :] = advanced * factor[k]
        for k in range(ORDERS):
            for offset in range(steps, BLOCK):
                buf[k, offset * 8 : offset * 8 + 8, :] = zero
            for tt in range(SLOT):
                low = buf[k, pl.ds(tt, 8, stride=8), :]
                high = buf[k, pl.ds(64 + tt, 8, stride=8), :]
                both = jnp.concatenate([low, high], axis=0).astype(BF16)
                out[k, pl.ds(pl.multiple_of(row, BLOCK), BLOCK), tt * 128 : tt * 128 + 128] = both
        return tuple(current), tuple(previous), tuple(count)

    def band(k, carry):
        first, row = k * DEGREES, k * PAD
        whole = DEGREES // BLOCK

        def inner(step, carry):
            return block(first + step * BLOCK, row + step * BLOCK, BLOCK, carry)

        carry = lax.fori_loop(0, whole, inner, carry)
        done = whole * BLOCK
        return block(first + done, row + done, DEGREES - done, carry)

    none = (zero,) * ORDERS
    lax.fori_loop(0, LATS, band, (none, none, none))


def legendre_table():
    lon, lat = lax.axis_index("lon"), lax.axis_index("lat")
    orders = (lon * ORDERS + jnp.arange(ORDERS, dtype=jnp.int32)) * LATS + lat
    order = orders.astype(F32)
    seeds = jnp.asarray(seed_constants().reshape(LONS, ORDERS, LATS))
    seed = lax.dynamic_slice(seeds, (lon, 0, lat), (1, ORDERS, 1)).reshape(ORDERS)
    slot = jnp.arange(1024, dtype=jnp.int32)
    tt, device = slot // DEVICES, slot % DEVICES
    lat, lon = device // LONS, device % LONS
    live = (tt < SLOT) & (lon < USED)
    row = jnp.where(live, ROWS * lat + SLOT * lon + tt, 0)
    angle = (row.astype(F32) + 0.5) * (math.pi / LAT)
    sine = jnp.sin(angle)
    x = jnp.where(live, jnp.cos(angle), 0.0).reshape(8, 128)
    root = jnp.where(live, jnp.sqrt(sine * (math.pi / LAT)), 0.0).reshape(8, 128)
    log_sine = jnp.log(sine).reshape(8, 128)
    degree = jnp.arange(L, dtype=jnp.int32)[None, :]
    past = degree > orders[:, None]
    val, ord_val = degree.astype(F32), order[:, None]
    divisor = jnp.where(past, val * val - ord_val * ord_val, 1.0)
    up = jnp.where(past, jnp.sqrt(jnp.maximum((4.0 * val * val - 1.0) / divisor, 0.0)), 0.0)
    lower = (val - 1.0) * (val - 1.0) - ord_val * ord_val
    back = jnp.sqrt(
        jnp.maximum(lower * (2.0 * val + 1.0) / ((2.0 * val - 3.0) * divisor), 0.0)
    )
    back = jnp.where(past, back, 0.0)
    start = (degree == orders[:, None]).astype(F32)
    smem = pl.BlockSpec(memory_space=pltpu.SMEM)
    vmem = pl.BlockSpec(memory_space=pltpu.VMEM)
    return pl.pallas_call(
        legendre_kernel,
        out_shape=jax.ShapeDtypeStruct((ORDERS, LATS * PAD, DEVICES * SLOT), BF16),
        in_specs=[smem] * 5 + [vmem] * 3,
        out_specs=vmem,
        scratch_shapes=[pltpu.VMEM((ORDERS, 8 * BLOCK, 128), F32)],
        compiler_params=limit(16),
        name="legendre",
    )(up.reshape(-1), back.reshape(-1), start.reshape(-1), seed, order, x, root, log_sine)


def forward_kernel(table, x_ref, out_ref, buf, held, ready):
    g = pl.program_id(0)
    arrive = stream(table, held, ready, 2)
    arrive()
    rows = LONS * Q

    for parity in range(2):

        @pl.when(g == parity)
        def _():
            for pair in range(SLOT // 2):
                both = []
                for half in range(2):
                    low = x_ref[:HALF, 2 * pair + half]
                    high = x_ref[HALF:, 2 * pair + half]
                    both.append((low - high if parity else low + high).reshape(HALF * PAD, C))
                done = jnp.dot(
                    held[parity], jnp.concatenate(both, axis=1), preferred_element_type=F32
                )
                for half in range(2):
                    for lat in range(LATS // 2):
                        first = lat * rows * SLOT + 2 * pair + half
                        buf[pl.ds(first, rows, stride=SLOT), :] = done[
                            lat * rows : lat * rows + rows, half * C : half * C + C
                        ]

    for lat in range(LATS // 2):
        first = lat * rows * SLOT
        out_ref[lat, 0] = buf[first : first + rows * SLOT, :].astype(BF16)


def fourier_forward(table, x):
    shape = (LATS // 2, 2, LONS * CHUNK, C)
    return pl.pallas_call(
        forward_kernel,
        grid=(2,),
        out_shape=pltpu.HBM(shape, BF16),
        in_specs=[whole(pltpu.HBM), whole()],
        out_specs=pl.BlockSpec((shape[0], 1) + shape[2:], lambda g: (0, g, 0, 0)),
        scratch_shapes=[pltpu.VMEM((M * SLOT, C), F32)] + streamed(table),
        compiler_params=limit(24),
        name="fourier_forward",
    )(far(table), near(x))


def analyse_kernel(table, x_ref, out_ref, wide, held, ready):
    g = pl.program_id(0)
    arrive = stream(table, held, ready, ORDERS)

    @pl.when(g == 0)
    def _():
        wide[...] = x_ref[...].astype(F32)

    def column(q):
        parts = [wide[pl.ds(q * SLOT + tt, DEVICES, stride=CHUNK), :] for tt in range(SLOT)]
        return jnp.concatenate(parts, axis=0).astype(BF16)

    right = jnp.concatenate([column(2 * g), column(2 * g + 1)], axis=1)
    arrive()
    done = jnp.dot(held[g], right, preferred_element_type=F32).astype(BF16)
    for half in range(2):
        out_ref[:, half] = done[:, half * C : half * C + C].reshape(LATS, PAD, C)


def analyse(table, x):
    return pl.pallas_call(
        analyse_kernel,
        grid=(ORDERS,),
        out_shape=pltpu.HBM((LATS, Q, PAD, C), BF16),
        in_specs=[whole(pltpu.HBM), whole()],
        out_specs=pl.BlockSpec((LATS, 2, PAD, C), lambda g: (0, g, 0, 0)),
        scratch_shapes=[pltpu.VMEM((DEVICES * CHUNK, C), F32)] + streamed(table),
        compiler_params=limit(26),
        name="analyse",
    )(far(table), near(x))


def mix_kernel(x_ref, weights, gathered, out_ref, wide, made, held, ready):
    g = pl.program_id(0)
    steps, each = held.shape[:2]
    slabs = LATS * Q
    arrive = stream(weights, held, ready, steps)

    @pl.when(g == 0)
    def _():
        for slab in range(slabs):
            wide[slab * ODD : slab * ODD + PAD, :] = x_ref[
                slab * PAD : slab * PAD + PAD, :
            ].astype(F32)
            made[slab * ODD + PAD - 8 : slab * ODD + PAD, :] = jnp.zeros((8, C), F32)

    arrive()

    @pl.when(g < steps)
    def _():
        for offset in range(each):
            rows = pl.ds(g * each + offset, slabs, stride=ODD)
            part = wide[rows, :].astype(BF16)
            gathered[offset] = part
            made[rows, :] = lax.dot_general(
                part, held[g, offset], (((1,), (1,)), ((), ())), preferred_element_type=F32
            )

    for step in range(TAIL):

        @pl.when(g == steps + step)
        def _():
            for slab in range(slabs // TAIL):
                first = (step * (slabs // TAIL) + slab) * ODD
                out_ref[slab * PAD : slab * PAD + PAD, :] = made[first : first + PAD, :].astype(
                    BF16
                )


def mix(x, weights):
    steps = 5
    each = DEGREES // steps
    size = LATS * Q * PAD
    weights = weights.reshape(steps, each, C, C)
    return pl.pallas_call(
        mix_kernel,
        grid=(steps + TAIL,),
        out_shape=(
            pltpu.HBM((DEGREES, LATS * Q, C), BF16),
            pltpu.HBM((size, C), BF16),
        ),
        in_specs=[whole(), whole(pltpu.HBM)],
        out_specs=(
            pl.BlockSpec((each, LATS * Q, C), lambda g: (jnp.minimum(g, steps - 1), 0, 0)),
            pl.BlockSpec((size // TAIL, C), lambda g: (jnp.maximum(g - steps, 0), 0)),
        ),
        scratch_shapes=[pltpu.VMEM((LATS * Q * ODD, C), F32)] * 2 + streamed(weights),
        compiler_params=limit(26),
        name="mix",
    )(near(x), far(weights))


def weigh_kernel(place, stored, gathered, keep, give):
    core, z = place[0], place[1]
    share = C // LONS
    for offset in range(stored.shape[0]):
        part = lax.dot_general(
            stored[offset], gathered[offset], (((0,), (0,)), ((), ())), preferred_element_type=F32
        )
        for column in range(4):
            to = lax.rem(column + 4 - z, 4)
            piece = part[column * 4 * share : column * 4 * share + 4 * share]
            here = jnp.concatenate([piece[:share], piece[2 * share : 3 * share]], axis=0)
            there = jnp.concatenate([piece[share : 2 * share], piece[3 * share :]], axis=0)
            keep[to, offset] = jnp.where(core == 0, here, there).astype(BF16)
            give[to, offset] = jnp.where(core == 0, there, here).astype(BF16)


def weigh(stored, gathered):
    steps = 5
    each = DEGREES // steps
    lon = lax.axis_index("lon")
    shape = (4, DEGREES, C // 8, C)
    rows = pl.BlockSpec((each, LATS * Q, C), lambda g: (g, 0, 0))
    sums = pl.BlockSpec((4, each, C // 8, C), lambda g: (0, g, 0, 0))
    return pl.pallas_call(
        weigh_kernel,
        grid=(steps,),
        out_shape=(pltpu.HBM(shape, BF16), pltpu.HBM(shape, BF16)),
        in_specs=[pl.BlockSpec(memory_space=pltpu.SMEM), rows, rows],
        out_specs=(sums, sums),
        compiler_params=limit(20),
        name="weigh",
    )(jnp.stack([lon & 1, lon >> 2]), far(stored), far(gathered))


def synthesise_kernel(table, x_ref, out_ref, made, held, ready):
    g = pl.program_id(0)
    arrive = stream(table, held, ready, ORDERS)
    arrive()

    @pl.when(g < ORDERS)
    def _():
        right = jnp.concatenate(
            [x_ref[:, 2 * g + half].reshape(LATS * PAD, C) for half in range(2)], axis=1
        )
        done = jnp.dot(held[g], right, preferred_element_type=F32)
        for half in range(2):
            for tt in range(SLOT):
                made[pl.ds((2 * g + half) * SLOT + tt, DEVICES, stride=CHUNK), :] = done[
                    tt * DEVICES : tt * DEVICES + DEVICES, half * C : half * C + C
                ]

    rows = out_ref.shape[0]
    for step in range(TAIL):

        @pl.when(g == ORDERS + step)
        def _():
            out_ref[...] = made[step * rows : step * rows + rows, :].astype(BF16)


def synthesise(table, x):
    return pl.pallas_call(
        synthesise_kernel,
        grid=(ORDERS + TAIL,),
        out_shape=pltpu.HBM((DEVICES * CHUNK, C), BF16),
        in_specs=[whole(pltpu.HBM), whole()],
        out_specs=pl.BlockSpec(
            (DEVICES * CHUNK // TAIL, C), lambda g: (jnp.maximum(g - ORDERS, 0), 0)
        ),
        scratch_shapes=[pltpu.VMEM((DEVICES * CHUNK, C), F32)] + streamed(table),
        compiler_params=limit(26),
        name="synthesise",
    )(far(table), near(x))


def backward_kernel(table, x_ref, out_ref, wide, right, held, ready):
    g = pl.program_id(0)
    arrive = stream(table, held, ready, held.shape[0])
    rows = LONS * Q

    @pl.when(g == 0)
    def _():
        wide[...] = x_ref[...].astype(F32)
        for tt in range(SLOT):
            part = wide[pl.ds(tt, 2 * M, stride=SLOT), :].astype(BF16)
            for lat in range(LATS):
                first = lat // 2 * rows
                right[lat % 2, first : first + rows, tt * C : tt * C + C] = part[
                    lat * rows : lat * rows + rows
                ]

    arrive()
    for pair in range(SLOT // 2):
        lanes = slice(2 * pair * C, 2 * pair * C + 2 * C)
        even = jnp.dot(held[g, :, :M], right[0, :, lanes], preferred_element_type=F32)
        odd = jnp.dot(held[g, :, M:], right[1, :, lanes], preferred_element_type=F32)
        for side, done in enumerate((even + odd, even - odd)):
            done = done.astype(BF16)
            for half in range(2):
                for j in range(out_ref.shape[1]):
                    out_ref[side, j, 2 * pair + half] = done[
                        j * PAD : j * PAD + PAD, half * C : half * C + C
                    ]


def fourier_backward(table, x):
    steps = 2
    each = HALF // steps
    table = table.reshape(steps, each * PAD, 2 * M)
    return pl.pallas_call(
        backward_kernel,
        grid=(steps,),
        out_shape=pltpu.HBM((2, HALF, SLOT, PAD, C), BF16),
        in_specs=[whole(pltpu.HBM), whole()],
        out_specs=pl.BlockSpec((2, each, SLOT, PAD, C), lambda g: (0, g, 0, 0, 0)),
        scratch_shapes=[
            pltpu.VMEM((DEVICES * CHUNK, C), F32),
            pltpu.VMEM((2, M, SLOT * C), BF16),
        ]
        + streamed(table),
        compiler_params=limit(26),
        name="fourier_backward",
    )(far(table), near(x))


def exchange(x, axis):
    return lax.all_to_all(x, axis, split_axis=0, concat_axis=0, tiled=True)


def cells(x):
    return x.reshape(DEVICES, CHUNK // 2, 2, C)


def on_device(grad_out, spectrum, weights):
    both = ("lat", "lon")
    rows = jnp.swapaxes(grad_out[0], 1, 2)
    rows = jnp.pad(rows, ((0, LONS * SLOT - ROWS), (0, PAD - COLS), (0, 0)))
    rows = exchange(rows.reshape(LONS, SLOT, PAD, C), "lon")
    forward, backward = fourier_tables()
    legendre = legendre_table()
    rows, forward, legendre = lax.optimization_barrier((rows, forward, legendre))

    spectra = fourier_forward(forward, rows)
    columns = exchange(cells(spectra), both).reshape(DEVICES * CHUNK, C)
    turned = jnp.swapaxes(legendre, 1, 2)
    stored = spectrum.reshape(ORDERS, LATS, DEGREES, 2, C).transpose(2, 1, 0, 3, 4)
    stored = stored.reshape(DEGREES, LATS * Q, C)
    columns, turned, stored = lax.optimization_barrier((columns, turned, stored))

    analysed = exchange(analyse(legendre, columns), "lat").reshape(LATS * Q * PAD, C)
    analysed, backward = lax.optimization_barrier((analysed, backward))
    gathered, spec_local = mix(analysed, weights)
    spec_grad = exchange(spec_local.reshape(LATS, Q, PAD, C), "lat")

    keep, give = weigh(stored, gathered)
    got = lax.ppermute(give, "lon", [(k, k ^ 1) for k in range(LONS)])
    sums = [keep[step].astype(F32) + got[step].astype(F32) for step in range(4)]
    held, got = sums[0], []
    for step in (1, 3, 2):
        pairs = [(k, (k + 4 * step) % LONS) for k in range(LONS)]
        got.append(lax.ppermute(sums[step].astype(BF16), "lon", pairs))
    spec_grad, held = lax.optimization_barrier((spec_grad, held))

    row_block = synthesise(turned, spec_grad)
    row_block = exchange(cells(row_block), both)
    for part in got:
        held = held + part.astype(F32)
    held = held.reshape(DEGREES, 2, C // LONS, C)
    y = (lax.axis_index("lon") >> 1) & 1
    keep = lax.dynamic_index_in_dim(held, y, 1, keepdims=False)
    give = lax.dynamic_index_in_dim(held, 1 - y, 1, keepdims=False).astype(BF16)
    row_block, keep, give = lax.optimization_barrier((row_block, keep, give))
    grid_part = fourier_backward(backward, row_block.reshape(DEVICES * CHUNK, C))
    grid_part = exchange(grid_part.reshape(LONS, SLOT, PAD, C), "lon")
    got = lax.ppermute(give, "lon", [(k, k ^ 2) for k in range(LONS)])
    weight_grad = keep + got.astype(F32)
    grad_in = grid_part[:USED].reshape(ROWS, PAD, C)[:, :COLS]
    return jnp.swapaxes(grad_in, 1, 2)[None], weight_grad


def solution(mesh):
    in_specs = (
        P(None, "lat", None, "lon"),
        P("lon", "lat", None, None, None),
        P("lat", None, None),
    )
    out_specs = (P(None, "lat", None, "lon"), P("lat", "lon", None))
    return jax.shard_map(
        on_device, mesh=mesh, in_specs=in_specs, out_specs=out_specs, check_vma=False
    )
```

```python
import math

import jax
import jax.numpy as jnp
import numpy as np
from jax import lax
from jax.experimental import pallas as pl
from jax.experimental.pallas import tpu as pltpu
from jax.sharding import PartitionSpec as P

LAT = 720
LON = 1440
L = 720
M = 640
C = 128
LATS = 8
LONS = 16
DEVICES = LATS * LONS
ROWS = LAT // LATS
COLS = LON // LONS
SLOT = 6
USED = ROWS // SLOT
PAD = 96
ODD = PAD + 1
ORDERS = M // (LATS * LONS)
HALF = LONS // 2
Q = 2 * ORDERS
CHUNK = Q * SLOT
DEGREES = L // LATS
BLOCK = 16
TAIL = 4
SHIFT = 40

F32 = jnp.float32
BF16 = jnp.bfloat16


def limit(mebibytes):
    return pltpu.CompilerParams(vmem_limit_bytes=mebibytes << 20)


def near(x):
    return pltpu.with_memory_space_constraint(x, pltpu.VMEM)


def far(x):
    return pltpu.with_memory_space_constraint(x, pltpu.HBM)


def whole(space=pltpu.VMEM):
    return pl.BlockSpec(memory_space=space)


def fetch(table, held, ready):
    parts = range(held.shape[0])
    copies = [pltpu.make_async_copy(table.at[k], held.at[k], ready.at[k]) for k in parts]
    for copy in copies:
        copy.start()
    return copies


def send(made, out, done):
    copy = pltpu.make_async_copy(made, out, done)
    copy.start()
    return copy


def finish(copies):
    for copy in copies:
        copy.wait()


def streamed(table):
    return [pltpu.VMEM(table.shape, table.dtype), pltpu.SemaphoreType.DMA((table.shape[0],))]


def cosine_values(position, order, part):
    step = position * order + part * (LON // 4)
    turn = step - LON * jnp.floor(step * (1.0 / LON))
    fold = (LON // 4) - jnp.abs(turn - LON // 2)
    angle = fold * (2.0 * math.pi / LON)
    square = angle * angle
    series = -1.0 / 39916800.0
    for term in (1.0 / 362880.0, -1.0 / 5040.0, 1.0 / 120.0, -1.0 / 6.0, 1.0):
        series = series * square + term
    return -(angle * series) * (1.0 / math.sqrt(LON))


def fourier_tables():
    def line(shape, axis):
        at = lax.broadcasted_iota(jnp.int32, shape, axis)
        inner = at % PAD
        return (at // PAD * COLS + inner).astype(F32), (inner < COLS).astype(F32)

    def modes(shape, axis):
        at = lax.broadcasted_iota(jnp.int32, shape, axis)
        device, kind = at // Q, at % Q
        parity, device = device // (DEVICES // 2), device % (DEVICES // 2)
        lat = device // LONS * 2 + parity
        order = device % LONS * (LATS * ORDERS) + kind // 2 * LATS + lat
        return order.astype(F32), (kind % 2).astype(F32)

    wide = HALF * PAD
    position, live = line((1, wide), 1)
    order, part = modes((2 * M, 1), 0)
    forward = (cosine_values(position, order, part) * live).astype(BF16)
    position, live = line((wide, 1), 0)
    order, part = modes((1, 2 * M), 1)
    backward = (cosine_values(position, order, part) * live).astype(BF16)
    return forward.reshape(2, M, wide), backward


def seed_constants():
    out = []
    for m in range(M):
        out.append(
            0.5 * math.log(m + 0.5)
            + 0.5 * math.lgamma(2.0 * m + 1.0)
            - math.lgamma(m + 1.0)
            - m * math.log(2.0)
        )
    return np.asarray(out, np.float32)


def legendre_kernel(up, back, start, seed, order, x_ref, root_ref, sine_ref, out, buf):
    x = x_ref[...]
    root = root_ref[...]
    base = [seed[k] + order[k] * sine_ref[...] for k in range(ORDERS)]
    zero = jnp.zeros_like(x)
    small = 2.0**-SHIFT
    unit = SHIFT * math.log(2.0)

    def block(first, row, steps, carry):
        current, previous, count = (list(part) for part in carry)
        factor = [None] * ORDERS
        for offset in range(steps):
            if offset % 8 == 0:
                for k in range(ORDERS):
                    big = jnp.maximum(jnp.abs(current[k]), jnp.abs(previous[k])) > 1.0
                    scale = jnp.where(big, small, 1.0)
                    current[k] = current[k] * scale
                    previous[k] = previous[k] * scale
                    count[k] = count[k] + jnp.where(big, 1.0, 0.0)
                    factor[k] = jnp.exp(base[k] + unit * count[k]) * root
            for k in range(ORDERS):
                at = k * L + first + offset
                advanced = (up[at] * x) * current[k] - back[at] * previous[k] + start[at]
                previous[k] = current[k]
                current[k] = advanced
                buf[k, offset * 8 : offset * 8 + 8, :] = advanced * factor[k]
        for k in range(ORDERS):
            for offset in range(steps, BLOCK):
                buf[k, offset * 8 : offset * 8 + 8, :] = zero
            for tt in range(SLOT):
                low = buf[k, pl.ds(tt, 8, stride=8), :]
                high = buf[k, pl.ds(64 + tt, 8, stride=8), :]
                both = jnp.concatenate([low, high], axis=0).astype(BF16)
                out[k, pl.ds(pl.multiple_of(row, BLOCK), BLOCK), tt * 128 : tt * 128 + 128] = both
        return tuple(current), tuple(previous), tuple(count)

    def band(k, carry):
        first, row = k * DEGREES, k * PAD
        whole = DEGREES // BLOCK

        def inner(step, carry):
            return block(first + step * BLOCK, row + step * BLOCK, BLOCK, carry)

        carry = lax.fori_loop(0, whole, inner, carry)
        done = whole * BLOCK
        return block(first + done, row + done, DEGREES - done, carry)

    none = (zero,) * ORDERS
    lax.fori_loop(0, LATS, band, (none, none, none))


def legendre_table():
    lon, lat = lax.axis_index("lon"), lax.axis_index("lat")
    orders = (lon * ORDERS + jnp.arange(ORDERS, dtype=jnp.int32)) * LATS + lat
    order = orders.astype(F32)
    seeds = jnp.asarray(seed_constants().reshape(LONS, ORDERS, LATS))
    seed = lax.dynamic_slice(seeds, (lon, 0, lat), (1, ORDERS, 1)).reshape(ORDERS)
    slot = jnp.arange(1024, dtype=jnp.int32)
    tt, device = slot // DEVICES, slot % DEVICES
    lat, lon = device // LONS, device % LONS
    live = (tt < SLOT) & (lon < USED)
    row = jnp.where(live, ROWS * lat + SLOT * lon + tt, 0)
    angle = (row.astype(F32) + 0.5) * (math.pi / LAT)
    sine = jnp.sin(angle)
    x = jnp.where(live, jnp.cos(angle), 0.0).reshape(8, 128)
    root = jnp.where(live, jnp.sqrt(sine * (math.pi / LAT)), 0.0).reshape(8, 128)
    log_sine = jnp.log(sine).reshape(8, 128)
    degree = jnp.arange(L, dtype=jnp.int32)[None, :]
    past = degree > orders[:, None]
    val, ord_val = degree.astype(F32), order[:, None]
    divisor = jnp.where(past, val * val - ord_val * ord_val, 1.0)
    up = jnp.where(past, jnp.sqrt(jnp.maximum((4.0 * val * val - 1.0) / divisor, 0.0)), 0.0)
    lower = (val - 1.0) * (val - 1.0) - ord_val * ord_val
    back = jnp.sqrt(
        jnp.maximum(lower * (2.0 * val + 1.0) / ((2.0 * val - 3.0) * divisor), 0.0)
    )
    back = jnp.where(past, back, 0.0)
    start = (degree == orders[:, None]).astype(F32)
    smem = pl.BlockSpec(memory_space=pltpu.SMEM)
    vmem = pl.BlockSpec(memory_space=pltpu.VMEM)
    return pl.pallas_call(
        legendre_kernel,
        out_shape=jax.ShapeDtypeStruct((ORDERS, LATS * PAD, DEVICES * SLOT), BF16),
        in_specs=[smem] * 5 + [vmem] * 3,
        out_specs=vmem,
        scratch_shapes=[pltpu.VMEM((ORDERS, 8 * BLOCK, 128), F32)],
        compiler_params=limit(16),
        name="legendre",
    )(up.reshape(-1), back.reshape(-1), start.reshape(-1), seed, order, x, root, log_sine)


def forward_kernel(table, x_ref, out_ref, buf, made, held, ready, done):
    copies = fetch(table, held, ready)
    rows = LONS * Q
    sent = []
    for parity in range(2):
        copies[parity].wait()
        for pair in range(SLOT // 2):
            both = []
            for half in range(2):
                low = x_ref[:HALF, 2 * pair + half]
                high = x_ref[HALF:, 2 * pair + half]
                both.append((low - high if parity else low + high).reshape(HALF * PAD, C))
            part = jnp.dot(held[parity], jnp.concatenate(both, axis=1), preferred_element_type=F32)
            for half in range(2):
                for lat in range(LATS // 2):
                    first = lat * rows * SLOT + 2 * pair + half
                    buf[parity, pl.ds(first, rows, stride=SLOT), :] = part[
                        lat * rows : lat * rows + rows, half * C : half * C + C
                    ]
        for lat in range(LATS // 2):
            first = lat * rows * SLOT
            made[parity, lat] = buf[parity, first : first + rows * SLOT, :].astype(BF16)
        sent.append(send(made.at[parity], out_ref.at[:, parity], done.at[parity]))
    finish(sent)


def fourier_forward(table, x):
    shape = (LATS // 2, 2, LONS * CHUNK, C)
    return pl.pallas_call(
        forward_kernel,
        out_shape=pltpu.HBM(shape, BF16),
        in_specs=[whole(pltpu.HBM), whole()],
        out_specs=whole(pltpu.HBM),
        scratch_shapes=[
            pltpu.VMEM((2, M * SLOT, C), F32),
            pltpu.VMEM((2, shape[0]) + shape[2:], BF16),
        ]
        + streamed(table)
        + [pltpu.SemaphoreType.DMA((2,))],
        compiler_params=limit(26),
        name="fourier_forward",
    )(far(table), near(x))


def analyse_kernel(table, x_ref, out_ref, wide, made, held, ready, done):
    copies = fetch(table, held, ready)
    wide[...] = x_ref[...].astype(F32)

    def column(q):
        parts = [wide[pl.ds(q * SLOT + tt, DEVICES, stride=CHUNK), :] for tt in range(SLOT)]
        return jnp.concatenate(parts, axis=0).astype(BF16)

    sent = []
    for k in range(ORDERS):
        right = jnp.concatenate([column(2 * k), column(2 * k + 1)], axis=1)
        copies[k].wait()
        part = jnp.dot(held[k], right, preferred_element_type=F32).astype(BF16)
        for half in range(2):
            made[k, :, half] = part[:, half * C : half * C + C].reshape(LATS, PAD, C)
        sent.append(send(made.at[k], out_ref.at[:, pl.ds(2 * k, 2)], done.at[k]))
    finish(sent)


def analyse(table, x):
    return pl.pallas_call(
        analyse_kernel,
        out_shape=pltpu.HBM((LATS, Q, PAD, C), BF16),
        in_specs=[whole(pltpu.HBM), whole()],
        out_specs=whole(pltpu.HBM),
        scratch_shapes=[
            pltpu.VMEM((DEVICES * CHUNK, C), F32),
            pltpu.VMEM((ORDERS, LATS, 2, PAD, C), BF16),
        ]
        + streamed(table)
        + [pltpu.SemaphoreType.DMA((ORDERS,))],
        compiler_params=limit(28),
        name="analyse",
    )(far(table), near(x))


def mix_kernel(x_ref, weights, gathered, out_ref, wide, mixed, rows, made, held, ready, done):
    copies = fetch(weights, held, ready)
    steps, each = held.shape[:2]
    slabs = LATS * Q
    for slab in range(slabs):
        wide[slab * ODD : slab * ODD + PAD, :] = x_ref[slab * PAD : slab * PAD + PAD, :].astype(
            F32
        )
        mixed[slab * ODD + PAD - 8 : slab * ODD + PAD, :] = jnp.zeros((8, C), F32)
    sent = []
    for step in range(steps):
        copies[step].wait()
        for offset in range(each):
            degree = step * each + offset
            across = pl.ds(degree, slabs, stride=ODD)
            part = wide[across, :].astype(BF16)
            rows[degree] = part
            mixed[across, :] = lax.dot_general(
                part, held[step, offset], (((1,), (1,)), ((), ())), preferred_element_type=F32
            )
        block = pl.ds(step * each, each)
        sent.append(send(rows.at[block], gathered.at[block], done.at[step]))
    for step in range(TAIL):
        first = step * (slabs // TAIL)
        for slab in range(first, first + slabs // TAIL):
            made[slab * PAD : slab * PAD + PAD, :] = mixed[
                slab * ODD : slab * ODD + PAD, :
            ].astype(BF16)
        block = pl.ds(first * PAD, slabs // TAIL * PAD)
        sent.append(send(made.at[block], out_ref.at[block], done.at[steps + step]))
    finish(sent)


def mix(x, weights):
    steps = 5
    size = LATS * Q * PAD
    weights = weights.reshape(steps, DEGREES // steps, C, C)
    return pl.pallas_call(
        mix_kernel,
        out_shape=(
            pltpu.HBM((DEGREES, LATS * Q, C), BF16),
            pltpu.HBM((size, C), BF16),
        ),
        in_specs=[whole(), whole(pltpu.HBM)],
        out_specs=(whole(pltpu.HBM), whole(pltpu.HBM)),
        scratch_shapes=[pltpu.VMEM((LATS * Q * ODD, C), F32)] * 2
        + [pltpu.VMEM((DEGREES, LATS * Q, C), BF16), pltpu.VMEM((size, C), BF16)]
        + streamed(weights)
        + [pltpu.SemaphoreType.DMA((steps + TAIL,))],
        compiler_params=limit(28),
        name="mix",
    )(near(x), far(weights))


def weigh_kernel(place, stored, gathered, keep, give):
    core, z = place[0], place[1]
    share = C // LONS
    for offset in range(stored.shape[0]):
        part = lax.dot_general(
            stored[offset], gathered[offset], (((0,), (0,)), ((), ())), preferred_element_type=F32
        )
        for column in range(4):
            to = lax.rem(column + 4 - z, 4)
            piece = part[column * 4 * share : column * 4 * share + 4 * share]
            here = jnp.concatenate([piece[:share], piece[2 * share : 3 * share]], axis=0)
            there = jnp.concatenate([piece[share : 2 * share], piece[3 * share :]], axis=0)
            keep[to, offset] = jnp.where(core == 0, here, there).astype(BF16)
            give[to, offset] = jnp.where(core == 0, there, here).astype(BF16)


def weigh(stored, gathered):
    steps = 5
    each = DEGREES // steps
    lon = lax.axis_index("lon")
    shape = (4, DEGREES, C // 8, C)
    rows = pl.BlockSpec((each, LATS * Q, C), lambda g: (g, 0, 0))
    sums = pl.BlockSpec((4, each, C // 8, C), lambda g: (0, g, 0, 0))
    return pl.pallas_call(
        weigh_kernel,
        grid=(steps,),
        out_shape=(pltpu.HBM(shape, BF16), pltpu.HBM(shape, BF16)),
        in_specs=[pl.BlockSpec(memory_space=pltpu.SMEM), rows, rows],
        out_specs=(sums, sums),
        compiler_params=limit(20),
        name="weigh",
    )(jnp.stack([lon & 1, lon >> 2]), far(stored), far(gathered))


def synthesise_kernel(table, x_ref, out_ref, mixed, made, held, ready, done):
    copies = fetch(table, held, ready)
    for k in range(ORDERS):
        right = jnp.concatenate(
            [x_ref[:, 2 * k + half].reshape(LATS * PAD, C) for half in range(2)], axis=1
        )
        copies[k].wait()
        part = jnp.dot(held[k], right, preferred_element_type=F32)
        for half in range(2):
            for tt in range(SLOT):
                mixed[pl.ds((2 * k + half) * SLOT + tt, DEVICES, stride=CHUNK), :] = part[
                    tt * DEVICES : tt * DEVICES + DEVICES, half * C : half * C + C
                ]
    sent = []
    rows = DEVICES * CHUNK // TAIL
    for step in range(TAIL):
        block = pl.ds(step * rows, rows)
        made[block, :] = mixed[block, :].astype(BF16)
        sent.append(send(made.at[block], out_ref.at[block], done.at[step]))
    finish(sent)


def synthesise(table, x):
    return pl.pallas_call(
        synthesise_kernel,
        out_shape=pltpu.HBM((DEVICES * CHUNK, C), BF16),
        in_specs=[whole(pltpu.HBM), whole()],
        out_specs=whole(pltpu.HBM),
        scratch_shapes=[
            pltpu.VMEM((DEVICES * CHUNK, C), F32),
            pltpu.VMEM((DEVICES * CHUNK, C), BF16),
        ]
        + streamed(table)
        + [pltpu.SemaphoreType.DMA((TAIL,))],
        compiler_params=limit(28),
        name="synthesise",
    )(far(table), near(x))


def backward_kernel(table, x_ref, out_ref, wide, right, made, held, ready, done):
    copies = fetch(table, held, ready)
    rows = LONS * Q
    wide[...] = x_ref[...].astype(F32)
    for tt in range(SLOT):
        part = wide[pl.ds(tt, 2 * M, stride=SLOT), :].astype(BF16)
        for lat in range(LATS):
            first = lat // 2 * rows
            right[lat % 2, first : first + rows, tt * C : tt * C + C] = part[
                lat * rows : lat * rows + rows
            ]
    sent = []
    each = made.shape[2]
    for step in range(held.shape[0]):
        copies[step].wait()
        for pair in range(SLOT // 2):
            lanes = slice(2 * pair * C, 2 * pair * C + 2 * C)
            even = jnp.dot(held[step, :, :M], right[0, :, lanes], preferred_element_type=F32)
            odd = jnp.dot(held[step, :, M:], right[1, :, lanes], preferred_element_type=F32)
            for side, whole_part in enumerate((even + odd, even - odd)):
                whole_part = whole_part.astype(BF16)
                for half in range(2):
                    for j in range(each):
                        made[step, side, j, 2 * pair + half] = whole_part[
                            j * PAD : j * PAD + PAD, half * C : half * C + C
                        ]
        block = pl.ds(step * each, each)
        sent.append(send(made.at[step], out_ref.at[:, block], done.at[step]))
    finish(sent)


def fourier_backward(table, x):
    steps = 2
    each = HALF // steps
    table = table.reshape(steps, each * PAD, 2 * M)
    return pl.pallas_call(
        backward_kernel,
        out_shape=pltpu.HBM((2, HALF, SLOT, PAD, C), BF16),
        in_specs=[whole(pltpu.HBM), whole()],
        out_specs=whole(pltpu.HBM),
        scratch_shapes=[
            pltpu.VMEM((DEVICES * CHUNK, C), F32),
            pltpu.VMEM((2, M, SLOT * C), BF16),
            pltpu.VMEM((steps, 2, each, SLOT, PAD, C), BF16),
        ]
        + streamed(table)
        + [pltpu.SemaphoreType.DMA((steps,))],
        compiler_params=limit(28),
        name="fourier_backward",
    )(far(table), near(x))


def exchange(x, axis):
    return lax.all_to_all(x, axis, split_axis=0, concat_axis=0, tiled=True)


def cells(x):
    return x.reshape(DEVICES, CHUNK // 2, 2, C)


def on_device(grad_out, spectrum, weights):
    both = ("lat", "lon")
    rows = jnp.swapaxes(grad_out[0], 1, 2)
    rows = jnp.pad(rows, ((0, LONS * SLOT - ROWS), (0, PAD - COLS), (0, 0)))
    rows = exchange(rows.reshape(LONS, SLOT, PAD, C), "lon")
    forward, backward = fourier_tables()
    legendre = legendre_table()
    rows, forward, legendre = lax.optimization_barrier((rows, forward, legendre))

    spectra = fourier_forward(forward, rows)
    columns = exchange(cells(spectra), both).reshape(DEVICES * CHUNK, C)
    turned = jnp.swapaxes(legendre, 1, 2)
    stored = spectrum.reshape(ORDERS, LATS, DEGREES, 2, C).transpose(2, 1, 0, 3, 4)
    stored = stored.reshape(DEGREES, LATS * Q, C)
    columns, turned, stored = lax.optimization_barrier((columns, turned, stored))

    analysed = exchange(analyse(legendre, columns), "lat").reshape(LATS * Q * PAD, C)
    analysed, backward = lax.optimization_barrier((analysed, backward))
    gathered, spec_local = mix(analysed, weights)
    spec_grad = exchange(spec_local.reshape(LATS, Q, PAD, C), "lat")

    keep, give = weigh(stored, gathered)
    got = lax.ppermute(give, "lon", [(k, k ^ 1) for k in range(LONS)])
    sums = [keep[step].astype(F32) + got[step].astype(F32) for step in range(4)]
    held, got = sums[0], []
    for step in (1, 3, 2):
        pairs = [(k, (k + 4 * step) % LONS) for k in range(LONS)]
        got.append(lax.ppermute(sums[step].astype(BF16), "lon", pairs))
    spec_grad, held = lax.optimization_barrier((spec_grad, held))

    row_block = synthesise(turned, spec_grad)
    row_block = exchange(cells(row_block), both)
    for part in got:
        held = held + part.astype(F32)
    held = held.reshape(DEGREES, 2, C // LONS, C)
    y = (lax.axis_index("lon") >> 1) & 1
    keep = lax.dynamic_index_in_dim(held, y, 1, keepdims=False)
    give = lax.dynamic_index_in_dim(held, 1 - y, 1, keepdims=False).astype(BF16)
    row_block, keep, give = lax.optimization_barrier((row_block, keep, give))
    grid_part = fourier_backward(backward, row_block.reshape(DEVICES * CHUNK, C))
    grid_part = exchange(grid_part.reshape(LONS, SLOT, PAD, C), "lon")
    got = lax.ppermute(give, "lon", [(k, k ^ 2) for k in range(LONS)])
    weight_grad = keep + got.astype(F32)
    grad_in = grid_part[:USED].reshape(ROWS, PAD, C)[:, :COLS]
    return jnp.swapaxes(grad_in, 1, 2)[None], weight_grad


def solution(mesh):
    in_specs = (
        P(None, "lat", None, "lon"),
        P("lon", "lat", None, None, None),
        P("lat", None, None),
    )
    out_specs = (P(None, "lat", None, "lon"), P("lat", "lon", None))
    return jax.shard_map(
        on_device, mesh=mesh, in_specs=in_specs, out_specs=out_specs, check_vma=False
    )
```

```python
import math

import jax
import jax.numpy as jnp
import numpy as np
from jax import lax
from jax.experimental import pallas as pl
from jax.experimental.pallas import tpu as pltpu
from jax.sharding import PartitionSpec as P

LAT = 720
LON = 1440
L = 720
M = 640
C = 128
LATS = 8
LONS = 16
DEVICES = LATS * LONS
ROWS = LAT // LATS
COLS = LON // LONS
SLOT = 6
USED = ROWS // SLOT
PAD = 96
ODD = PAD + 1
ORDERS = M // (LATS * LONS)
HALF = LONS // 2
Q = 2 * ORDERS
CHUNK = Q * SLOT
DEGREES = L // LATS
BLOCK = 16
TAIL = 4
SHIFT = 40

F32 = jnp.float32
BF16 = jnp.bfloat16


def limit(mebibytes):
    return pltpu.CompilerParams(vmem_limit_bytes=mebibytes << 20)


def near(x):
    return pltpu.with_memory_space_constraint(x, pltpu.VMEM)


def far(x):
    return pltpu.with_memory_space_constraint(x, pltpu.HBM)


def whole(space=pltpu.VMEM):
    return pl.BlockSpec(memory_space=space)


def stream(table, held, ready, steps):
    g = pl.program_id(0)

    def copy(step):
        return pltpu.make_async_copy(table.at[step], held.at[step], ready.at[step])

    @pl.when(g == 0)
    def _():
        for step in range(steps):
            copy(step).start()

    def arrive():
        @pl.when(g < steps)
        def _():
            copy(jnp.minimum(g, steps - 1)).wait()

    return arrive


def fetch(table, held, ready):
    parts = range(held.shape[0])
    copies = [pltpu.make_async_copy(table.at[k], held.at[k], ready.at[k]) for k in parts]
    for copy in copies:
        copy.start()
    return copies


def send(made, out, done):
    copy = pltpu.make_async_copy(made, out, done)
    copy.start()
    return copy


def finish(copies):
    for copy in copies:
        copy.wait()


def streamed(table):
    return [pltpu.VMEM(table.shape, table.dtype), pltpu.SemaphoreType.DMA((table.shape[0],))]


def cosine_values(position, order, part):
    step = position * order + part * (LON // 4)
    turn = step - LON * jnp.floor(step * (1.0 / LON))
    fold = (LON // 4) - jnp.abs(turn - LON // 2)
    angle = fold * (2.0 * math.pi / LON)
    square = angle * angle
    series = -1.0 / 39916800.0
    for term in (1.0 / 362880.0, -1.0 / 5040.0, 1.0 / 120.0, -1.0 / 6.0, 1.0):
        series = series * square + term
    return -(angle * series) * (1.0 / math.sqrt(LON))


def fourier_tables():
    def line(shape, axis):
        at = lax.broadcasted_iota(jnp.int32, shape, axis)
        inner = at % PAD
        return (at // PAD * COLS + inner).astype(F32), (inner < COLS).astype(F32)

    def modes(shape, axis):
        at = lax.broadcasted_iota(jnp.int32, shape, axis)
        device, kind = at // Q, at % Q
        parity, device = device // (DEVICES // 2), device % (DEVICES // 2)
        lat = device // LONS * 2 + parity
        order = device % LONS * (LATS * ORDERS) + kind // 2 * LATS + lat
        return order.astype(F32), (kind % 2).astype(F32)

    wide = HALF * PAD
    position, live = line((1, wide), 1)
    order, part = modes((2 * M, 1), 0)
    forward = (cosine_values(position, order, part) * live).astype(BF16)
    position, live = line((wide, 1), 0)
    order, part = modes((1, 2 * M), 1)
    backward = (cosine_values(position, order, part) * live).astype(BF16)
    return forward.reshape(2, M, wide), backward


def seed_constants():
    out = []
    for m in range(M):
        out.append(
            0.5 * math.log(m + 0.5)
            + 0.5 * math.lgamma(2.0 * m + 1.0)
            - math.lgamma(m + 1.0)
            - m * math.log(2.0)
        )
    return np.asarray(out, np.float32)


def legendre_kernel(up, back, start, seed, order, x_ref, root_ref, sine_ref, out, buf):
    x = x_ref[...]
    root = root_ref[...]
    base = [seed[k] + order[k] * sine_ref[...] for k in range(ORDERS)]
    zero = jnp.zeros_like(x)
    small = 2.0**-SHIFT
    unit = SHIFT * math.log(2.0)

    def block(first, row, steps, carry):
        current, previous, count = (list(part) for part in carry)
        factor = [None] * ORDERS
        for offset in range(steps):
            if offset % 8 == 0:
                for k in range(ORDERS):
                    big = jnp.maximum(jnp.abs(current[k]), jnp.abs(previous[k])) > 1.0
                    scale = jnp.where(big, small, 1.0)
                    current[k] = current[k] * scale
                    previous[k] = previous[k] * scale
                    count[k] = count[k] + jnp.where(big, 1.0, 0.0)
                    factor[k] = jnp.exp(base[k] + unit * count[k]) * root
            for k in range(ORDERS):
                at = k * L + first + offset
                advanced = (up[at] * x) * current[k] - back[at] * previous[k] + start[at]
                previous[k] = current[k]
                current[k] = advanced
                buf[k, offset * 8 : offset * 8 + 8, :] = advanced * factor[k]
        for k in range(ORDERS):
            for offset in range(steps, BLOCK):
                buf[k, offset * 8 : offset * 8 + 8, :] = zero
            for tt in range(SLOT):
                low = buf[k, pl.ds(tt, 8, stride=8), :]
                high = buf[k, pl.ds(64 + tt, 8, stride=8), :]
                both = jnp.concatenate([low, high], axis=0).astype(BF16)
                out[k, pl.ds(pl.multiple_of(row, BLOCK), BLOCK), tt * 128 : tt * 128 + 128] = both
        return tuple(current), tuple(previous), tuple(count)

    def band(k, carry):
        first, row = k * DEGREES, k * PAD
        whole = DEGREES // BLOCK

        def inner(step, carry):
            return block(first + step * BLOCK, row + step * BLOCK, BLOCK, carry)

        carry = lax.fori_loop(0, whole, inner, carry)
        done = whole * BLOCK
        return block(first + done, row + done, DEGREES - done, carry)

    none = (zero,) * ORDERS
    lax.fori_loop(0, LATS, band, (none, none, none))


def legendre_table():
    lon, lat = lax.axis_index("lon"), lax.axis_index("lat")
    orders = (lon * ORDERS + jnp.arange(ORDERS, dtype=jnp.int32)) * LATS + lat
    order = orders.astype(F32)
    seeds = jnp.asarray(seed_constants().reshape(LONS, ORDERS, LATS))
    seed = lax.dynamic_slice(seeds, (lon, 0, lat), (1, ORDERS, 1)).reshape(ORDERS)
    slot = jnp.arange(1024, dtype=jnp.int32)
    tt, device = slot // DEVICES, slot % DEVICES
    lat, lon = device // LONS, device % LONS
    live = (tt < SLOT) & (lon < USED)
    row = jnp.where(live, ROWS * lat + SLOT * lon + tt, 0)
    angle = (row.astype(F32) + 0.5) * (math.pi / LAT)
    sine = jnp.sin(angle)
    x = jnp.where(live, jnp.cos(angle), 0.0).reshape(8, 128)
    root = jnp.where(live, jnp.sqrt(sine * (math.pi / LAT)), 0.0).reshape(8, 128)
    log_sine = jnp.log(sine).reshape(8, 128)
    degree = jnp.arange(L, dtype=jnp.int32)[None, :]
    past = degree > orders[:, None]
    val, ord_val = degree.astype(F32), order[:, None]
    divisor = jnp.where(past, val * val - ord_val * ord_val, 1.0)
    up = jnp.where(past, jnp.sqrt(jnp.maximum((4.0 * val * val - 1.0) / divisor, 0.0)), 0.0)
    lower = (val - 1.0) * (val - 1.0) - ord_val * ord_val
    back = jnp.sqrt(
        jnp.maximum(lower * (2.0 * val + 1.0) / ((2.0 * val - 3.0) * divisor), 0.0)
    )
    back = jnp.where(past, back, 0.0)
    start = (degree == orders[:, None]).astype(F32)
    smem = pl.BlockSpec(memory_space=pltpu.SMEM)
    vmem = pl.BlockSpec(memory_space=pltpu.VMEM)
    return pl.pallas_call(
        legendre_kernel,
        out_shape=jax.ShapeDtypeStruct((ORDERS, LATS * PAD, DEVICES * SLOT), BF16),
        in_specs=[smem] * 5 + [vmem] * 3,
        out_specs=vmem,
        scratch_shapes=[pltpu.VMEM((ORDERS, 8 * BLOCK, 128), F32)],
        compiler_params=limit(16),
        name="legendre",
    )(up.reshape(-1), back.reshape(-1), start.reshape(-1), seed, order, x, root, log_sine)


def forward_kernel(table, x_ref, out_ref, buf, held, ready):
    g = pl.program_id(0)
    arrive = stream(table, held, ready, 2)
    arrive()
    rows = LONS * Q

    for parity in range(2):

        @pl.when(g == parity)
        def _():
            for pair in range(SLOT // 2):
                both = []
                for half in range(2):
                    low = x_ref[:HALF, 2 * pair + half]
                    high = x_ref[HALF:, 2 * pair + half]
                    both.append((low - high if parity else low + high).reshape(HALF * PAD, C))
                done = jnp.dot(
                    held[parity], jnp.concatenate(both, axis=1), preferred_element_type=F32
                )
                for half in range(2):
                    for lat in range(LATS // 2):
                        first = lat * rows * SLOT + 2 * pair + half
                        buf[pl.ds(first, rows, stride=SLOT), :] = done[
                            lat * rows : lat * rows + rows, half * C : half * C + C
                        ]

    for lat in range(LATS // 2):
        first = lat * rows * SLOT
        out_ref[lat, 0] = buf[first : first + rows * SLOT, :].astype(BF16)


def fourier_forward(table, x):
    shape = (LATS // 2, 2, LONS * CHUNK, C)
    return pl.pallas_call(
        forward_kernel,
        grid=(2,),
        out_shape=pltpu.HBM(shape, BF16),
        in_specs=[whole(pltpu.HBM), whole()],
        out_specs=pl.BlockSpec((shape[0], 1) + shape[2:], lambda g: (0, g, 0, 0)),
        scratch_shapes=[pltpu.VMEM((M * SLOT, C), F32)] + streamed(table),
        compiler_params=limit(24),
        name="fourier_forward",
    )(far(table), near(x))


def analyse_kernel(table, x_ref, out_ref, wide, held, ready):
    g = pl.program_id(0)
    arrive = stream(table, held, ready, ORDERS)

    @pl.when(g == 0)
    def _():
        wide[...] = x_ref[...].astype(F32)

    def column(q):
        parts = [wide[pl.ds(q * SLOT + tt, DEVICES, stride=CHUNK), :] for tt in range(SLOT)]
        return jnp.concatenate(parts, axis=0).astype(BF16)

    right = jnp.concatenate([column(2 * g), column(2 * g + 1)], axis=1)
    arrive()
    done = jnp.dot(held[g], right, preferred_element_type=F32).astype(BF16)
    for half in range(2):
        out_ref[:, half] = done[:, half * C : half * C + C].reshape(LATS, PAD, C)


def analyse(table, x):
    return pl.pallas_call(
        analyse_kernel,
        grid=(ORDERS,),
        out_shape=pltpu.HBM((LATS, Q, PAD, C), BF16),
        in_specs=[whole(pltpu.HBM), whole()],
        out_specs=pl.BlockSpec((LATS, 2, PAD, C), lambda g: (0, g, 0, 0)),
        scratch_shapes=[pltpu.VMEM((DEVICES * CHUNK, C), F32)] + streamed(table),
        compiler_params=limit(26),
        name="analyse",
    )(far(table), near(x))


def mix_kernel(x_ref, weights, gathered, out_ref, wide, mixed, rows, made, held, ready, done):
    copies = fetch(weights, held, ready)
    steps, each = held.shape[:2]
    slabs = LATS * Q
    for slab in range(slabs):
        wide[slab * ODD : slab * ODD + PAD, :] = x_ref[slab * PAD : slab * PAD + PAD, :].astype(
            F32
        )
        mixed[slab * ODD + PAD - 8 : slab * ODD + PAD, :] = jnp.zeros((8, C), F32)
    sent = []
    for step in range(steps):
        copies[step].wait()
        for offset in range(each):
            degree = step * each + offset
            across = pl.ds(degree, slabs, stride=ODD)
            part = wide[across, :].astype(BF16)
            rows[degree] = part
            mixed[across, :] = lax.dot_general(
                part, held[step, offset], (((1,), (1,)), ((), ())), preferred_element_type=F32
            )
        block = pl.ds(step * each, each)
        sent.append(send(rows.at[block], gathered.at[block], done.at[step]))
    for step in range(TAIL):
        first = step * (slabs // TAIL)
        for slab in range(first, first + slabs // TAIL):
            made[slab * PAD : slab * PAD + PAD, :] = mixed[
                slab * ODD : slab * ODD + PAD, :
            ].astype(BF16)
        block = pl.ds(first * PAD, slabs // TAIL * PAD)
        sent.append(send(made.at[block], out_ref.at[block], done.at[steps + step]))
    finish(sent)


def mix(x, weights):
    steps = 5
    size = LATS * Q * PAD
    weights = weights.reshape(steps, DEGREES // steps, C, C)
    return pl.pallas_call(
        mix_kernel,
        out_shape=(
            pltpu.HBM((DEGREES, LATS * Q, C), BF16),
            pltpu.HBM((size, C), BF16),
        ),
        in_specs=[whole(), whole(pltpu.HBM)],
        out_specs=(whole(pltpu.HBM), whole(pltpu.HBM)),
        scratch_shapes=[pltpu.VMEM((LATS * Q * ODD, C), F32)] * 2
        + [pltpu.VMEM((DEGREES, LATS * Q, C), BF16), pltpu.VMEM((size, C), BF16)]
        + streamed(weights)
        + [pltpu.SemaphoreType.DMA((steps + TAIL,))],
        compiler_params=limit(28),
        name="mix",
    )(near(x), far(weights))


def weigh_kernel(place, stored, gathered, keep, give):
    core, z = place[0], place[1]
    share = C // LONS
    for offset in range(stored.shape[0]):
        part = lax.dot_general(
            stored[offset], gathered[offset], (((0,), (0,)), ((), ())), preferred_element_type=F32
        )
        for column in range(4):
            to = lax.rem(column + 4 - z, 4)
            piece = part[column * 4 * share : column * 4 * share + 4 * share]
            here = jnp.concatenate([piece[:share], piece[2 * share : 3 * share]], axis=0)
            there = jnp.concatenate([piece[share : 2 * share], piece[3 * share :]], axis=0)
            keep[to, offset] = jnp.where(core == 0, here, there).astype(BF16)
            give[to, offset] = jnp.where(core == 0, there, here).astype(BF16)


def weigh(stored, gathered):
    steps = 5
    each = DEGREES // steps
    lon = lax.axis_index("lon")
    shape = (4, DEGREES, C // 8, C)
    rows = pl.BlockSpec((each, LATS * Q, C), lambda g: (g, 0, 0))
    sums = pl.BlockSpec((4, each, C // 8, C), lambda g: (0, g, 0, 0))
    return pl.pallas_call(
        weigh_kernel,
        grid=(steps,),
        out_shape=(pltpu.HBM(shape, BF16), pltpu.HBM(shape, BF16)),
        in_specs=[pl.BlockSpec(memory_space=pltpu.SMEM), rows, rows],
        out_specs=(sums, sums),
        compiler_params=limit(20),
        name="weigh",
    )(jnp.stack([lon & 1, lon >> 2]), far(stored), far(gathered))


def synthesise_kernel(table, x_ref, out_ref, made, held, ready):
    g = pl.program_id(0)
    arrive = stream(table, held, ready, ORDERS)
    arrive()
    right = jnp.concatenate(
        [x_ref[:, 2 * g + half].reshape(LATS * PAD, C) for half in range(2)], axis=1
    )
    done = jnp.dot(held[g], right, preferred_element_type=F32)
    for half in range(2):
        for tt in range(SLOT):
            made[pl.ds((2 * g + half) * SLOT + tt, DEVICES, stride=CHUNK), :] = done[
                tt * DEVICES : tt * DEVICES + DEVICES, half * C : half * C + C
            ]

    @pl.when(g == ORDERS - 1)
    def _():
        out_ref[...] = made[...].astype(BF16)


def synthesise(table, x):
    return pl.pallas_call(
        synthesise_kernel,
        grid=(ORDERS,),
        out_shape=pltpu.HBM((DEVICES * CHUNK, C), BF16),
        in_specs=[whole(pltpu.HBM), whole()],
        out_specs=pl.BlockSpec((DEVICES * CHUNK, C), lambda g: (0, 0)),
        scratch_shapes=[pltpu.VMEM((DEVICES * CHUNK, C), F32)] + streamed(table),
        compiler_params=limit(26),
        name="synthesise",
    )(far(table), near(x))


def backward_kernel(table, x_ref, out_ref, wide, right, held, ready):
    g = pl.program_id(0)
    arrive = stream(table, held, ready, held.shape[0])
    rows = LONS * Q

    @pl.when(g == 0)
    def _():
        wide[...] = x_ref[...].astype(F32)
        for tt in range(SLOT):
            part = wide[pl.ds(tt, 2 * M, stride=SLOT), :].astype(BF16)
            for lat in range(LATS):
                first = lat // 2 * rows
                right[lat % 2, first : first + rows, tt * C : tt * C + C] = part[
                    lat * rows : lat * rows + rows
                ]

    arrive()
    for pair in range(SLOT // 2):
        lanes = slice(2 * pair * C, 2 * pair * C + 2 * C)
        even = jnp.dot(held[g, :, :M], right[0, :, lanes], preferred_element_type=F32)
        odd = jnp.dot(held[g, :, M:], right[1, :, lanes], preferred_element_type=F32)
        for side, done in enumerate((even + odd, even - odd)):
            done = done.astype(BF16)
            for half in range(2):
                for j in range(out_ref.shape[1]):
                    out_ref[side, j, 2 * pair + half] = done[
                        j * PAD : j * PAD + PAD, half * C : half * C + C
                    ]


def fourier_backward(table, x):
    steps = 2
    each = HALF // steps
    table = table.reshape(steps, each * PAD, 2 * M)
    return pl.pallas_call(
        backward_kernel,
        grid=(steps,),
        out_shape=pltpu.HBM((2, HALF, SLOT, PAD, C), BF16),
        in_specs=[whole(pltpu.HBM), whole()],
        out_specs=pl.BlockSpec((2, each, SLOT, PAD, C), lambda g: (0, g, 0, 0, 0)),
        scratch_shapes=[
            pltpu.VMEM((DEVICES * CHUNK, C), F32),
            pltpu.VMEM((2, M, SLOT * C), BF16),
        ]
        + streamed(table),
        compiler_params=limit(26),
        name="fourier_backward",
    )(far(table), near(x))


def exchange(x, axis):
    return lax.all_to_all(x, axis, split_axis=0, concat_axis=0, tiled=True)


def cells(x):
    return x.reshape(DEVICES, CHUNK // 2, 2, C)


def on_device(grad_out, spectrum, weights):
    both = ("lat", "lon")
    rows = jnp.swapaxes(grad_out[0], 1, 2)
    rows = jnp.pad(rows, ((0, LONS * SLOT - ROWS), (0, PAD - COLS), (0, 0)))
    rows = exchange(rows.reshape(LONS, SLOT, PAD, C), "lon")
    forward, backward = fourier_tables()
    legendre = legendre_table()
    rows, forward, legendre = lax.optimization_barrier((rows, forward, legendre))

    spectra = fourier_forward(forward, rows)
    columns = exchange(cells(spectra), both).reshape(DEVICES * CHUNK, C)
    turned = jnp.swapaxes(legendre, 1, 2)
    stored = spectrum.reshape(ORDERS, LATS, DEGREES, 2, C).transpose(2, 1, 0, 3, 4)
    stored = stored.reshape(DEGREES, LATS * Q, C)
    columns, turned, stored = lax.optimization_barrier((columns, turned, stored))

    analysed = exchange(analyse(legendre, columns), "lat").reshape(LATS * Q * PAD, C)
    analysed, backward = lax.optimization_barrier((analysed, backward))
    gathered, spec_local = mix(analysed, weights)
    spec_grad = exchange(spec_local.reshape(LATS, Q, PAD, C), "lat")

    keep, give = weigh(stored, gathered)
    got = lax.ppermute(give, "lon", [(k, k ^ 1) for k in range(LONS)])
    sums = [keep[step].astype(F32) + got[step].astype(F32) for step in range(4)]
    held, got = sums[0], []
    for step in (1, 3, 2):
        pairs = [(k, (k + 4 * step) % LONS) for k in range(LONS)]
        got.append(lax.ppermute(sums[step].astype(BF16), "lon", pairs))
    spec_grad, held = lax.optimization_barrier((spec_grad, held))

    row_block = synthesise(turned, spec_grad)
    row_block = exchange(cells(row_block), both)
    for part in got:
        held = held + part.astype(F32)
    held = held.reshape(DEGREES, 2, C // LONS, C)
    y = (lax.axis_index("lon") >> 1) & 1
    keep = lax.dynamic_index_in_dim(held, y, 1, keepdims=False)
    give = lax.dynamic_index_in_dim(held, 1 - y, 1, keepdims=False).astype(BF16)
    got = lax.ppermute(give, "lon", [(k, k ^ 2) for k in range(LONS)])
    weight_grad = keep + got.astype(F32)
    row_block, weight_grad = lax.optimization_barrier((row_block, weight_grad))
    grid_part = fourier_backward(backward, row_block.reshape(DEVICES * CHUNK, C))
    grid_part = exchange(grid_part.reshape(LONS, SLOT, PAD, C), "lon")
    grad_in = grid_part[:USED].reshape(ROWS, PAD, C)[:, :COLS]
    return jnp.swapaxes(grad_in, 1, 2)[None], weight_grad


def solution(mesh):
    in_specs = (
        P(None, "lat", None, "lon"),
        P("lon", "lat", None, None, None),
        P("lat", None, None),
    )
    out_specs = (P(None, "lat", None, "lon"), P("lat", "lon", None))
    return jax.shard_map(
        on_device, mesh=mesh, in_specs=in_specs, out_specs=out_specs, check_vma=False
    )
```

```python
import math

import jax
import jax.numpy as jnp
import numpy as np
from jax import lax
from jax.experimental import pallas as pl
from jax.experimental.pallas import tpu as pltpu
from jax.sharding import PartitionSpec as P

LAT = 720
LON = 1440
L = 720
M = 640
C = 128
LATS = 8
LONS = 16
DEVICES = LATS * LONS
ROWS = LAT // LATS
COLS = LON // LONS
SLOT = 6
USED = ROWS // SLOT
PAD = 96
ODD = PAD + 1
ORDERS = M // (LATS * LONS)
HALF = LONS // 2
Q = 2 * ORDERS
CHUNK = Q * SLOT
DEGREES = L // LATS
BLOCK = 16
TAIL = 4
SHIFT = 40

F32 = jnp.float32
BF16 = jnp.bfloat16


def limit(mebibytes):
    return pltpu.CompilerParams(vmem_limit_bytes=mebibytes << 20)


def near(x):
    return pltpu.with_memory_space_constraint(x, pltpu.VMEM)


def far(x):
    return pltpu.with_memory_space_constraint(x, pltpu.HBM)


def whole(space=pltpu.VMEM):
    return pl.BlockSpec(memory_space=space)


def stream(table, held, ready, steps):
    g = pl.program_id(0)

    def copy(step):
        return pltpu.make_async_copy(table.at[step], held.at[step], ready.at[step])

    @pl.when(g == 0)
    def _():
        for step in range(steps):
            copy(step).start()

    def arrive():
        @pl.when(g < steps)
        def _():
            copy(jnp.minimum(g, steps - 1)).wait()

    return arrive


def send(made, out, done):
    copy = pltpu.make_async_copy(made, out, done)
    copy.start()
    return copy


def finish(copies):
    for copy in copies:
        copy.wait()


def streamed(table):
    return [pltpu.VMEM(table.shape, table.dtype), pltpu.SemaphoreType.DMA((table.shape[0],))]


def cosine_values(position, order, part):
    step = position * order + part * (LON // 4)
    turn = step - LON * jnp.floor(step * (1.0 / LON))
    fold = (LON // 4) - jnp.abs(turn - LON // 2)
    angle = fold * (2.0 * math.pi / LON)
    square = angle * angle
    series = -1.0 / 39916800.0
    for term in (1.0 / 362880.0, -1.0 / 5040.0, 1.0 / 120.0, -1.0 / 6.0, 1.0):
        series = series * square + term
    return -(angle * series) * (1.0 / math.sqrt(LON))


def fourier_tables():
    def line(shape, axis):
        at = lax.broadcasted_iota(jnp.int32, shape, axis)
        inner = at % PAD
        return (at // PAD * COLS + inner).astype(F32), (inner < COLS).astype(F32)

    def modes(shape, axis):
        at = lax.broadcasted_iota(jnp.int32, shape, axis)
        device, kind = at // Q, at % Q
        parity, device = device // (DEVICES // 2), device % (DEVICES // 2)
        lat = device // LONS * 2 + parity
        order = device % LONS * (LATS * ORDERS) + kind // 2 * LATS + lat
        return order.astype(F32), (kind % 2).astype(F32)

    wide = HALF * PAD
    position, live = line((1, wide), 1)
    order, part = modes((2 * M, 1), 0)
    forward = (cosine_values(position, order, part) * live).astype(BF16)
    position, live = line((wide, 1), 0)
    order, part = modes((1, 2 * M), 1)
    backward = (cosine_values(position, order, part) * live).astype(BF16)
    return forward.reshape(2, M, wide), backward


def seed_constants():
    out = []
    for m in range(M):
        out.append(
            0.5 * math.log(m + 0.5)
            + 0.5 * math.lgamma(2.0 * m + 1.0)
            - math.lgamma(m + 1.0)
            - m * math.log(2.0)
        )
    return np.asarray(out, np.float32)


def legendre_kernel(up, back, start, seed, order, x_ref, root_ref, sine_ref, out, buf):
    x = x_ref[...]
    root = root_ref[...]
    base = [seed[k] + order[k] * sine_ref[...] for k in range(ORDERS)]
    zero = jnp.zeros_like(x)
    small = 2.0**-SHIFT
    unit = SHIFT * math.log(2.0)

    def block(first, row, steps, carry):
        current, previous, count = (list(part) for part in carry)
        factor = [None] * ORDERS
        for offset in range(steps):
            if offset % 8 == 0:
                for k in range(ORDERS):
                    big = jnp.maximum(jnp.abs(current[k]), jnp.abs(previous[k])) > 1.0
                    scale = jnp.where(big, small, 1.0)
                    current[k] = current[k] * scale
                    previous[k] = previous[k] * scale
                    count[k] = count[k] + jnp.where(big, 1.0, 0.0)
                    factor[k] = jnp.exp(base[k] + unit * count[k]) * root
            for k in range(ORDERS):
                at = k * L + first + offset
                advanced = (up[at] * x) * current[k] - back[at] * previous[k] + start[at]
                previous[k] = current[k]
                current[k] = advanced
                buf[k, offset * 8 : offset * 8 + 8, :] = advanced * factor[k]
        for k in range(ORDERS):
            for offset in range(steps, BLOCK):
                buf[k, offset * 8 : offset * 8 + 8, :] = zero
            for tt in range(SLOT):
                low = buf[k, pl.ds(tt, 8, stride=8), :]
                high = buf[k, pl.ds(64 + tt, 8, stride=8), :]
                both = jnp.concatenate([low, high], axis=0).astype(BF16)
                out[k, pl.ds(pl.multiple_of(row, BLOCK), BLOCK), tt * 128 : tt * 128 + 128] = both
        return tuple(current), tuple(previous), tuple(count)

    def band(k, carry):
        first, row = k * DEGREES, k * PAD
        whole = DEGREES // BLOCK

        def inner(step, carry):
            return block(first + step * BLOCK, row + step * BLOCK, BLOCK, carry)

        carry = lax.fori_loop(0, whole, inner, carry)
        done = whole * BLOCK
        return block(first + done, row + done, DEGREES - done, carry)

    none = (zero,) * ORDERS
    lax.fori_loop(0, LATS, band, (none, none, none))


def legendre_table():
    lon, lat = lax.axis_index("lon"), lax.axis_index("lat")
    orders = (lon * ORDERS + jnp.arange(ORDERS, dtype=jnp.int32)) * LATS + lat
    order = orders.astype(F32)
    seeds = jnp.asarray(seed_constants().reshape(LONS, ORDERS, LATS))
    seed = lax.dynamic_slice(seeds, (lon, 0, lat), (1, ORDERS, 1)).reshape(ORDERS)
    slot = jnp.arange(1024, dtype=jnp.int32)
    tt, device = slot // DEVICES, slot % DEVICES
    lat, lon = device // LONS, device % LONS
    live = (tt < SLOT) & (lon < USED)
    row = jnp.where(live, ROWS * lat + SLOT * lon + tt, 0)
    angle = (row.astype(F32) + 0.5) * (math.pi / LAT)
    sine = jnp.sin(angle)
    x = jnp.where(live, jnp.cos(angle), 0.0).reshape(8, 128)
    root = jnp.where(live, jnp.sqrt(sine * (math.pi / LAT)), 0.0).reshape(8, 128)
    log_sine = jnp.log(sine).reshape(8, 128)
    degree = jnp.arange(L, dtype=jnp.int32)[None, :]
    past = degree > orders[:, None]
    val, ord_val = degree.astype(F32), order[:, None]
    divisor = jnp.where(past, val * val - ord_val * ord_val, 1.0)
    up = jnp.where(past, jnp.sqrt(jnp.maximum((4.0 * val * val - 1.0) / divisor, 0.0)), 0.0)
    lower = (val - 1.0) * (val - 1.0) - ord_val * ord_val
    back = jnp.sqrt(
        jnp.maximum(lower * (2.0 * val + 1.0) / ((2.0 * val - 3.0) * divisor), 0.0)
    )
    back = jnp.where(past, back, 0.0)
    start = (degree == orders[:, None]).astype(F32)
    smem = pl.BlockSpec(memory_space=pltpu.SMEM)
    vmem = pl.BlockSpec(memory_space=pltpu.VMEM)
    return pl.pallas_call(
        legendre_kernel,
        out_shape=jax.ShapeDtypeStruct((ORDERS, LATS * PAD, DEVICES * SLOT), BF16),
        in_specs=[smem] * 5 + [vmem] * 3,
        out_specs=vmem,
        scratch_shapes=[pltpu.VMEM((ORDERS, 8 * BLOCK, 128), F32)],
        compiler_params=limit(16),
        name="legendre",
    )(up.reshape(-1), back.reshape(-1), start.reshape(-1), seed, order, x, root, log_sine)


def forward_kernel(table, x_ref, out_ref, buf, held, ready):
    g = pl.program_id(0)
    arrive = stream(table, held, ready, 2)
    arrive()
    rows = LONS * Q

    for parity in range(2):

        @pl.when(g == parity)
        def _():
            for pair in range(SLOT // 2):
                both = []
                for half in range(2):
                    low = x_ref[:HALF, 2 * pair + half]
                    high = x_ref[HALF:, 2 * pair + half]
                    both.append((low - high if parity else low + high).reshape(HALF * PAD, C))
                done = jnp.dot(
                    held[parity], jnp.concatenate(both, axis=1), preferred_element_type=F32
                )
                for half in range(2):
                    for lat in range(LATS // 2):
                        first = lat * rows * SLOT + 2 * pair + half
                        buf[pl.ds(first, rows, stride=SLOT), :] = done[
                            lat * rows : lat * rows + rows, half * C : half * C + C
                        ]

    for lat in range(LATS // 2):
        first = lat * rows * SLOT
        out_ref[lat, 0] = buf[first : first + rows * SLOT, :].astype(BF16)


def fourier_forward(table, x):
    shape = (LATS // 2, 2, LONS * CHUNK, C)
    return pl.pallas_call(
        forward_kernel,
        grid=(2,),
        out_shape=pltpu.HBM(shape, BF16),
        in_specs=[whole(pltpu.HBM), whole()],
        out_specs=pl.BlockSpec((shape[0], 1) + shape[2:], lambda g: (0, g, 0, 0)),
        scratch_shapes=[pltpu.VMEM((M * SLOT, C), F32)] + streamed(table),
        compiler_params=limit(24),
        name="fourier_forward",
    )(far(table), near(x))


def analyse_kernel(table, x_ref, out_ref, wide, held, ready):
    g = pl.program_id(0)
    arrive = stream(table, held, ready, ORDERS)

    @pl.when(g == 0)
    def _():
        wide[...] = x_ref[...].astype(F32)

    def column(q):
        parts = [wide[pl.ds(q * SLOT + tt, DEVICES, stride=CHUNK), :] for tt in range(SLOT)]
        return jnp.concatenate(parts, axis=0).astype(BF16)

    right = jnp.concatenate([column(2 * g), column(2 * g + 1)], axis=1)
    arrive()
    done = jnp.dot(held[g], right, preferred_element_type=F32).astype(BF16)
    for half in range(2):
        out_ref[:, half] = done[:, half * C : half * C + C].reshape(LATS, PAD, C)


def analyse(table, x):
    return pl.pallas_call(
        analyse_kernel,
        grid=(ORDERS,),
        out_shape=pltpu.HBM((LATS, Q, PAD, C), BF16),
        in_specs=[whole(pltpu.HBM), whole()],
        out_specs=pl.BlockSpec((LATS, 2, PAD, C), lambda g: (0, g, 0, 0)),
        scratch_shapes=[pltpu.VMEM((DEVICES * CHUNK, C), F32)] + streamed(table),
        compiler_params=limit(26),
        name="analyse",
    )(far(table), near(x))


def mix_kernel(x_ref, weights, gathered, out_ref, wide, mixed, rows, made, held, ready, done):
    steps, each = held.shape[:2]
    copies = [
        pltpu.make_async_copy(weights.at[k], held.at[k], ready.at[k]) for k in range(steps)
    ]
    for copy in copies[:2]:
        copy.start()
    slabs = LATS * Q
    for slab in range(slabs):
        wide[slab * ODD : slab * ODD + PAD, :] = x_ref[slab * PAD : slab * PAD + PAD, :].astype(
            F32
        )
        mixed[slab * ODD + PAD - 8 : slab * ODD + PAD, :] = jnp.zeros((8, C), F32)
    sent = []
    for step in range(steps):
        copies[step].wait()
        if step + 2 < steps:
            copies[step + 2].start()
        for offset in range(each):
            degree = step * each + offset
            across = pl.ds(degree, slabs, stride=ODD)
            part = wide[across, :].astype(BF16)
            rows[degree] = part
            mixed[across, :] = lax.dot_general(
                part, held[step, offset], (((1,), (1,)), ((), ())), preferred_element_type=F32
            )
        block = pl.ds(step * each, each)
        sent.append(send(rows.at[block], gathered.at[block], done.at[step]))
    for step in range(TAIL):
        first = step * (slabs // TAIL)
        for slab in range(first, first + slabs // TAIL):
            made[slab * PAD : slab * PAD + PAD, :] = mixed[
                slab * ODD : slab * ODD + PAD, :
            ].astype(BF16)
        block = pl.ds(first * PAD, slabs // TAIL * PAD)
        sent.append(send(made.at[block], out_ref.at[block], done.at[steps + step]))
    finish(sent)


def mix(x, weights):
    steps = 5
    size = LATS * Q * PAD
    weights = weights.reshape(steps, DEGREES // steps, C, C)
    return pl.pallas_call(
        mix_kernel,
        out_shape=(
            pltpu.HBM((DEGREES, LATS * Q, C), BF16),
            pltpu.HBM((size, C), BF16),
        ),
        in_specs=[whole(), whole(pltpu.HBM)],
        out_specs=(whole(pltpu.HBM), whole(pltpu.HBM)),
        scratch_shapes=[pltpu.VMEM((LATS * Q * ODD, C), F32)] * 2
        + [pltpu.VMEM((DEGREES, LATS * Q, C), BF16), pltpu.VMEM((size, C), BF16)]
        + streamed(weights)
        + [pltpu.SemaphoreType.DMA((steps + TAIL,))],
        compiler_params=limit(28),
        name="mix",
    )(near(x), far(weights))


def weigh_kernel(place, stored, gathered, keep, give):
    core, z = place[0], place[1]
    share = C // LONS
    for offset in range(stored.shape[0]):
        part = lax.dot_general(
            stored[offset], gathered[offset], (((0,), (0,)), ((), ())), preferred_element_type=F32
        )
        for column in range(4):
            to = lax.rem(column + 4 - z, 4)
            piece = part[column * 4 * share : column * 4 * share + 4 * share]
            here = jnp.concatenate([piece[:share], piece[2 * share : 3 * share]], axis=0)
            there = jnp.concatenate([piece[share : 2 * share], piece[3 * share :]], axis=0)
            keep[to, offset] = jnp.where(core == 0, here, there).astype(BF16)
            give[to, offset] = jnp.where(core == 0, there, here).astype(BF16)


def weigh(stored, gathered):
    steps = 5
    each = DEGREES // steps
    lon = lax.axis_index("lon")
    shape = (4, DEGREES, C // 8, C)
    rows = pl.BlockSpec((each, LATS * Q, C), lambda g: (g, 0, 0))
    sums = pl.BlockSpec((4, each, C // 8, C), lambda g: (0, g, 0, 0))
    return pl.pallas_call(
        weigh_kernel,
        grid=(steps,),
        out_shape=(pltpu.HBM(shape, BF16), pltpu.HBM(shape, BF16)),
        in_specs=[pl.BlockSpec(memory_space=pltpu.SMEM), rows, rows],
        out_specs=(sums, sums),
        compiler_params=limit(20),
        name="weigh",
    )(jnp.stack([lon & 1, lon >> 2]), far(stored), far(gathered))


def synthesise_kernel(table, x_ref, out_ref, made, held, ready):
    g = pl.program_id(0)
    arrive = stream(table, held, ready, ORDERS)
    arrive()
    right = jnp.concatenate(
        [x_ref[:, 2 * g + half].reshape(LATS * PAD, C) for half in range(2)], axis=1
    )
    done = jnp.dot(held[g], right, preferred_element_type=F32)
    for half in range(2):
        for tt in range(SLOT):
            made[pl.ds((2 * g + half) * SLOT + tt, DEVICES, stride=CHUNK), :] = done[
                tt * DEVICES : tt * DEVICES + DEVICES, half * C : half * C + C
            ]

    @pl.when(g == ORDERS - 1)
    def _():
        out_ref[...] = made[...].astype(BF16)


def synthesise(table, x):
    return pl.pallas_call(
        synthesise_kernel,
        grid=(ORDERS,),
        out_shape=pltpu.HBM((DEVICES * CHUNK, C), BF16),
        in_specs=[whole(pltpu.HBM), whole()],
        out_specs=pl.BlockSpec((DEVICES * CHUNK, C), lambda g: (0, 0)),
        scratch_shapes=[pltpu.VMEM((DEVICES * CHUNK, C), F32)] + streamed(table),
        compiler_params=limit(26),
        name="synthesise",
    )(far(table), near(x))


def backward_kernel(table, x_ref, out_ref, wide, right, held, ready):
    g = pl.program_id(0)
    arrive = stream(table, held, ready, held.shape[0])
    rows = LONS * Q

    @pl.when(g == 0)
    def _():
        wide[...] = x_ref[...].astype(F32)
        for tt in range(SLOT):
            part = wide[pl.ds(tt, 2 * M, stride=SLOT), :].astype(BF16)
            for lat in range(LATS):
                first = lat // 2 * rows
                right[lat % 2, first : first + rows, tt * C : tt * C + C] = part[
                    lat * rows : lat * rows + rows
                ]

    arrive()
    for pair in range(SLOT // 2):
        lanes = slice(2 * pair * C, 2 * pair * C + 2 * C)
        even = jnp.dot(held[g, :, :M], right[0, :, lanes], preferred_element_type=F32)
        odd = jnp.dot(held[g, :, M:], right[1, :, lanes], preferred_element_type=F32)
        for side, done in enumerate((even + odd, even - odd)):
            done = done.astype(BF16)
            for half in range(2):
                for j in range(out_ref.shape[1]):
                    out_ref[side, j, 2 * pair + half] = done[
                        j * PAD : j * PAD + PAD, half * C : half * C + C
                    ]


def fourier_backward(table, x):
    steps = 2
    each = HALF // steps
    table = table.reshape(steps, each * PAD, 2 * M)
    return pl.pallas_call(
        backward_kernel,
        grid=(steps,),
        out_shape=pltpu.HBM((2, HALF, SLOT, PAD, C), BF16),
        in_specs=[whole(pltpu.HBM), whole()],
        out_specs=pl.BlockSpec((2, each, SLOT, PAD, C), lambda g: (0, g, 0, 0, 0)),
        scratch_shapes=[
            pltpu.VMEM((DEVICES * CHUNK, C), F32),
            pltpu.VMEM((2, M, SLOT * C), BF16),
        ]
        + streamed(table),
        compiler_params=limit(26),
        name="fourier_backward",
    )(far(table), near(x))


def exchange(x, axis):
    return lax.all_to_all(x, axis, split_axis=0, concat_axis=0, tiled=True)


def cells(x):
    return x.reshape(DEVICES, CHUNK // 2, 2, C)


def on_device(grad_out, spectrum, weights):
    both = ("lat", "lon")
    rows = jnp.swapaxes(grad_out[0], 1, 2)
    rows = jnp.pad(rows, ((0, LONS * SLOT - ROWS), (0, PAD - COLS), (0, 0)))
    rows = exchange(rows.reshape(LONS, SLOT, PAD, C), "lon")
    forward, backward = fourier_tables()
    legendre = legendre_table()
    rows, forward, legendre = lax.optimization_barrier((rows, forward, legendre))

    spectra = fourier_forward(forward, rows)
    columns = exchange(cells(spectra), both).reshape(DEVICES * CHUNK, C)
    turned = jnp.swapaxes(legendre, 1, 2)
    stored = spectrum.reshape(ORDERS, LATS, DEGREES, 2, C).transpose(2, 1, 0, 3, 4)
    stored = stored.reshape(DEGREES, LATS * Q, C)
    columns, turned, stored = lax.optimization_barrier((columns, turned, stored))

    analysed = exchange(analyse(legendre, columns), "lat").reshape(LATS * Q * PAD, C)
    analysed, backward = lax.optimization_barrier((analysed, backward))
    gathered, spec_local = mix(analysed, weights)
    spec_grad = exchange(spec_local.reshape(LATS, Q, PAD, C), "lat")

    keep, give = weigh(stored, gathered)
    got = lax.ppermute(give, "lon", [(k, k ^ 1) for k in range(LONS)])
    sums = [keep[step].astype(F32) + got[step].astype(F32) for step in range(4)]
    held, got = sums[0], []
    for step in (1, 3, 2):
        pairs = [(k, (k + 4 * step) % LONS) for k in range(LONS)]
        got.append(lax.ppermute(sums[step].astype(BF16), "lon", pairs))
    spec_grad, held = lax.optimization_barrier((spec_grad, held))

    row_block = synthesise(turned, spec_grad)
    row_block = exchange(cells(row_block), both)
    for part in got:
        held = held + part.astype(F32)
    held = held.reshape(DEGREES, 2, C // LONS, C)
    y = (lax.axis_index("lon") >> 1) & 1
    keep = lax.dynamic_index_in_dim(held, y, 1, keepdims=False)
    give = lax.dynamic_index_in_dim(held, 1 - y, 1, keepdims=False).astype(BF16)
    row_block, keep, give = lax.optimization_barrier((row_block, keep, give))
    grid_part = fourier_backward(backward, row_block.reshape(DEVICES * CHUNK, C))
    grid_part = exchange(grid_part.reshape(LONS, SLOT, PAD, C), "lon")
    got = lax.ppermute(give, "lon", [(k, k ^ 2) for k in range(LONS)])
    weight_grad = keep + got.astype(F32)
    grad_in = grid_part[:USED].reshape(ROWS, PAD, C)[:, :COLS]
    return jnp.swapaxes(grad_in, 1, 2)[None], weight_grad


def solution(mesh):
    in_specs = (
        P(None, "lat", None, "lon"),
        P("lon", "lat", None, None, None),
        P("lat", None, None),
    )
    out_specs = (P(None, "lat", None, "lon"), P("lat", "lon", None))
    return jax.shard_map(
        on_device, mesh=mesh, in_specs=in_specs, out_specs=out_specs, check_vma=False
    )
```
